32 devices in a mesh: slides: 2 (over y), cols: 16 (over z, x, core).
Axes of the slice: x: 2, y: 2, z: 4, core: 2. Of those that a mesh axis runs over, the one named last changes fastest.
Arguments:
- patches: bfloat16 [16, 256, 512], P('slides', 'cols'), parts along dimension 0, may hold values from -6 to 6
- norm_gain: float32 [512], replicated, may hold values from 0.25 to 1.75
- w_in: bfloat16 [512, 2048], replicated, may hold values from -0.25 to 0.25
- conv_w: float32 [3, 3, 1024], replicated, may hold values from -1.5 to 1.5
- w_bc: bfloat16 [1024, 32], replicated, may hold values from -0.1875 to 0.1875
- skip: float32 [1024], replicated, may hold values from 0.5 to 1.5
- w_out: bfloat16 [1024, 512], replicated, may hold values from -0.1875 to 0.1875
- decay_h: float32 [16, 256, 1024], P('slides', 'cols'), parts along dimension 0, may hold values from 0.3 to 1, as said below
- decay_v: float32 [16, 256, 1024], P('slides', 'cols'), parts along dimension 0, may hold values from 0.3 to 1, as said below
Outputs:
- mixed_out: bfloat16 [16, 256, 512], P('slides', 'cols'), parts along dimension 0
The draws below stay inside these ranges and needn't reach their ends.
There are 2 independent parts, one for each index of `slides`. The reference program is written for one: setup_inputs(seed, part) draws one part's arguments, and reference() takes and returns one part's arrays. A program takes and returns all parts, laid end to end along the dimension named above; an argument that names none is the same for every part. Nothing has to cross between parts.
Inputs may be any that keep to these rules, and one draw needn't show every extreme that they name: decay_h lies strictly between 0 and 1. decay_v lies strictly between 0 and 1.
All inputs are finite; a program needn't handle non-finite values.
Results may differ from the reference program's by a relative error of at most 0.0086.
Values may be sent and summed in bfloat16 or wider, within the bound.
A program may use at most 192 MiB of HBM per device.

```python
import math
import jax
import jax.numpy as jnp
from jax import lax

D = 512
INNER = 1024
STATE = 16
ROWS = 8
SLIDE_COLS = 256


def decay_field(key, chain_length, axis_dim):
    random_subkeys = jax.random.split(key, 7)
    fast_share = 0.5
    chooser = jax.random.uniform(random_subkeys[0], (INNER,))
    slow_rate = jnp.exp(jax.random.uniform(random_subkeys[1], (INNER,), minval=math.log(0.1), maxval=math.log(0.8))) / chain_length
    fast_rate = jax.random.uniform(random_subkeys[2], (INNER,), minval=1.0 / 50.0, maxval=1.0 / 30.0)
    decay_speed = jnp.where(chooser < fast_share, fast_rate, slow_rate)
    patch_cell_factor = jnp.exp(jax.random.uniform(random_subkeys[3], (ROWS, SLIDE_COLS, INNER), minval=math.log(0.5), maxval=math.log(2.0)))
    if axis_dim == 1:
        scanline_shape = (1, SLIDE_COLS, 1)
    else:
        scanline_shape = (ROWS, 1, 1)
    scanline_factor = jnp.exp(jax.random.uniform(random_subkeys[4], scanline_shape, minval=math.log(0.5), maxval=math.log(2.0)))
    spike_locations = jax.random.randint(random_subkeys[5], (3,), 0, chain_length)
    grid_positions = jnp.arange(chain_length)
    spike_mask = jnp.any(grid_positions[:, None] == spike_locations[None, :], axis=1)
    spike_depth = jax.random.uniform(random_subkeys[6], (chain_length,), minval=0.5, maxval=0.8)
    spike_factor = jnp.where(spike_mask, spike_depth, 1.0).reshape(scanline_shape)
    return (jnp.exp(-decay_speed * patch_cell_factor * scanline_factor) * spike_factor).astype(jnp.float32)


def draw_decay_h(key, part):
    return decay_field(jax.random.fold_in(key, 11), SLIDE_COLS, 1)


def draw_decay_v(key, part):
    return decay_field(jax.random.fold_in(key, 23), ROWS, 0)


def shard_levels(stream_key, extent, pieces, low, high):
    def one(dim, parts):
        draws = jax.random.uniform(jax.random.fold_in(jax.random.fold_in(stream_key, 6), dim), (parts,), jnp.float32, low / len(pieces), high / len(pieces))
        return jnp.repeat(jnp.exp(draws), extent[dim] // parts).reshape((-1,) + (1,) * (len(extent) - dim - 1))

    factor_of = one(*pieces[0])
    for cut in pieces[1:]:
        factor_of = factor_of * one(*cut)
    return factor_of


def normal_values(stream_key, shape, width, reach, pieces=(), dtype=jnp.bfloat16):
    entries = jax.random.normal(stream_key, shape, jnp.float32) * width
    if len(pieces) > 0:
        entries = shard_levels(stream_key, shape, pieces, -0.22, 0.18) * entries
    return jnp.clip(entries, min=-reach, max=reach).astype(dtype)


def setup_inputs(seed: int = 0, part: int = 0) -> dict:
    key_of = jax.random.split(jax.random.key(seed), 10)
    own_keys = jax.random.split(jax.random.fold_in(key_of[9], part), 10)
    patches = normal_values(own_keys[0], (ROWS, SLIDE_COLS, D), 1.0, 6.0, ((1, 16),))
    norm_gain = jnp.clip(1.0 + 0.15 * jax.random.normal(key_of[1], (D,), jnp.float32), 0.25, 1.75)
    w_in = normal_values(key_of[2], (D, 2 * INNER), D ** -0.5, 0.25)
    conv_w = normal_values(key_of[3], (3, 3, INNER), 0.33, 1.5, (), jnp.float32)
    w_bc = normal_values(key_of[4], (INNER, 2 * STATE), INNER ** -0.5, 0.1875)
    skip = jnp.clip(jax.random.uniform(key_of[5], (INNER,), jnp.float32, 0.5, 1.5), 0.5, 1.5)
    w_out = normal_values(key_of[6], (INNER, D), INNER ** -0.5, 0.1875)
    decay_h = draw_decay_h(jax.random.fold_in(jax.random.fold_in(key_of[9], part), 71), part)
    decay_v = draw_decay_v(jax.random.fold_in(jax.random.fold_in(key_of[9], part), 71), part)
    return {"patches": patches, "norm_gain": norm_gain, "w_in": w_in, "conv_w": conv_w, "w_bc": w_bc, "skip": skip, "w_out": w_out, "decay_h": decay_h, "decay_v": decay_v}


def reference(patches, norm_gain, w_in, conv_w, w_bc, skip, w_out, decay_h, decay_v):
    feats = patches.astype(jnp.float32)
    meansq = lax.optimization_barrier(jnp.mean(feats * feats, axis=-1, keepdims=True))
    normed = (feats * lax.rsqrt(meansq + 1e-05) * norm_gain).astype(jnp.bfloat16)
    projected = jnp.dot(normed.reshape(-1, D), w_in, preferred_element_type=jnp.float32)
    projected = projected.reshape(ROWS, SLIDE_COLS, 2 * INNER)
    branch = projected[:, :, :INNER].astype(jnp.bfloat16)
    gate_half = projected[:, :, INNER:].astype(jnp.bfloat16)
    padded = jnp.pad(branch, ((1, 1), (1, 1), (0, 0)))
    convolved = jnp.zeros((ROWS, SLIDE_COLS, INNER), jnp.float32)
    for row_shift in range(3):
        for col_shift in range(3):
            window = padded[row_shift:row_shift + ROWS, col_shift:col_shift + SLIDE_COLS].astype(jnp.float32)
            convolved = convolved + conv_w[row_shift, col_shift] * window
    signal = jax.nn.silu(convolved)
    coeffs = jnp.dot(signal.astype(jnp.bfloat16).reshape(-1, INNER), w_bc, preferred_element_type=jnp.float32)
    coeffs = coeffs.reshape(ROWS, SLIDE_COLS, 2 * STATE)
    in_coef = coeffs[:, :, :STATE]
    out_coef = coeffs[:, :, STATE:]

    def column_step(state, inputs):
        decay_col, vert_col, signal_col, in_col, out_col = inputs
        state = decay_col[:, None, :] * state + (jnp.sqrt(1.0 - decay_col * decay_col) * signal_col)[:, None, :] * in_col[:, :, None]

        def row_step(carry, row_inputs):
            vert_row, state_row, out_row = row_inputs
            carry = vert_row[None, :] * carry + jnp.sqrt(1.0 - vert_row * vert_row)[None, :] * state_row
            return (carry, lax.optimization_barrier(jnp.sum(out_row[:, None] * carry, axis=0)))
        _, outputs = lax.scan(row_step, jnp.zeros((STATE, INNER), jnp.float32), (vert_col, state, out_col))
        return (state, outputs)

    def columns_first(array):
        return jnp.swapaxes(array, 0, 1)
    _, columns = lax.scan(column_step, jnp.zeros((ROWS, STATE, INNER), jnp.float32), (columns_first(decay_h), columns_first(decay_v), columns_first(signal), columns_first(in_coef), columns_first(out_coef)))
    scanned = jnp.swapaxes(columns, 0, 1)
    combined = scanned + skip * signal
    gated_out = (combined * jax.nn.silu(gate_half.astype(jnp.float32))).astype(jnp.bfloat16)
    result = jnp.dot(gated_out.reshape(-1, INNER), w_out, preferred_element_type=jnp.float32)
    return result.reshape(ROWS, SLIDE_COLS, D).astype(jnp.bfloat16)
```

```python
import functools

import jax
import jax.numpy as jnp
from jax import lax
from jax.experimental import pallas as pl
from jax.experimental.pallas import tpu as pltpu
from jax.sharding import PartitionSpec as P

F32 = jnp.float32
BF16 = jnp.bfloat16
LANES = 128


def copy_to(src, dst, send_sem, recv_sem, target):
    return pltpu.make_async_remote_copy(
        src_ref=src,
        dst_ref=dst,
        send_sem=send_sem,
        recv_sem=recv_sem,
        device_id={"cols": target},
        device_id_type=pl.DeviceIdType.MESH,
    )


def drain(ref, sem):
    pltpu.make_async_copy(ref, ref, sem).wait()


def kernel(
    n, split, subs, rows, cols, states,
    x_hbm, gain_hbm, w_in_hbm, conv_hbm, w_bc_hbm, skip_hbm, w_out_hbm, dh_hbm, dv_hbm,
    out_ref,
    x_ref, gain_ref, w_in_ref, conv_ref, w_bc_ref, skip_ref, w_out_ref, dh_ref, dv_ref,
    edge_out, edge_in, pad, gate, signal, weight, hmix, vmix, fix, b_full, c_full, scanned, reach, c_pair, gated,
    s_send, p_send, s_recv, p_recv, c_send, carry,
    load_sem, edge_send_sem, edge_recv_sem, s_send_sem, s_recv_sem, p_send_sem, p_recv_sem,
    c_send_sem, c_recv_sem,
):
    me = lax.axis_index("cols")
    inner = w_out_ref.shape[0]
    width = inner // split
    part = width // subs
    blocks = rows * split
    owners = min(blocks, n)
    patches = rows * cols

    pairs = (
        (x_hbm, x_ref), (gain_hbm, gain_ref), (dh_hbm, dh_ref),
        (w_in_hbm.at[:, pl.ds(0, inner)], w_in_ref.at[:, pl.ds(0, inner)]),
        (conv_hbm, conv_ref),
        (w_in_hbm.at[:, pl.ds(inner, inner)], w_in_ref.at[:, pl.ds(inner, inner)]),
        (w_bc_hbm, w_bc_ref), (dv_hbm, dv_ref), (skip_hbm, skip_ref), (w_out_hbm, w_out_ref),
    )
    loads = [
        pltpu.make_async_copy(src, dst, load_sem.at[k]) for k, (src, dst) in enumerate(pairs)
    ]
    (
        x_load, gain_load, dh_load, branch_load, conv_load, gate_load, bc_load, dv_load,
        skip_load, out_load,
    ) = loads

    early = (x_load, gain_load, dh_load, branch_load, conv_load, bc_load)
    for load in early:
        load.start()

    barrier = pltpu.get_barrier_semaphore()

    def greet(turn, _):
        pl.semaphore_signal(
            barrier,
            inc=1,
            device_id={"cols": lax.rem(me + turn, n)},
            device_id_type=pl.DeviceIdType.MESH,
        )
        return 0

    lax.fori_loop(1, n, greet, 0)

    def normalise(feats):
        meansq = jnp.mean(feats * feats, axis=-1, keepdims=True)
        return (feats * lax.rsqrt(meansq + 1e-05) * gain_ref[...]).astype(BF16)

    x_load.wait()
    chunk = 2 * LANES
    dh_load.wait()

    @pl.loop(0, inner // chunk)
    def _(turn):
        at = pl.ds(pl.multiple_of(turn * chunk, chunk), chunk)
        place = lax.broadcasted_iota(jnp.int32, (cols, chunk), 0)
        for row in range(rows):
            here = pl.ds(row * cols, cols)
            decay = dh_ref[here, at]
            product = decay
            step = 1
            while step < cols:
                product = product * jnp.where(
                    place < cols - step, pltpu.roll(product, cols - step, 0), 1.0
                )
                step *= 2
            after = jnp.where(place < cols - 1, pltpu.roll(product, cols - 1, 0), 1.0)
            mix = jnp.sqrt(1.0 - decay * decay)
            hmix[here, at] = mix
            weight[here, at] = after * mix
            p_send[row, :, at] = product[0:1]

    gain_load.wait()
    normed = normalise(x_ref[...].astype(F32))
    branch_load.wait()
    for load in (gate_load, dv_load, skip_load, out_load):
        load.start()
    branch = jnp.dot(normed, w_in_ref[:, :inner], preferred_element_type=F32)
    branch = branch.astype(BF16).astype(F32)
    edge_rows = jnp.zeros((8, inner), F32)
    pad[0] = jnp.zeros(pad.shape[1:], F32)
    pad[rows + 1] = jnp.zeros(pad.shape[1:], F32)
    for row in range(rows):
        pad[row + 1, 0:8, :] = edge_rows
        pad[row + 1, 8 : 8 + cols, :] = branch[row * cols : (row + 1) * cols]
        pad[row + 1, 8 + cols : 16 + cols, :] = edge_rows
        for side, place in ((0, row * cols), (1, (row + 1) * cols - 1)):
            fix[side, row : row + 1, :] = branch[place : place + 1]
    for side in range(2):
        edge_out[side] = fix[side].astype(BF16)

    pl.semaphore_wait(barrier, n - 1)

    to_right = copy_to(
        edge_out.at[1], edge_in.at[0], edge_send_sem.at[0], edge_recv_sem.at[0],
        lax.rem(me + 1, n),
    )
    to_left = copy_to(
        edge_out.at[0], edge_in.at[1], edge_send_sem.at[1], edge_recv_sem.at[1],
        lax.rem(me + n - 1, n),
    )
    to_right.start()
    to_left.start()

    def block_of(owner):
        return owner // split, pl.ds(pl.multiple_of(lax.rem(owner, split) * width, width), width)

    def part_of(owner, sub):
        begin = lax.rem(owner, split) * width + sub * part
        return owner // split, pl.ds(pl.multiple_of(begin, part), part)

    def send_products(turn, _):
        owner = lax.rem(me + turn, n)

        @pl.when(owner < owners)
        def _():
            row, at = block_of(owner)
            copy_to(
                p_send.at[row, :, at], p_recv.at[me], p_send_sem, p_recv_sem, owner
            ).start()

        return 0

    lax.fori_loop(1, n, send_products, 0)

    conv_load.wait()

    @pl.loop(0, inner // chunk)
    def _(turn):
        at = pl.ds(pl.multiple_of(turn * chunk, chunk), chunk)
        taps = [[conv_ref[a, pl.ds(b, 1), at] for b in range(3)] for a in range(3)]
        for row in range(rows):
            lines = [pad[row + a, :, at] for a in range(3)]
            parts = [
                taps[0][b] * lines[0] + taps[1][b] * lines[1] + taps[2][b] * lines[2]
                for b in range(3)
            ]
            total = parts[0].shape[0]
            sum_all = (
                pltpu.roll(parts[0], 1, 0) + parts[1] + pltpu.roll(parts[2], total - 1, 0)
            )
            signal[pl.ds(row * cols, cols), at] = sum_all[8 : 8 + cols]

    to_right.wait()
    to_left.wait()
    line = lax.broadcasted_iota(jnp.int32, (rows, inner), 0)
    for side, inside, tap in ((0, me > 0, 0), (1, me < n - 1, 2)):
        edge = edge_in[side].astype(F32) * jnp.where(inside, 1.0, 0.0).astype(F32)
        above = jnp.where(line > 0, pltpu.roll(edge, 1, 0), 0.0)
        below = jnp.where(line < rows - 1, pltpu.roll(edge, rows - 1, 0), 0.0)
        fix[side] = (
            conv_ref[0, tap : tap + 1, :] * above
            + conv_ref[1, tap : tap + 1, :] * edge
            + conv_ref[2, tap : tap + 1, :] * below
        )

    @pl.loop(0, inner // chunk)
    def _(turn):
        at = pl.ds(pl.multiple_of(turn * chunk, chunk), chunk)
        place = lax.broadcasted_iota(jnp.int32, (cols, chunk), 0)
        for row in range(rows):
            here = pl.ds(row * cols, cols)
            conv = (
                signal[here, at]
                + jnp.where(place == 0, fix[0, row : row + 1, at], 0.0)
                + jnp.where(place == cols - 1, fix[1, row : row + 1, at], 0.0)
            )
            sig = conv * jax.nn.sigmoid(conv)
            signal[here, at] = sig
            weight[here, at] = weight[here, at] * sig

    bc_load.wait()
    coeffs = lax.dot_general(
        signal[...].astype(BF16), w_bc_ref[...], (((1,), (1,)), ((), ())),
        preferred_element_type=F32,
    )
    spread = jnp.concatenate([coeffs[:, :states]] * rows, axis=1)
    src = lax.broadcasted_iota(jnp.int32, spread.shape, 0) // cols
    dst = lax.broadcasted_iota(jnp.int32, spread.shape, 1) // states
    spread = jnp.where(src == dst, spread, 0.0)
    ends = lax.dot_general(
        spread.astype(BF16), weight[...].astype(BF16), (((0,), (0,)), ((), ())),
        preferred_element_type=F32,
    )
    s_send[...] = ends.reshape(rows, states, inner).astype(BF16)

    def send_states(sub, turn):
        owner = lax.rem(me + turn, n)

        @pl.when(owner < owners)
        def _():
            row, at = part_of(owner, sub)
            copy_to(
                s_send.at[row, :, at], s_recv.at[sub, me], s_send_sem, s_recv_sem.at[sub], owner
            ).start()

    for sub in range(subs):

        @pl.loop(1, n)
        def _(turn):
            send_states(sub, turn)

    @pl.when(me < owners)
    def _():
        row, at = block_of(me)
        pltpu.make_async_copy(p_send.at[row, :, at], p_recv.at[me], p_recv_sem).start()
        for sub in range(subs):
            row, at = part_of(me, sub)
            pltpu.make_async_copy(
                s_send.at[row, :, at], s_recv.at[sub, me], s_recv_sem.at[sub]
            ).start()

    turned = coeffs.T
    for p in range(patches):
        full = jnp.broadcast_to(turned[:, p : p + 1], (2 * states, LANES))
        b_full[p] = full[:states]
        c_full[p] = full[states:]
    dv_load.wait()
    vert = dv_ref[...]
    vmix[...] = jnp.sqrt(1.0 - vert * vert)
    weight[...] = hmix[...] * signal[...]
    gate_load.wait()
    half = jnp.dot(
        normalise(x_ref[...].astype(F32)), w_in_ref[:, inner:], preferred_element_type=F32
    )
    half = half.astype(BF16).astype(F32)
    gate[...] = half * jax.nn.sigmoid(half)
    @pl.loop(0, inner // chunk)
    def _(turn):
        at = pl.ds(pl.multiple_of(turn * chunk, chunk), chunk)
        place = lax.broadcasted_iota(jnp.int32, (cols, chunk), 0)
        earlier = []
        for row in range(rows):
            here = pl.ds(row * cols, cols)
            product = dh_ref[here, at]
            step = 1
            while step < cols:
                product = product * jnp.where(place >= step, pltpu.roll(product, step, 0), 1.0)
                step *= 2
            decay = dv_ref[here, at]
            earlier = [decay * value for value in earlier] + [vmix[here, at] * product]
            for source in range(row + 1):
                reach[row * (row + 1) // 2 + source, :, at] = earlier[source]

    out_coef = coeffs[:, states:]
    coarse = out_coef.astype(BF16)
    c_pair[...] = jnp.concatenate(
        [coarse, (out_coef - coarse.astype(F32)).astype(BF16)], axis=1
    )
    skip_load.wait()
    out_load.wait()

    def prefixes(sub):
        drain(s_recv.at[sub], s_recv_sem.at[sub])
        row, at = part_of(me, sub)

        def band(turn, state):
            c_send[sub, turn] = state.astype(BF16)

            @pl.when(turn != me)
            def _():
                copy_to(
                    c_send.at[sub, turn], carry.at[row, :, at], c_send_sem, c_recv_sem.at[sub],
                    turn,
                ).start()

            product = p_recv[turn, :, sub * part : (sub + 1) * part]
            return product * state + s_recv[sub, turn].astype(F32)

        lax.fori_loop(0, n, band, jnp.zeros((states, part), F32))
        pltpu.make_async_copy(
            c_send.at[sub, me], carry.at[row, :, at], c_recv_sem.at[sub]
        ).start()

    def own_part(turn):
        at = pl.ds(pl.multiple_of(turn * LANES, LANES), LANES)
        g = [None] * rows
        for col in range(cols):
            h = None
            for row in range(rows):
                p = row * cols + col
                here = pl.ds(p, 1)
                drive = weight[here, at] * b_full[p]
                g[row] = drive if col == 0 else dh_ref[here, at] * g[row] + drive
                fresh = vmix[here, at] * g[row]
                h = fresh if h is None else dv_ref[here, at] * h + fresh
                scanned[here, at] = jnp.sum(c_full[p] * h, axis=0, keepdims=True)

    turns = inner // LANES
    for sub in range(subs):

        @pl.when(me < owners)
        def _():
            if sub == 0:
                drain(p_recv, p_recv_sem)
            prefixes(sub)

        pl.loop(sub * turns // subs, (sub + 1) * turns // subs)(own_part)

    scanned[...] = scanned[...] + skip_ref[...] * signal[...]

    piece = min(chunk, part)
    for sub in range(subs):
        drain(carry.at[:, :, pl.ds(0, inner // subs)], c_recv_sem.at[sub])
        for turn in range(split * part // piece):
            begin = (turn * piece // part) * width + sub * part + (turn * piece) % part
            at = pl.ds(begin, piece)
            sums = [scanned[pl.ds(row * cols, cols), at] for row in range(rows)]
            for source in range(rows):
                state = carry[source, :, at]
                seen = jnp.dot(
                    c_pair[pl.ds(source * cols, (rows - source) * cols), :],
                    jnp.concatenate([state, state], axis=0),
                    preferred_element_type=F32,
                )
                for row in range(source, rows):
                    sums[row] = sums[row] + (
                        reach[row * (row + 1) // 2 + source, :, at]
                        * seen[(row - source) * cols : (row - source + 1) * cols]
                    )
            for row in range(rows):
                here = pl.ds(row * cols, cols)
                gated[here, at] = (sums[row] * gate[here, at]).astype(BF16)

    out_ref[...] = jnp.dot(gated[...], w_out_ref[...], preferred_element_type=F32).astype(BF16)

    @pl.when(me < owners)
    def _():
        drain(s_recv.at[:, pl.ds(0, owners - 1)], s_send_sem)
        drain(p_recv.at[pl.ds(0, owners - 1)], p_send_sem)
        drain(c_send.at[:, pl.ds(0, n - 1)], c_send_sem)

    if owners < n:

        @pl.when(me >= owners)
        def _():
            drain(s_recv.at[:, pl.ds(0, owners)], s_send_sem)
            drain(p_recv.at[pl.ds(0, owners)], p_send_sem)


def on_device(n, patches, norm_gain, w_in, conv_w, w_bc, skip, w_out, decay_h, decay_v):
    rows, cols, depth = patches.shape
    inner = w_out.shape[0]
    states = w_bc.shape[1] // 2
    split = 1
    while rows * split * 2 <= n and inner // (split * 2) >= LANES:
        split *= 2
    width = inner // split
    subs = 2 if width >= 2 * LANES else 1
    part = width // subs
    count = rows * cols
    vmem = pl.BlockSpec(memory_space=pltpu.VMEM)
    dma = pltpu.SemaphoreType.DMA
    out = pl.pallas_call(
        functools.partial(kernel, n, split, subs, rows, cols, states),
        out_shape=jax.ShapeDtypeStruct((count, w_out.shape[1]), BF16),
        in_specs=[pl.BlockSpec(memory_space=pltpu.HBM)] * 9,
        out_specs=vmem,
        scratch_shapes=[
            pltpu.VMEM((count, depth), BF16),
            pltpu.VMEM((1, depth), F32),
            pltpu.VMEM(w_in.shape, BF16),
            pltpu.VMEM(conv_w.shape, F32),
            pltpu.VMEM((2 * states, inner), BF16),
            pltpu.VMEM((1, inner), F32),
            pltpu.VMEM(w_out.shape, BF16),
            pltpu.VMEM((count, inner), F32),
            pltpu.VMEM((count, inner), F32),
            pltpu.VMEM((2, rows, inner), BF16),
            pltpu.VMEM((2, rows, inner), BF16),
            pltpu.VMEM((rows + 2, cols + 16, inner), F32),
            pltpu.VMEM((count, inner), F32),
            pltpu.VMEM((count, inner), F32),
            pltpu.VMEM((count, inner), F32),
            pltpu.VMEM((count, inner), F32),
            pltpu.VMEM((count, inner), F32),
            pltpu.VMEM((2, rows, inner), F32),
            pltpu.VMEM((count, states, LANES), F32),
            pltpu.VMEM((count, states, LANES), F32),
            pltpu.VMEM((count, inner), F32),
            pltpu.VMEM((rows * (rows + 1) // 2, cols, inner), F32),
            pltpu.VMEM((count, 2 * states), BF16),
            pltpu.VMEM((count, inner), BF16),
            pltpu.VMEM((rows, states, inner), BF16),
            pltpu.VMEM((rows, 1, inner), F32),
            pltpu.VMEM((subs, n, states, part), BF16),
            pltpu.VMEM((n, 1, width), F32),
            pltpu.VMEM((subs, n, states, part), BF16),
            pltpu.VMEM((rows, states, inner), BF16),
            dma((10,)), dma((2,)), dma((2,)), dma, dma((subs,)), dma, dma, dma, dma((subs,)),
        ],
        compiler_params=pltpu.CompilerParams(
            collective_id=0, has_side_effects=True, vmem_limit_bytes=40 << 20
        ),
    )(*[
        pltpu.with_memory_space_constraint(a, pltpu.HBM)
        for a in (
            patches.reshape(count, depth),
            norm_gain.reshape(1, depth),
            w_in,
            conv_w,
            w_bc.T,
            skip.reshape(1, inner),
            w_out,
            decay_h.reshape(count, inner),
            decay_v.reshape(count, inner),
        )
    ])
    return out.reshape(rows, cols, w_out.shape[1])


def solution(mesh):
    n = mesh.shape["cols"]
    banded = P("slides", "cols", None)
    return jax.shard_map(
        functools.partial(on_device, n),
        mesh=mesh,
        in_specs=(banded, P(), P(), P(), P(), P(), P(), banded, banded),
        out_specs=banded,
        check_vma=False,
    )
```

```python
import functools

import jax
import jax.numpy as jnp
from jax import lax
from jax.experimental import pallas as pl
from jax.experimental.pallas import tpu as pltpu
from jax.sharding import PartitionSpec as P

F32 = jnp.float32
BF16 = jnp.bfloat16
LANES = 128


def copy_to(src, dst, send_sem, recv_sem, target):
    return pltpu.make_async_remote_copy(
        src_ref=src,
        dst_ref=dst,
        send_sem=send_sem,
        recv_sem=recv_sem,
        device_id={"cols": target},
        device_id_type=pl.DeviceIdType.MESH,
    )


def drain(ref, sem):
    pltpu.make_async_copy(ref, ref, sem).wait()


def kernel(
    n, split, subs, rows, cols, states,
    x_hbm, gain_hbm, w_in_hbm, conv_hbm, w_bc_hbm, skip_hbm, w_out_hbm, dh_hbm, dv_hbm,
    out_ref,
    x_ref, gain_ref, w_in_ref, conv_ref, w_bc_ref, skip_ref, w_out_ref, dh_ref, dv_ref,
    edge_out, edge_in, fix, edge_conv, edge_scale, edge_drive,
    grid, prefix, scale, signal, drive, ends, gate, across, local, far, near, from_drive, from_carry,
    s_send, p_send, s_recv, p_recv, c_send, carry,
    load_sem, edge_send_sem, edge_recv_sem, s_send_sem, s_recv_sem, p_send_sem, p_recv_sem,
    c_send_sem, c_recv_sem, first_sem,
):
    me = lax.axis_index("cols")
    inner = w_out_ref.shape[0]
    width = inner // split
    part = width // subs
    blocks = rows * split
    owners = min(blocks, n)
    patches = rows * cols
    last = n - 1

    pairs = (
        (x_hbm, x_ref), (gain_hbm, gain_ref), (dh_hbm, dh_ref),
        (w_in_hbm.at[:, pl.ds(0, inner)], w_in_ref.at[:, pl.ds(0, inner)]),
        (conv_hbm, conv_ref),
        (w_in_hbm.at[:, pl.ds(inner, inner)], w_in_ref.at[:, pl.ds(inner, inner)]),
        (w_bc_hbm, w_bc_ref), (dv_hbm, dv_ref), (skip_hbm, skip_ref), (w_out_hbm, w_out_ref),
    )
    loads = [
        pltpu.make_async_copy(src, dst, load_sem.at[k]) for k, (src, dst) in enumerate(pairs)
    ]
    (
        x_load, gain_load, dh_load, branch_load, conv_load, gate_load, bc_load, dv_load,
        skip_load, out_load,
    ) = loads

    early = (x_load, gain_load, dh_load, branch_load, conv_load, bc_load)
    for load in early:
        load.start()

    barrier = pltpu.get_barrier_semaphore()

    def greet(turn, _):
        pl.semaphore_signal(
            barrier,
            inc=1,
            device_id={"cols": lax.rem(me + turn, n)},
            device_id_type=pl.DeviceIdType.MESH,
        )
        return 0

    lax.fori_loop(1, n, greet, 0)
    for load in (gate_load, dv_load, skip_load, out_load):
        load.start()

    chunk = 2 * LANES
    dh_load.wait()

    @pl.loop(0, inner // chunk)
    def _(turn):
        at = pl.ds(pl.multiple_of(turn * chunk, chunk), chunk)
        place = lax.broadcasted_iota(jnp.int32, (cols, chunk), 0)
        for row in range(rows):
            here = pl.ds(row * cols, cols)
            decay = dh_ref[here, at]
            product = decay
            step = 1
            while step < cols:
                product = product * jnp.where(place >= step, pltpu.roll(product, step, 0), 1.0)
                step *= 2
            prefix[here, at] = product
            p_send[row, :, at] = product[cols - 1 : cols]
            rest = 1.0 - decay * decay
            value = rest * lax.rsqrt(rest * (product * product))
            scale[here, at] = value
            edge_scale[pl.ds(row, 1), at] = value[0:1]
            edge_scale[pl.ds(rows + row, 1), at] = value[cols - 1 : cols]

    x_load.wait()
    gain_load.wait()
    feats = x_ref[...].astype(F32)
    meansq = jnp.mean(feats * feats, axis=-1, keepdims=True)
    normed = (feats * lax.rsqrt(meansq + 1e-05) * gain_ref[...]).astype(BF16)
    x_ref[...] = normed
    branch_load.wait()
    branch = jnp.dot(normed, w_in_ref[:, :inner], preferred_element_type=F32)
    branch = branch.astype(BF16).astype(F32)
    grid[pl.ds(0, cols), :] = jnp.zeros((cols, inner), F32)
    grid[pl.ds((rows + 1) * cols, cols), :] = jnp.zeros((cols, inner), F32)
    grid[pl.ds(cols, patches), :] = branch
    for row in range(rows):
        for side, place in ((0, row * cols), (1, (row + 1) * cols - 1)):
            fix[side, row : row + 1, :] = branch[place : place + 1]
    for side in range(2):
        edge_out[side] = fix[side].astype(BF16)

    pl.semaphore_wait(barrier, n - 1)

    to_right = copy_to(
        edge_out.at[1], edge_in.at[0], edge_send_sem.at[0], edge_recv_sem.at[0],
        lax.rem(me + 1, n),
    )
    to_left = copy_to(
        edge_out.at[0], edge_in.at[1], edge_send_sem.at[1], edge_recv_sem.at[1],
        lax.rem(me + n - 1, n),
    )
    to_right.start()
    to_left.start()

    def block_of(owner):
        return owner // split, pl.ds(pl.multiple_of(lax.rem(owner, split) * width, width), width)

    def part_of(owner, sub):
        begin = lax.rem(owner, split) * width + sub * part
        return owner // split, pl.ds(pl.multiple_of(begin, part), part)

    def send_products(turn, _):
        owner = lax.rem(me + turn, n)

        @pl.when(owner < owners)
        def _():
            row, at = block_of(owner)
            copy_to(
                p_send.at[row, :, at], p_recv.at[me], p_send_sem, p_recv_sem, owner
            ).start()

        return 0

    @pl.when(me < last)
    def _():
        lax.fori_loop(1, n, send_products, 0)

    conv_load.wait()

    @pl.loop(0, inner // chunk)
    def _(turn):
        at = pl.ds(pl.multiple_of(turn * chunk, chunk), chunk)
        taps = [[conv_ref[a, pl.ds(b, 1), at] for b in range(3)] for a in range(3)]
        place = lax.broadcasted_iota(jnp.int32, (cols, chunk), 0)
        for row in range(rows):
            here = pl.ds(row * cols, cols)
            lines = [grid[pl.ds((row + a) * cols, cols), at] for a in range(3)]
            parts = [
                taps[0][b] * lines[0] + taps[1][b] * lines[1] + taps[2][b] * lines[2]
                for b in range(3)
            ]
            conv = (
                jnp.where(place > 0, pltpu.roll(parts[0], 1, 0), 0.0)
                + parts[1]
                + jnp.where(place < cols - 1, pltpu.roll(parts[2], cols - 1, 0), 0.0)
            )
            edge_conv[pl.ds(row, 1), at] = conv[0:1]
            edge_conv[pl.ds(rows + row, 1), at] = conv[cols - 1 : cols]
            sig = conv * jax.nn.sigmoid(conv)
            signal[here, at] = sig
            inside = (place > 0) & (place < cols - 1)
            drive[here, at] = jnp.where(inside, sig * scale[here, at], 0.0).astype(BF16)

    def project(values):
        return lax.dot_general(
            values.astype(BF16), w_bc_ref[...], (((1,), (1,)), ((), ())),
            preferred_element_type=F32,
        )

    def place_states(coefs, row_of):
        spread = jnp.concatenate([coefs[:, :states]] * rows, axis=1)
        src = row_of(lax.broadcasted_iota(jnp.int32, spread.shape, 0))
        dst = lax.broadcasted_iota(jnp.int32, spread.shape, 1) // states
        return jnp.where(src == dst, spread, 0.0).astype(BF16)

    bc_load.wait()
    inner_spread = place_states(project(signal[...]), lambda p: p // cols)
    ends[...] = lax.dot_general(
        inner_spread, drive[...], (((0,), (0,)), ((), ())), preferred_element_type=F32
    )

    to_right.wait()
    to_left.wait()
    line = lax.broadcasted_iota(jnp.int32, (rows, inner), 0)
    for side, inside, tap in ((0, me > 0, 0), (1, me < last, 2)):
        edge = edge_in[side].astype(F32) * jnp.where(inside, 1.0, 0.0).astype(F32)
        above = jnp.where(line > 0, pltpu.roll(edge, 1, 0), 0.0)
        below = jnp.where(line < rows - 1, pltpu.roll(edge, rows - 1, 0), 0.0)
        which = pl.ds(side * rows, rows)
        conv = edge_conv[which, :] + (
            conv_ref[0, tap : tap + 1, :] * above
            + conv_ref[1, tap : tap + 1, :] * edge
            + conv_ref[2, tap : tap + 1, :] * below
        )
        sig = conv * jax.nn.sigmoid(conv)
        fix[side] = sig
        edge_drive[which, :] = sig * edge_scale[which, :]
    edge_signal = jnp.concatenate([fix[0], fix[1]], axis=0)
    edge_spread = place_states(project(edge_signal), lambda p: lax.rem(p, rows))
    for begin in range(0, inner, 2 * chunk):
        at = pl.ds(begin, 2 * chunk)
        added = lax.dot_general(
            edge_spread, edge_drive[:, at].astype(BF16), (((0,), (0,)), ((), ())),
            preferred_element_type=F32,
        )
        for row in range(rows):
            which = pl.ds(row * states, states)
            total = ends[which, at] + added[row * states : (row + 1) * states]
            s_send[row, :, at] = (total * p_send[row, :, at]).astype(BF16)

    def send_states(sub, turn):
        owner = lax.rem(me + turn, n)

        @pl.when(owner < owners)
        def _():
            row, at = part_of(owner, sub)
            copy_to(
                s_send.at[row, :, at], s_recv.at[sub, me], s_send_sem, s_recv_sem.at[sub], owner
            ).start()

    @pl.when(me < last)
    def _():
        for sub in range(subs):

            @pl.loop(1, n)
            def _(turn):
                send_states(sub, turn)

    def to_second(sub, half):
        at = pl.ds(half * width + sub * part, part)
        return copy_to(
            s_send.at[:, :, at], carry.at[:, :, at], first_sem, c_recv_sem.at[sub],
            lax.rem(me + 1, n),
        )

    @pl.when(me == 0)
    def _():
        for sub in range(subs):
            for half in range(split):
                to_second(sub, half).start()
        carry[...] = jnp.zeros_like(carry)

    @pl.when((me < owners) & (me < last))
    def _():
        row, at = block_of(me)
        pltpu.make_async_copy(p_send.at[row, :, at], p_recv.at[me], p_recv_sem).start()
        for sub in range(subs):
            row, at = part_of(me, sub)
            pltpu.make_async_copy(
                s_send.at[row, :, at], s_recv.at[sub, me], s_recv_sem.at[sub]
            ).start()

    @pl.loop(0, inner // chunk)
    def _(turn):
        at = pl.ds(pl.multiple_of(turn * chunk, chunk), chunk)
        place = lax.broadcasted_iota(jnp.int32, (cols, chunk), 0)
        for row in range(rows):
            here = pl.ds(row * cols, cols)
            sig = jnp.where(
                place == 0,
                fix[0, row : row + 1, at],
                jnp.where(place == cols - 1, fix[1, row : row + 1, at], signal[here, at]),
            )
            signal[here, at] = sig
            drive[here, at] = (sig * scale[here, at]).astype(BF16)

    coeffs = project(signal[...])
    in_coef, out_coef = coeffs[:, :states], coeffs[:, states:]
    in_high, out_high = in_coef.astype(BF16), out_coef.astype(BF16)
    in_low = (in_coef - in_high.astype(F32)).astype(BF16)
    out_low = (out_coef - out_high.astype(F32)).astype(BF16)
    pairing = lax.dot_general(
        jnp.concatenate([out_high, out_low, out_high], axis=1),
        jnp.concatenate([in_high, in_high, in_low], axis=1),
        (((1,), (1,)), ((), ())),
        preferred_element_type=F32,
    )
    at_row = lax.broadcasted_iota(jnp.int32, pairing.shape, 0)
    at_col = lax.broadcasted_iota(jnp.int32, pairing.shape, 1)
    pairing = jnp.where(lax.rem(at_col, cols) <= lax.rem(at_row, cols), pairing, 0.0)
    high_wide = jnp.concatenate([out_high.astype(F32)] * rows, axis=1)
    low_wide = jnp.concatenate([out_low.astype(F32)] * rows, axis=1)
    wide_col = lax.broadcasted_iota(jnp.int32, high_wide.shape, 1) // states
    begins = [0]
    for source in range(rows):
        begin, count = begins[-1], (rows - source) * cols
        begins.append(begin + count)
        here = pl.ds(begin, count)
        below = slice(source * cols, patches)
        from_drive[here, :] = jnp.where(at_col // cols == source, pairing, 0.0)[below].astype(BF16)
        mine = wide_col == source
        from_carry[here, : rows * states] = jnp.where(mine, high_wide, 0.0)[below].astype(BF16)
        from_carry[here, rows * states :] = jnp.where(mine, low_wide, 0.0)[below].astype(BF16)

    def seen_sum(seen, at):
        sums = [None] * rows
        for source in range(rows):
            reach = across[pl.ds(source * cols, cols), at]
            for row in range(source, rows):
                begin = begins[source] + (row - source) * cols
                term = reach * seen[begin : begin + cols]
                sums[row] = term if sums[row] is None else sums[row] + term
        return sums

    dv_load.wait()
    gate_load.wait()
    skip_load.wait()

    def nearby(turn):
        at = pl.ds(pl.multiple_of(turn * chunk, chunk), chunk)
        half_at = pl.ds(pl.multiple_of(inner + turn * chunk, chunk), chunk)
        half = jnp.dot(x_ref[...], w_in_ref[:, half_at], preferred_element_type=F32)
        half = half.astype(BF16).astype(F32)
        gate[:, at] = half * jax.nn.sigmoid(half)
        down = None
        for row in range(rows):
            here = pl.ds(row * cols, cols)
            decay = dv_ref[here, at]
            down = decay if down is None else down * decay
            rest = 1.0 - decay * decay
            across[here, at] = prefix[here, at] * (rest * lax.rsqrt(rest * (down * down)))
            far[here, at] = down * gate[here, at]
        seen = jnp.dot(from_drive[...], drive[:, at], preferred_element_type=F32)
        sums = seen_sum(seen, at)
        for row in range(rows):
            here = pl.ds(row * cols, cols)
            near[here, at] = (
                far[here, at] * sums[row] + skip_ref[:, at] * signal[here, at] * gate[here, at]
            )

    def prefixes(sub):
        drain(s_recv.at[sub], s_recv_sem.at[sub])
        row, at = part_of(me, sub)

        def band(turn, state):
            @pl.when(turn > 1)
            def _():
                c_send[sub, turn] = state.astype(BF16)

                @pl.when(turn != me)
                def _():
                    copy_to(
                        c_send.at[sub, turn], carry.at[row, :, at], c_send_sem,
                        c_recv_sem.at[sub], turn,
                    ).start()

            product = p_recv[turn, :, sub * part : (sub + 1) * part]
            return product * state + s_recv[sub, turn].astype(F32)

        start = s_recv[sub, 0].astype(F32)
        state = lax.fori_loop(1, last, band, start)
        c_send[sub, last] = state.astype(BF16)

        @pl.when(me != last)
        def _():
            copy_to(
                c_send.at[sub, last], carry.at[row, :, at], c_send_sem, c_recv_sem.at[sub], last
            ).start()

        @pl.when(me > 1)
        def _():
            pltpu.make_async_copy(
                c_send.at[sub, me], carry.at[row, :, at], c_recv_sem.at[sub]
            ).start()

    turns = inner // chunk
    for sub in range(subs):
        pl.loop(sub * turns // subs, (sub + 1) * turns // subs)(nearby)

    for sub in range(subs):

        @pl.when(me < owners)
        def _():
            if sub == 0:
                drain(p_recv, p_recv_sem)
            prefixes(sub)

    out_load.wait()
    piece = min(chunk, part)
    for sub in range(subs):

        @pl.when(me > 0)
        def _():
            drain(carry.at[:, :, pl.ds(0, inner // subs)], c_recv_sem.at[sub])

        for turn in range(split * part // piece):
            begin = (turn * piece // part) * width + sub * part + (turn * piece) % part
            at = pl.ds(begin, piece)
            state = carry[:, :, at].reshape(rows * states, piece)
            seen = jnp.dot(
                from_carry[...], jnp.concatenate([state, state], axis=0),
                preferred_element_type=F32,
            )
            sums = seen_sum(seen, at)
            for row in range(rows):
                here = pl.ds(row * cols, cols)
                local[here, at] = (near[here, at] + far[here, at] * sums[row]).astype(BF16)

    out_ref[...] = jnp.dot(local[...], w_out_ref[...], preferred_element_type=F32).astype(BF16)

    @pl.when(me == 0)
    def _():
        for sub in range(subs):
            for half in range(split):
                to_second(sub, half).wait_send()

    @pl.when(me < owners)
    def _():
        drain(c_send.at[:, pl.ds(0, n - 3)], c_send_sem)

        @pl.when(me < 2)
        def _():
            drain(c_send.at[:, 0], c_send_sem)

        @pl.when(me < last)
        def _():
            drain(c_send.at[:, pl.ds(0, owners - 1)], s_send_sem)
            drain(p_recv.at[pl.ds(0, owners - 1)], p_send_sem)

    if owners < n:

        @pl.when((me >= owners) & (me < last))
        def _():
            drain(c_send.at[:, pl.ds(0, owners)], s_send_sem)
            drain(p_recv.at[pl.ds(0, owners)], p_send_sem)


def on_device(n, patches, norm_gain, w_in, conv_w, w_bc, skip, w_out, decay_h, decay_v):
    rows, cols, depth = patches.shape
    inner = w_out.shape[0]
    states = w_bc.shape[1] // 2
    split = 1
    while rows * split * 2 <= n and inner // (split * 2) >= LANES:
        split *= 2
    width = inner // split
    subs = 2 if width >= 2 * LANES else 1
    part = width // subs
    count = rows * cols
    vmem = pl.BlockSpec(memory_space=pltpu.VMEM)
    dma = pltpu.SemaphoreType.DMA
    out = pl.pallas_call(
        functools.partial(kernel, n, split, subs, rows, cols, states),
        out_shape=jax.ShapeDtypeStruct((count, w_out.shape[1]), BF16),
        in_specs=[pl.BlockSpec(memory_space=pltpu.HBM)] * 9,
        out_specs=vmem,
        scratch_shapes=[
            pltpu.VMEM((count, depth), BF16),
            pltpu.VMEM((1, depth), F32),
            pltpu.VMEM(w_in.shape, BF16),
            pltpu.VMEM(conv_w.shape, F32),
            pltpu.VMEM((2 * states, inner), BF16),
            pltpu.VMEM((1, inner), F32),
            pltpu.VMEM(w_out.shape, BF16),
            pltpu.VMEM((count, inner), F32),
            pltpu.VMEM((count, inner), F32),
            pltpu.VMEM((2, rows, inner), BF16),
            pltpu.VMEM((2, rows, inner), BF16),
            pltpu.VMEM((2, rows, inner), F32),
            pltpu.VMEM((2 * rows, inner), F32),
            pltpu.VMEM((2 * rows, inner), F32),
            pltpu.VMEM((2 * rows, inner), F32),
            pltpu.VMEM((count + 2 * cols, inner), F32),
            pltpu.VMEM((count, inner), F32),
            pltpu.VMEM((count, inner), F32),
            pltpu.VMEM((count, inner), F32),
            pltpu.VMEM((count, inner), BF16),
            pltpu.VMEM((rows * states, inner), F32),
            pltpu.VMEM((count, inner), F32),
            pltpu.VMEM((count, inner), F32),
            pltpu.VMEM((count, inner), BF16),
            pltpu.VMEM((count, inner), F32),
            pltpu.VMEM((count, inner), F32),
            pltpu.VMEM((count * (rows + 1) // 2, count), BF16),
            pltpu.VMEM((count * (rows + 1) // 2, 2 * rows * states), BF16),
            pltpu.VMEM((rows, states, inner), BF16),
            pltpu.VMEM((rows, 1, inner), F32),
            pltpu.VMEM((subs, n - 1, states, part), BF16),
            pltpu.VMEM((n - 1, 1, width), F32),
            pltpu.VMEM((subs, n, states, part), BF16),
            pltpu.VMEM((rows, states, inner), BF16),
            dma((10,)), dma((2,)), dma((2,)), dma, dma((subs,)), dma, dma, dma, dma((subs,)), dma,
        ],
        compiler_params=pltpu.CompilerParams(
            collective_id=0, has_side_effects=True, vmem_limit_bytes=40 << 20
        ),
    )(*[
        pltpu.with_memory_space_constraint(a, pltpu.HBM)
        for a in (
            patches.reshape(count, depth),
            norm_gain.reshape(1, depth),
            w_in,
            conv_w,
            w_bc.T,
            skip.reshape(1, inner),
            w_out,
            decay_h.reshape(count, inner),
            decay_v.reshape(count, inner),
        )
    ])
    return out.reshape(rows, cols, w_out.shape[1])


def solution(mesh):
    n = mesh.shape["cols"]
    banded = P("slides", "cols", None)
    return jax.shard_map(
        functools.partial(on_device, n),
        mesh=mesh,
        in_specs=(banded, P(), P(), P(), P(), P(), P(), banded, banded),
        out_specs=banded,
        check_vma=False,
    )
```

```python
import functools

import jax
import jax.numpy as jnp
from jax import lax
from jax.experimental import pallas as pl
from jax.experimental.pallas import tpu as pltpu
from jax.sharding import PartitionSpec as P

F32 = jnp.float32
BF16 = jnp.bfloat16
LANES = 128
SUBS = 4
AHEAD = 1


def copy_to(src, dst, send_sem, recv_sem, target):
    return pltpu.make_async_remote_copy(
        src_ref=src,
        dst_ref=dst,
        send_sem=send_sem,
        recv_sem=recv_sem,
        device_id={"cols": target},
        device_id_type=pl.DeviceIdType.MESH,
    )


def drain(ref, sem):
    pltpu.make_async_copy(ref, ref, sem).wait()


def kernel(
    n, subs, ahead, rows, cols, states,
    x_hbm, gain_hbm, w_in_hbm, conv_hbm, w_bc_hbm, skip_hbm, w_out_hbm, dh_hbm, dv_hbm,
    out_ref,
    x_ref, gain_ref, w_in_ref, conv_ref, w_bc_ref, skip_ref, w_out_ref, dh_ref, dv_ref,
    edge_out, edge_in, fix, edge_conv, edge_scale, edge_drive,
    grid, prefix, scale, signal, drive, ends, gate, across, local, far, near, from_drive, from_carry,
    s_send, p_send, s_recv, p_recv, c_send, carry, e_send, e_recv, extra, first_state, total_out,
    load_sem, edge_send_sem, edge_recv_sem, s_send_sem, s_recv_sem, p_send_sem, p_recv_sem,
    c_send_sem, c_recv_sem, first_sem, e_send_sem, e_recv_sem,
):
    me = lax.axis_index("cols")
    inner = w_out_ref.shape[0]
    part = inner // subs
    early_part = ahead * part
    patches = rows * cols
    last = n - 1
    first = (n - rows) // 2
    mine = me - first
    owns = (me >= first) & (me < first + rows)

    def each_owner(start_copy):
        half = rows // 2
        far_half = jnp.where(me < n // 2, 1, 0)

        @pl.when(me < last)
        def _():
            @pl.loop(0, rows)
            def _(step):
                side = lax.rem(step // half + far_half, 2)
                row = side * half + lax.rem(step + me, half)

                @pl.when(first + row != me)
                def _():
                    start_copy(row, first + row)


    pairs = (
        (x_hbm, x_ref), (gain_hbm, gain_ref), (dh_hbm, dh_ref),
        (w_in_hbm.at[:, pl.ds(0, inner)], w_in_ref.at[:, pl.ds(0, inner)]),
        (conv_hbm, conv_ref),
        (w_in_hbm.at[:, pl.ds(inner, inner)], w_in_ref.at[:, pl.ds(inner, inner)]),
        (w_bc_hbm, w_bc_ref), (dv_hbm, dv_ref), (skip_hbm, skip_ref), (w_out_hbm, w_out_ref),
    )
    loads = [
        pltpu.make_async_copy(src, dst, load_sem.at[k]) for k, (src, dst) in enumerate(pairs)
    ]
    (
        x_load, gain_load, dh_load, branch_load, conv_load, gate_load, bc_load, dv_load,
        skip_load, out_load,
    ) = loads

    early = (x_load, gain_load, dh_load, branch_load, conv_load, bc_load)
    for load in early:
        load.start()

    barrier = pltpu.get_barrier_semaphore()

    def greet(turn, _):
        pl.semaphore_signal(
            barrier,
            inc=1,
            device_id={"cols": lax.rem(me + turn, n)},
            device_id_type=pl.DeviceIdType.MESH,
        )
        return 0

    lax.fori_loop(1, n, greet, 0)
    for load in (gate_load, dv_load, skip_load, out_load):
        load.start()

    chunk = 2 * LANES
    dh_load.wait()

    @pl.loop(0, inner // chunk)
    def _(turn):
        at = pl.ds(pl.multiple_of(turn * chunk, chunk), chunk)
        place = lax.broadcasted_iota(jnp.int32, (cols, chunk), 0)
        for row in range(rows):
            here = pl.ds(row * cols, cols)
            decay = dh_ref[here, at]
            product = decay
            step = 1
            while step < cols:
                product = product * jnp.where(place >= step, pltpu.roll(product, step, 0), 1.0)
                step *= 2
            prefix[here, at] = product
            p_send[row, :, at] = product[cols - 1 : cols]
            rest = 1.0 - decay * decay
            value = rest * lax.rsqrt(rest * (product * product))
            scale[here, at] = value
            edge_scale[pl.ds(row, 1), at] = value[0:1]
            edge_scale[pl.ds(rows + row, 1), at] = value[cols - 1 : cols]

    x_load.wait()
    gain_load.wait()
    feats = x_ref[...].astype(F32)
    meansq = jnp.mean(feats * feats, axis=-1, keepdims=True)
    normed = (feats * lax.rsqrt(meansq + 1e-05) * gain_ref[...]).astype(BF16)
    x_ref[...] = normed
    branch_load.wait()
    branch = jnp.dot(normed, w_in_ref[:, :inner], preferred_element_type=F32)
    branch = branch.astype(BF16).astype(F32)
    grid[pl.ds(0, cols), :] = jnp.zeros((cols, inner), F32)
    grid[pl.ds((rows + 1) * cols, cols), :] = jnp.zeros((cols, inner), F32)
    grid[pl.ds(cols, patches), :] = branch
    for row in range(rows):
        for side, place in ((0, row * cols), (1, (row + 1) * cols - 1)):
            fix[side, row : row + 1, :] = branch[place : place + 1]
    for side in range(2):
        edge_out[side] = fix[side].astype(BF16)

    pl.semaphore_wait(barrier, n - 1)

    to_right = copy_to(
        edge_out.at[1], edge_in.at[0], edge_send_sem.at[0], edge_recv_sem.at[0],
        lax.rem(me + 1, n),
    )
    to_left = copy_to(
        edge_out.at[0], edge_in.at[1], edge_send_sem.at[1], edge_recv_sem.at[1],
        lax.rem(me + n - 1, n),
    )

    @pl.when(me < last)
    def _():
        to_right.start()

    @pl.when(me > 0)
    def _():
        to_left.start()

    def send_product(row, owner):
        copy_to(p_send.at[row], p_recv.at[me], p_send_sem, p_recv_sem, owner).start()

    each_owner(send_product)
    conv_load.wait()

    @pl.loop(0, inner // chunk)
    def _(turn):
        at = pl.ds(pl.multiple_of(turn * chunk, chunk), chunk)
        taps = [[conv_ref[a, pl.ds(b, 1), at] for b in range(3)] for a in range(3)]
        place = lax.broadcasted_iota(jnp.int32, (cols, chunk), 0)
        for row in range(rows):
            here = pl.ds(row * cols, cols)
            lines = [grid[pl.ds((row + a) * cols, cols), at] for a in range(3)]
            parts = [
                taps[0][b] * lines[0] + taps[1][b] * lines[1] + taps[2][b] * lines[2]
                for b in range(3)
            ]
            conv = (
                jnp.where(place > 0, pltpu.roll(parts[0], 1, 0), 0.0)
                + parts[1]
                + jnp.where(place < cols - 1, pltpu.roll(parts[2], cols - 1, 0), 0.0)
            )
            edge_conv[pl.ds(row, 1), at] = conv[0:1]
            edge_conv[pl.ds(rows + row, 1), at] = conv[cols - 1 : cols]
            sig = conv * jax.nn.sigmoid(conv)
            signal[here, at] = sig
            inside = (place > 0) & (place < cols - 1)
            drive[here, at] = jnp.where(inside, sig * scale[here, at], 0.0).astype(BF16)

    def project(values):
        return lax.dot_general(
            values.astype(BF16), w_bc_ref[...], (((1,), (1,)), ((), ())),
            preferred_element_type=F32,
        )

    def place_states(coefs, row_of):
        spread = jnp.concatenate([coefs[:, :states]] * rows, axis=1)
        src = row_of(lax.broadcasted_iota(jnp.int32, spread.shape, 0))
        dst = lax.broadcasted_iota(jnp.int32, spread.shape, 1) // states
        return jnp.where(src == dst, spread, 0.0).astype(BF16)

    bc_load.wait()
    inner_spread = place_states(project(signal[...]), lambda p: p // cols)
    ends[...] = lax.dot_general(
        inner_spread, drive[...], (((0,), (0,)), ((), ())), preferred_element_type=F32
    )


    def channels(sub):
        return pl.ds(sub * part, part)

    def send_states(sub):
        def send_state(row, owner):
            copy_to(
                s_send.at[row, :, channels(sub)], s_recv.at[sub, me], s_send_sem,
                s_recv_sem.at[sub], owner,
            ).start()

        each_owner(send_state)

    for sub in range(ahead):
        at = channels(sub)
        for row in range(rows):
            total = ends[pl.ds(row * states, states), at]
            s_send[row, :, at] = (total * p_send[row, :, at]).astype(BF16)
        send_states(sub)

    dv_load.wait()
    gate_load.wait()
    skip_load.wait()

    @pl.loop(0, inner // chunk)
    def _(turn):
        at = pl.ds(pl.multiple_of(turn * chunk, chunk), chunk)
        half_at = pl.ds(pl.multiple_of(inner + turn * chunk, chunk), chunk)
        half = jnp.dot(x_ref[...], w_in_ref[:, half_at], preferred_element_type=F32)
        half = half.astype(BF16).astype(F32)
        gate[:, at] = half * jax.nn.sigmoid(half)
        down = None
        for row in range(rows):
            here = pl.ds(row * cols, cols)
            decay = dv_ref[here, at]
            down = decay if down is None else down * decay
            rest = 1.0 - decay * decay
            across[here, at] = prefix[here, at] * (rest * lax.rsqrt(rest * (down * down)))
            far[here, at] = down * gate[here, at]

    @pl.when(me < last)
    def _():
        to_right.wait_send()
        to_left.wait_recv()

    @pl.when(me > 0)
    def _():
        to_left.wait_send()
        to_right.wait_recv()

    line = lax.broadcasted_iota(jnp.int32, (rows, inner), 0)
    for side, inside, tap in ((0, me > 0, 0), (1, me < last, 2)):
        edge = jnp.where(inside, edge_in[side].astype(F32), 0.0)
        above = jnp.where(line > 0, pltpu.roll(edge, 1, 0), 0.0)
        below = jnp.where(line < rows - 1, pltpu.roll(edge, rows - 1, 0), 0.0)
        which = pl.ds(side * rows, rows)
        conv = edge_conv[which, :] + (
            conv_ref[0, tap : tap + 1, :] * above
            + conv_ref[1, tap : tap + 1, :] * edge
            + conv_ref[2, tap : tap + 1, :] * below
        )
        sig = conv * jax.nn.sigmoid(conv)
        fix[side] = sig
        edge_drive[which, :] = sig * edge_scale[which, :]
    edge_signal = jnp.concatenate([fix[0], fix[1]], axis=0)
    edge_coefs = project(edge_signal)
    edge_spread = place_states(edge_coefs, lambda p: lax.rem(p, rows))
    edge_wide = jnp.concatenate([edge_coefs[:, :states]] * rows, axis=1)
    if ahead:
        source = pl.ds(0, early_part)
        for side in range(2):
            for row in range(rows):
                line_at = pl.ds(side * rows + row, 1)
                e_send[row, :, pl.ds(side * early_part, early_part)] = (
                    edge_drive[line_at, source] * p_send[row, :, source]
                )
                e_send[row, :, pl.ds(2 * early_part + side * rows * states, rows * states)] = (
                    edge_wide[side * rows + row : side * rows + row + 1]
                )

        def send_edges(row, owner):
            copy_to(e_send.at[row], e_recv.at[me], e_send_sem, e_recv_sem, owner).start()

        each_owner(send_edges)

    def whole_states(target, sub):
        at = channels(sub)
        added = lax.dot_general(
            edge_spread, edge_drive[:, at].astype(BF16), (((0,), (0,)), ((), ())),
            preferred_element_type=F32,
        )
        for row in range(rows):
            total = ends[pl.ds(row * states, states), at] + (
                added[row * states : (row + 1) * states]
            )
            target[row, :, at] = (total * p_send[row, :, at]).astype(BF16)

    for sub in range(ahead, subs):
        whole_states(s_send, sub)
        send_states(sub)

    def to_second(sub):
        held = first_state if sub < ahead else s_send
        at = channels(sub)
        return copy_to(
            held.at[:, :, at], carry.at[:, :, at], first_sem, c_recv_sem.at[sub],
            lax.rem(me + 1, n),
        )

    @pl.when(me == 0)
    def _():
        for sub in range(subs):
            if sub < ahead:
                whole_states(first_state, sub)
            to_second(sub).start()
        carry[...] = jnp.zeros_like(carry)

    @pl.when(owns & (me < last))
    def _():
        pltpu.make_async_copy(p_send.at[mine], p_recv.at[me], p_recv_sem).start()
        if ahead:
            pltpu.make_async_copy(e_send.at[mine], e_recv.at[me], e_recv_sem).start()
        for sub in range(subs):
            pltpu.make_async_copy(
                s_send.at[mine, :, channels(sub)], s_recv.at[sub, me], s_recv_sem.at[sub]
            ).start()

    @pl.loop(0, inner // chunk)
    def _(turn):
        at = pl.ds(pl.multiple_of(turn * chunk, chunk), chunk)
        place = lax.broadcasted_iota(jnp.int32, (cols, chunk), 0)
        for row in range(rows):
            here = pl.ds(row * cols, cols)
            sig = jnp.where(
                place == 0,
                fix[0, row : row + 1, at],
                jnp.where(place == cols - 1, fix[1, row : row + 1, at], signal[here, at]),
            )
            signal[here, at] = sig
            drive[here, at] = (sig * scale[here, at]).astype(BF16)

    coeffs = project(signal[...])
    in_coef, out_coef = coeffs[:, :states], coeffs[:, states:]
    in_high, out_high = in_coef.astype(BF16), out_coef.astype(BF16)
    in_low = (in_coef - in_high.astype(F32)).astype(BF16)
    out_low = (out_coef - out_high.astype(F32)).astype(BF16)
    pairing = lax.dot_general(
        jnp.concatenate([out_high, out_low, out_high], axis=1),
        jnp.concatenate([in_high, in_high, in_low], axis=1),
        (((1,), (1,)), ((), ())),
        preferred_element_type=F32,
    )
    at_row = lax.broadcasted_iota(jnp.int32, pairing.shape, 0)
    at_col = lax.broadcasted_iota(jnp.int32, pairing.shape, 1)
    pairing = jnp.where(lax.rem(at_col, cols) <= lax.rem(at_row, cols), pairing, 0.0)
    high_wide = jnp.concatenate([out_high.astype(F32)] * rows, axis=1)
    low_wide = jnp.concatenate([out_low.astype(F32)] * rows, axis=1)
    wide_col = lax.broadcasted_iota(jnp.int32, high_wide.shape, 1) // states
    begins = [0]
    for source in range(rows):
        begin, count = begins[-1], (rows - source) * cols
        begins.append(begin + count)
        here = pl.ds(begin, count)
        below = slice(source * cols, patches)
        from_drive[here, :] = jnp.where(at_col // cols == source, pairing, 0.0)[below].astype(BF16)
        placed = wide_col == source
        from_carry[here, : rows * states] = jnp.where(placed, high_wide, 0.0)[below].astype(BF16)
        from_carry[here, rows * states :] = jnp.where(placed, low_wide, 0.0)[below].astype(BF16)

    def seen_sum(seen, at):
        sums = [None] * rows
        for source in range(rows):
            reach = across[pl.ds(source * cols, cols), at]
            for row in range(source, rows):
                begin = begins[source] + (row - source) * cols
                term = reach * seen[begin : begin + cols]
                sums[row] = term if sums[row] is None else sums[row] + term
        return sums

    def nearby(turn):
        at = pl.ds(pl.multiple_of(turn * chunk, chunk), chunk)
        seen = jnp.dot(from_drive[...], drive[:, at], preferred_element_type=F32)
        sums = seen_sum(seen, at)
        for row in range(rows):
            here = pl.ds(row * cols, cols)
            near[here, at] = (
                far[here, at] * sums[row] + skip_ref[:, at] * signal[here, at] * gate[here, at]
            )

    def prefixes(sub):
        drain(s_recv.at[sub], s_recv_sem.at[sub])
        at = channels(sub)
        if sub == 0 and ahead:
            drain(e_recv, e_recv_sem)
            late = e_recv[...].reshape(last, e_recv.shape[-1])
            sums = None
            for side in range(2):
                begin = 2 * early_part + side * rows * states
                wide = jnp.concatenate(
                    [late[:, begin : begin + rows * states]] * -(-last // rows), axis=1
                )
                own = lax.broadcasted_iota(jnp.int32, wide.shape, 1) // states
                own = own == lax.broadcasted_iota(jnp.int32, wide.shape, 0)
                term = lax.dot_general(
                    jnp.where(own, wide, 0.0).astype(BF16),
                    late[:, side * early_part : (side + 1) * early_part].astype(BF16),
                    (((0,), (0,)), ((), ())), preferred_element_type=F32,
                )
                sums = term if sums is None else sums + term
            extra[...] = sums

        def arrived(turn):
            value = s_recv[sub, turn].astype(F32)
            if sub < ahead:
                value = value + extra[pl.ds(turn * states, states), at]
            return value

        def band(turn, state):
            c_send[sub, turn] = state.astype(BF16)
            product = p_recv[turn, :, at]
            return product * state + arrived(turn)

        state = lax.fori_loop(1, last, band, arrived(0))
        c_send[sub, last] = state.astype(BF16)

        @pl.loop(0, n)
        def _(step):
            turn = lax.rem(me + n // 2 + step, n)

            @pl.when((turn != me) & (turn > 1))
            def _():
                copy_to(
                    c_send.at[sub, turn], carry.at[mine, :, at], c_send_sem,
                    c_recv_sem.at[sub], turn,
                ).start()

        @pl.when(me > 1)
        def _():
            pltpu.make_async_copy(
                c_send.at[sub, me], carry.at[mine, :, at], c_recv_sem.at[sub]
            ).start()

    turns = inner // chunk
    for sub in range(subs):
        pl.loop(sub * turns // subs, (sub + 1) * turns // subs)(nearby)

    for sub in range(subs):

        @pl.when(owns)
        def _():
            if sub == 0:
                drain(p_recv, p_recv_sem)
            prefixes(sub)

    out_load.wait()
    piece = min(chunk, part)
    for sub in range(subs):

        @pl.when(me > 0)
        def _():
            drain(carry.at[:, :, pl.ds(0, inner // subs)], c_recv_sem.at[sub])

        for turn in range(part // piece):
            at = pl.ds(sub * part + turn * piece, piece)
            state = carry[:, :, at].reshape(rows * states, piece)
            seen = jnp.dot(
                from_carry[...], jnp.concatenate([state, state], axis=0),
                preferred_element_type=F32,
            )
            sums = seen_sum(seen, at)
            for row in range(rows):
                here = pl.ds(row * cols, cols)
                local[here, at] = (near[here, at] + far[here, at] * sums[row]).astype(BF16)
        result = None if sub == 0 else total_out[...]
        at = channels(sub)
        term = jnp.dot(local[:, at], w_out_ref[at, :], preferred_element_type=F32)
        result = term if result is None else result + term
        if sub == subs - 1:
            out_ref[...] = result.astype(BF16)
        else:
            total_out[...] = result

    @pl.when(me == 0)
    def _():
        for sub in range(subs):
            to_second(sub).wait_send()

    def sent(count):
        drain(c_send.at[:, pl.ds(0, count)], s_send_sem)
        drain(p_recv.at[pl.ds(0, count)], p_send_sem)
        if ahead:
            drain(e_recv.at[pl.ds(0, count)], e_send_sem)

    @pl.when(owns)
    def _():
        drain(c_send.at[:, pl.ds(0, n - 3)], c_send_sem)

        @pl.when(me < 2)
        def _():
            drain(c_send.at[:, 0], c_send_sem)

        @pl.when(me < last)
        def _():
            sent(rows - 1)

    @pl.when(jnp.logical_not(owns) & (me < last))
    def _():
        sent(rows)


def on_device(n, patches, norm_gain, w_in, conv_w, w_bc, skip, w_out, decay_h, decay_v):
    rows, cols, depth = patches.shape
    inner = w_out.shape[0]
    states = w_bc.shape[1] // 2
    subs = SUBS
    ahead = AHEAD
    part = inner // subs
    count = rows * cols
    vmem = pl.BlockSpec(memory_space=pltpu.VMEM)
    dma = pltpu.SemaphoreType.DMA
    out = pl.pallas_call(
        functools.partial(kernel, n, subs, ahead, rows, cols, states),
        out_shape=jax.ShapeDtypeStruct((count, w_out.shape[1]), BF16),
        in_specs=[pl.BlockSpec(memory_space=pltpu.HBM)] * 9,
        out_specs=vmem,
        scratch_shapes=[
            pltpu.VMEM((count, depth), BF16),
            pltpu.VMEM((1, depth), F32),
            pltpu.VMEM(w_in.shape, BF16),
            pltpu.VMEM(conv_w.shape, F32),
            pltpu.VMEM((2 * states, inner), BF16),
            pltpu.VMEM((1, inner), F32),
            pltpu.VMEM(w_out.shape, BF16),
            pltpu.VMEM((count, inner), F32),
            pltpu.VMEM((count, inner), F32),
            pltpu.VMEM((2, rows, inner), BF16),
            pltpu.VMEM((2, rows, inner), BF16),
            pltpu.VMEM((2, rows, inner), F32),
            pltpu.VMEM((2 * rows, inner), F32),
            pltpu.VMEM((2 * rows, inner), F32),
            pltpu.VMEM((2 * rows, inner), F32),
            pltpu.VMEM((count + 2 * cols, inner), F32),
            pltpu.VMEM((count, inner), F32),
            pltpu.VMEM((count, inner), F32),
            pltpu.VMEM((count, inner), F32),
            pltpu.VMEM((count, inner), BF16),
            pltpu.VMEM((rows * states, inner), F32),
            pltpu.VMEM((count, inner), F32),
            pltpu.VMEM((count, inner), F32),
            pltpu.VMEM((count, inner), BF16),
            pltpu.VMEM((count, inner), F32),
            pltpu.VMEM((count, inner), F32),
            pltpu.VMEM((count * (rows + 1) // 2, count), BF16),
            pltpu.VMEM((count * (rows + 1) // 2, 2 * rows * states), BF16),
            pltpu.VMEM((rows, states, inner), BF16),
            pltpu.VMEM((rows, 1, inner), F32),
            pltpu.VMEM((subs, n - 1, states, part), BF16),
            pltpu.VMEM((n - 1, 1, inner), F32),
            pltpu.VMEM((subs, n, states, part), BF16),
            pltpu.VMEM((rows, states, inner), BF16),
            pltpu.VMEM((rows, 1, 2 * ahead * part + 2 * rows * states), F32),
            pltpu.VMEM((n - 1, 1, 2 * ahead * part + 2 * rows * states), F32),
            pltpu.VMEM((-(-(n - 1) // rows) * rows * states, ahead * part), F32),
            pltpu.VMEM((rows, states, inner), BF16),
            pltpu.VMEM((count, w_out.shape[1]), F32),
            dma((10,)), dma((2,)), dma((2,)), dma, dma((subs,)), dma, dma, dma, dma((subs,)), dma, dma, dma,
        ],
        compiler_params=pltpu.CompilerParams(
            collective_id=0, has_side_effects=True, vmem_limit_bytes=40 << 20
        ),
    )(*[
        pltpu.with_memory_space_constraint(a, pltpu.HBM)
        for a in (
            patches.reshape(count, depth),
            norm_gain.reshape(1, depth),
            w_in,
            conv_w,
            w_bc.T,
            skip.reshape(1, inner),
            w_out,
            decay_h.reshape(count, inner),
            decay_v.reshape(count, inner),
        )
    ])
    return out.reshape(rows, cols, w_out.shape[1])


def solution(mesh):
    n = mesh.shape["cols"]
    banded = P("slides", "cols", None)
    return jax.shard_map(
        functools.partial(on_device, n),
        mesh=mesh,
        in_specs=(banded, P(), P(), P(), P(), P(), P(), banded, banded),
        out_specs=banded,
        check_vma=False,
    )
```

```python
import functools

import jax
import jax.numpy as jnp
from jax import lax
from jax.experimental import pallas as pl
from jax.experimental.pallas import tpu as pltpu
from jax.sharding import PartitionSpec as P

F32 = jnp.float32
BF16 = jnp.bfloat16
LANES = 128
SHARES = (2, 2, 2, 2)
DIRECT = (3,)
AHEAD = 1
GROUPS = 4


def cut(inner):
    return [share * inner // 8 for share in SHARES]


def copy_to(src, dst, send_sem, recv_sem, target):
    return pltpu.make_async_remote_copy(
        src_ref=src,
        dst_ref=dst,
        send_sem=send_sem,
        recv_sem=recv_sem,
        device_id={"cols": target},
        device_id_type=pl.DeviceIdType.MESH,
    )


def drain(ref, sem):
    pltpu.make_async_copy(ref, ref, sem).wait()


def kernel(
    n, ahead, rows, cols, states,
    x_hbm, gain_hbm, w_in_hbm, conv_hbm, w_bc_hbm, skip_hbm, w_out_hbm, dh_hbm, dv_hbm,
    out_ref,
    x_ref, gain_ref, w_in_ref, conv_ref, w_bc_ref, skip_ref, w_out_ref, dh_ref, dv_ref,
    edge_out, edge_in, fix, edge_conv, edge_scale, edge_drive,
    grid, prefix, scale, signal, drive, ends, gate, across, local, far, near, from_drive, from_carry,
    s_send, p_send, s_recv, p_recv, c_send, carry, e_send, e_recv, extra, first_state, total_out,
    pair_s, pair_p,
    load_sem, edge_send_sem, edge_recv_sem, s_send_sem, s_recv_sem, p_send_sem, p_recv_sem,
    c_send_sem, c_recv_sem, pair_send_sem, pair_recv_sem, e_send_sem, e_recv_sem,
    f_send_sem, f_recv_sem,
):
    me = lax.axis_index("cols")
    inner = w_out_ref.shape[0]
    sizes = cut(inner)
    subs = len(sizes)
    early_part = sum(sizes[:ahead])
    patches = rows * cols
    last = n - 1
    stride = -(-n // GROUPS)
    first = (n - rows) // 2
    mine = me - first
    owns = (me >= first) & (me < first + rows)

    late_side = lax.rem(me, 2)
    odd = late_side == 1
    sibling = me + 1 - 2 * late_side
    half_rows = rows // 2
    early_at, rest_at = pl.ds(0, early_part), pl.ds(early_part, inner - early_part)

    def each_owner(start_copy, sends=True):
        half = rows // 2
        far_half = jnp.where(me < n // 2, 1, 0)

        @pl.when((me < last) & sends)
        def _():
            @pl.loop(0, rows)
            def _(step):
                side = lax.rem(step // half + far_half, 2)
                row = side * half + lax.rem(step + me, half)

                @pl.when(first + row != me)
                def _():
                    start_copy(row, first + row)


    pairs = (
        (x_hbm, x_ref), (gain_hbm, gain_ref), (dh_hbm, dh_ref),
        (w_in_hbm.at[:, pl.ds(0, inner)], w_in_ref.at[:, pl.ds(0, inner)]),
        (conv_hbm, conv_ref),
        (w_in_hbm.at[:, pl.ds(inner, inner)], w_in_ref.at[:, pl.ds(inner, inner)]),
        (w_bc_hbm, w_bc_ref), (dv_hbm, dv_ref), (skip_hbm, skip_ref), (w_out_hbm, w_out_ref),
    )
    loads = [
        pltpu.make_async_copy(src, dst, load_sem.at[k]) for k, (src, dst) in enumerate(pairs)
    ]
    (
        x_load, gain_load, dh_load, branch_load, conv_load, gate_load, bc_load, dv_load,
        skip_load, out_load,
    ) = loads

    early = (x_load, gain_load, dh_load, branch_load, conv_load, bc_load)
    for load in early:
        load.start()

    barrier = pltpu.get_barrier_semaphore()

    def owner_at(band):
        return (band >= first) & (band < first + rows)

    @pl.loop(1, n)
    def _(turn):
        other = lax.rem(me + turn, n)

        @pl.when(owns | owner_at(other) | (other == me - 1) | (other == me + 1))
        def _():
            pl.semaphore_signal(
                barrier, inc=1, device_id={"cols": other}, device_id_type=pl.DeviceIdType.MESH
            )

    one_left = jnp.where((me > 0) & jnp.logical_not(owner_at(me - 1)), 1, 0)
    one_right = jnp.where((me < last) & jnp.logical_not(owner_at(me + 1)), 1, 0)
    partners = jnp.where(owns, n - 1, rows + one_left + one_right)

    chunk = 2 * LANES
    dh_load.wait()

    @pl.loop(0, inner // chunk)
    def _(turn):
        at = pl.ds(pl.multiple_of(turn * chunk, chunk), chunk)
        place = lax.broadcasted_iota(jnp.int32, (cols, chunk), 0)
        for row in range(rows):
            here = pl.ds(row * cols, cols)
            decay = dh_ref[here, at]
            product = decay
            step = 1
            while step < cols:
                product = product * jnp.where(place >= step, pltpu.roll(product, step, 0), 1.0)
                step *= 2
            prefix[here, at] = product
            p_send[row, :, at] = product[cols - 1 : cols]
            rest = 1.0 - decay * decay
            value = rest * lax.rsqrt(rest * (product * product))
            scale[here, at] = value
            edge_scale[pl.ds(row, 1), at] = value[0:1]
            edge_scale[pl.ds(rows + row, 1), at] = value[cols - 1 : cols]

    x_load.wait()
    gain_load.wait()
    feats = x_ref[...].astype(F32)
    meansq = jnp.mean(feats * feats, axis=-1, keepdims=True)
    normed = (feats * lax.rsqrt(meansq + 1e-05) * gain_ref[...]).astype(BF16)
    x_ref[...] = normed
    branch_load.wait()
    for load in (gate_load, dv_load, skip_load, out_load):
        load.start()
    branch = jnp.dot(normed, w_in_ref[:, :inner], preferred_element_type=F32)
    branch = branch.astype(BF16).astype(F32)
    grid[pl.ds(0, cols), :] = jnp.zeros((cols, inner), F32)
    grid[pl.ds((rows + 1) * cols, cols), :] = jnp.zeros((cols, inner), F32)
    grid[pl.ds(cols, patches), :] = branch
    for row in range(rows):
        for side, place in ((0, row * cols), (1, (row + 1) * cols - 1)):
            fix[side, row : row + 1, :] = branch[place : place + 1]
    for side in range(2):
        edge_out[side] = fix[side].astype(BF16)

    pl.semaphore_wait(barrier, partners)

    to_right = copy_to(
        edge_out.at[1], edge_in.at[0], edge_send_sem.at[0], edge_recv_sem.at[0],
        lax.rem(me + 1, n),
    )
    to_left = copy_to(
        edge_out.at[0], edge_in.at[1], edge_send_sem.at[1], edge_recv_sem.at[1],
        lax.rem(me + n - 1, n),
    )

    @pl.when(me < last)
    def _():
        to_right.start()

    @pl.when(me > 0)
    def _():
        to_left.start()

    def send_product(row, owner):
        copy_to(p_send.at[row], p_recv.at[me], p_send_sem, p_recv_sem, owner).start()

    each_owner(send_product)

    def to_sibling(k):
        source, target = (
            (p_send, pair_p),
            (s_send.at[:, :, rest_at], pair_s.at[:, :, rest_at]),
            (first_state.at[:, :, early_at], pair_s.at[:, :, early_at]),
        )[k]
        return copy_to(source, target, pair_send_sem, pair_recv_sem.at[k], sibling)

    @pl.when(jnp.logical_not(odd))
    def _():
        to_sibling(0).start()

    conv_load.wait()

    @pl.loop(0, inner // chunk)
    def _(turn):
        at = pl.ds(pl.multiple_of(turn * chunk, chunk), chunk)
        taps = [[conv_ref[a, pl.ds(b, 1), at] for b in range(3)] for a in range(3)]
        place = lax.broadcasted_iota(jnp.int32, (cols, chunk), 0)
        for row in range(rows):
            here = pl.ds(row * cols, cols)
            lines = [grid[pl.ds((row + a) * cols, cols), at] for a in range(3)]
            parts = [
                taps[0][b] * lines[0] + taps[1][b] * lines[1] + taps[2][b] * lines[2]
                for b in range(3)
            ]
            conv = (
                jnp.where(place > 0, pltpu.roll(parts[0], 1, 0), 0.0)
                + parts[1]
                + jnp.where(place < cols - 1, pltpu.roll(parts[2], cols - 1, 0), 0.0)
            )
            edge_conv[pl.ds(row, 1), at] = conv[0:1]
            edge_conv[pl.ds(rows + row, 1), at] = conv[cols - 1 : cols]
            sig = conv * jax.nn.sigmoid(conv)
            signal[here, at] = sig
            inside = (place > 0) & (place < cols - 1)
            drive[here, at] = jnp.where(inside, sig * scale[here, at], 0.0).astype(BF16)

    def project(values):
        return lax.dot_general(
            values.astype(BF16), w_bc_ref[...], (((1,), (1,)), ((), ())),
            preferred_element_type=F32,
        )

    def place_states(coefs, row_of):
        spread = jnp.concatenate([coefs[:, :states]] * rows, axis=1)
        src = row_of(lax.broadcasted_iota(jnp.int32, spread.shape, 0))
        dst = lax.broadcasted_iota(jnp.int32, spread.shape, 1) // states
        return jnp.where(src == dst, spread, 0.0).astype(BF16)

    line = lax.broadcasted_iota(jnp.int32, (rows, inner), 0)

    def edge(side):
        present = ((side == 0) & (me > 0)) | ((side == 1) & (me < last))

        @pl.when(present)
        def _():
            drain(edge_in.at[side], edge_recv_sem.at[side])

        value = jnp.where(present, edge_in[side].astype(F32), 0.0)
        above = jnp.where(line > 0, pltpu.roll(value, 1, 0), 0.0)
        below = jnp.where(line < rows - 1, pltpu.roll(value, rows - 1, 0), 0.0)
        which = pl.ds(pl.multiple_of(side * rows, rows), rows)
        tap = pl.ds(2 * side, 1)
        conv = edge_conv[which, :] + (
            conv_ref[0, tap, :] * above
            + conv_ref[1, tap, :] * value
            + conv_ref[2, tap, :] * below
        )
        sig = conv * jax.nn.sigmoid(conv)
        fix[side] = sig
        edge_drive[which, :] = sig * edge_scale[which, :]
        return project(sig), which

    bc_load.wait()
    inner_spread = place_states(project(signal[...]), lambda p: p // cols)
    inner_ends = lax.dot_general(
        inner_spread, drive[...], (((0,), (0,)), ((), ())), preferred_element_type=F32
    )
    soon_coefs, soon_rows = edge(1 - late_side)
    ends[...] = inner_ends + lax.dot_general(
        place_states(soon_coefs, lambda p: p), edge_drive[soon_rows, :].astype(BF16),
        (((0,), (0,)), ((), ())), preferred_element_type=F32,
    )

    def channels(sub):
        return pl.ds(sum(sizes[:sub]), sizes[sub])

    def send_states(sub):
        def send_state(row, owner):
            copy_to(
                s_send.at[row, :, channels(sub)], s_recv.at[me, :, channels(sub)], s_send_sem,
                s_recv_sem.at[sub, me // stride], owner,
            ).start()

        each_owner(send_state, True if sub < ahead else odd)

    for sub in range(ahead):
        at = channels(sub)
        for row in range(rows):
            total = ends[pl.ds(row * states, states), at]
            s_send[row, :, at] = (total * p_send[row, :, at]).astype(BF16)
        send_states(sub)

    late_coefs, late_rows = edge(late_side)
    edge_spread = place_states(late_coefs, lambda p: p)
    edge_wide = jnp.concatenate([late_coefs[:, :states]] * rows, axis=1)

    @pl.when(me < last)
    def _():
        to_right.wait_send()

    @pl.when(me > 0)
    def _():
        to_left.wait_send()

    if ahead:
        source = pl.ds(0, early_part)
        late_drive = edge_drive[late_rows, source]
        for row in range(rows):
            e_send[row, :, source] = late_drive[row : row + 1] * p_send[row, :, source]
            e_send[row, :, pl.ds(early_part, rows * states)] = edge_wide[row : row + 1]

        def send_edges(row, owner):
            copy_to(
                e_send.at[row], e_recv.at[me], e_send_sem, e_recv_sem.at[me // stride], owner
            ).start()

        each_owner(send_edges)

    def whole_states(target, sub):
        at = channels(sub)
        added = lax.dot_general(
            edge_spread, edge_drive[late_rows, at].astype(BF16), (((0,), (0,)), ((), ())),
            preferred_element_type=F32,
        )
        for row in range(rows):
            total = ends[pl.ds(row * states, states), at] + (
                added[row * states : (row + 1) * states]
            )
            target[row, :, at] = (total * p_send[row, :, at]).astype(BF16)

    for sub in range(ahead, subs):
        whole_states(s_send, sub)

    @pl.when(jnp.logical_not(odd))
    def _():
        to_sibling(1).start()
        for sub in range(ahead):
            whole_states(first_state, sub)
        to_sibling(2).start()

    @pl.when(odd)
    def _():
        drain(pair_s.at[:, :, rest_at], pair_recv_sem.at[1])
        for sub in range(ahead, subs):
            at = channels(sub)
            for row in range(rows):
                s_send[row, :, at] = (
                    p_send[row, :, at] * pair_s[row, :, at].astype(F32)
                    + s_send[row, :, at].astype(F32)
                ).astype(BF16)

    for sub in range(ahead, subs):
        send_states(sub)

    @pl.when(me < 2)
    def _():
        carry[...] = jnp.zeros_like(carry)

    @pl.when(owns & (me < last))
    def _():
        pltpu.make_async_copy(p_send.at[mine], p_recv.at[me], p_recv_sem).start()
        if ahead:
            pltpu.make_async_copy(
                e_send.at[mine], e_recv.at[me], e_recv_sem.at[me // stride]
            ).start()

        def keep(sub):
            pltpu.make_async_copy(
                s_send.at[mine, :, channels(sub)], s_recv.at[me, :, channels(sub)],
                s_recv_sem.at[sub, me // stride],
            ).start()

        for sub in range(ahead):
            keep(sub)

        @pl.when(odd)
        def _():
            for sub in range(ahead, subs):
                keep(sub)


    dv_load.wait()
    gate_load.wait()
    skip_load.wait()

    @pl.loop(0, inner // chunk)
    def _(turn):
        at = pl.ds(pl.multiple_of(turn * chunk, chunk), chunk)
        half_at = pl.ds(pl.multiple_of(inner + turn * chunk, chunk), chunk)
        half = jnp.dot(x_ref[...], w_in_ref[:, half_at], preferred_element_type=F32)
        half = half.astype(BF16).astype(F32)
        gate[:, at] = half * jax.nn.sigmoid(half)
        down = None
        for row in range(rows):
            here = pl.ds(row * cols, cols)
            decay = dv_ref[here, at]
            down = decay if down is None else down * decay
            rest = 1.0 - decay * decay
            across[here, at] = prefix[here, at] * (rest * lax.rsqrt(rest * (down * down)))
            far[here, at] = down * gate[here, at]

    @pl.loop(0, inner // chunk)
    def _(turn):
        at = pl.ds(pl.multiple_of(turn * chunk, chunk), chunk)
        place = lax.broadcasted_iota(jnp.int32, (cols, chunk), 0)
        for row in range(rows):
            here = pl.ds(row * cols, cols)
            sig = jnp.where(
                place == 0,
                fix[0, row : row + 1, at],
                jnp.where(place == cols - 1, fix[1, row : row + 1, at], signal[here, at]),
            )
            signal[here, at] = sig
            drive[here, at] = (sig * scale[here, at]).astype(BF16)

    coeffs = project(signal[...])
    in_coef, out_coef = coeffs[:, :states], coeffs[:, states:]
    in_high, out_high = in_coef.astype(BF16), out_coef.astype(BF16)
    in_low = (in_coef - in_high.astype(F32)).astype(BF16)
    out_low = (out_coef - out_high.astype(F32)).astype(BF16)
    pairing = lax.dot_general(
        jnp.concatenate([out_high, out_low, out_high], axis=1),
        jnp.concatenate([in_high, in_high, in_low], axis=1),
        (((1,), (1,)), ((), ())),
        preferred_element_type=F32,
    )
    at_row = lax.broadcasted_iota(jnp.int32, pairing.shape, 0)
    at_col = lax.broadcasted_iota(jnp.int32, pairing.shape, 1)
    pairing = jnp.where(lax.rem(at_col, cols) <= lax.rem(at_row, cols), pairing, 0.0)
    high_wide = jnp.concatenate([out_high.astype(F32)] * rows, axis=1)
    low_wide = jnp.concatenate([out_low.astype(F32)] * rows, axis=1)
    wide_col = lax.broadcasted_iota(jnp.int32, high_wide.shape, 1) // states
    begins = [0]
    for source in range(rows):
        begin, count = begins[-1], (rows - source) * cols
        begins.append(begin + count)
        here = pl.ds(begin, count)
        below = slice(source * cols, patches)
        from_drive[here, :] = jnp.where(at_col // cols == source, pairing, 0.0)[below].astype(BF16)
        placed = wide_col == source
        from_carry[here, : rows * states] = jnp.where(placed, high_wide, 0.0)[below].astype(BF16)
        from_carry[here, rows * states :] = jnp.where(placed, low_wide, 0.0)[below].astype(BF16)

    def seen_sum(seen, at):
        sums = [None] * rows
        for source in range(rows):
            reach = across[pl.ds(source * cols, cols), at]
            for row in range(source, rows):
                begin = begins[source] + (row - source) * cols
                term = reach * seen[begin : begin + cols]
                sums[row] = term if sums[row] is None else sums[row] + term
        return sums

    def nearby(turn):
        at = pl.ds(pl.multiple_of(turn * chunk, chunk), chunk)
        seen = jnp.dot(from_drive[...], drive[:, at], preferred_element_type=F32)
        sums = seen_sum(seen, at)
        for row in range(rows):
            here = pl.ds(row * cols, cols)
            near[here, at] = (
                far[here, at] * sums[row] + skip_ref[:, at] * signal[here, at] * gate[here, at]
            )

    def late_states(begin, count):
        late = e_recv[pl.ds(begin, count)].reshape(count, e_recv.shape[-1])
        wide = jnp.concatenate([late[:, early_part:]] * -(-count // rows), axis=1)
        wide = wide[:, : count * states]
        own = lax.broadcasted_iota(jnp.int32, wide.shape, 1) // states
        own = own == lax.broadcasted_iota(jnp.int32, wide.shape, 0)
        extra[pl.ds(begin * states, count * states), :] = lax.dot_general(
            jnp.where(own, wide, 0.0).astype(BF16), late[:, :early_part].astype(BF16),
            (((0,), (0,)), ((), ())), preferred_element_type=F32,
        )

    core = jnp.where(mine < half_rows, 0, 1)

    def prefixes(sub):
        at = channels(sub)

        def send_carry(even, to):
            @pl.when(to != me)
            def _():
                copy_to(
                    c_send.at[even, :, at], carry.at[mine, :, at], c_send_sem,
                    c_recv_sem.at[sub], to,
                ).start()

            @pl.when(to == me)
            def _():
                pltpu.make_async_copy(
                    c_send.at[even, :, at], carry.at[mine, :, at], c_recv_sem.at[sub]
                ).start()

        def chip(turn, state):
            left, right = 2 * turn, 2 * turn + 1
            if sub < ahead:
                for band in (left, right):
                    value = s_recv[band, :, at].astype(F32)
                    value = value + extra[pl.ds(band * states, states), at]
                    state = p_recv[band, :, at] * state + value
            else:
                product = p_recv[left, :, at] * p_recv[right, :, at]
                state = product * state + s_recv[right, :, at].astype(F32)
            even = left + 2
            c_send[even, :, at] = state.astype(BF16)
            if sub in DIRECT:
                send_carry(even, even)
                send_carry(even, even + 1)
            else:
                send_carry(even, even + core)
            return state

        state = jnp.zeros((states, sizes[sub]), F32)
        for group in range(GROUPS):
            begin = min(group * stride, last)
            end = min(begin + stride, last)
            stop = min((begin + stride) // 2, n // 2 - 1)
            if begin < end:
                if sub < ahead:
                    drain(s_recv.at[pl.ds(begin, end - begin), :, at], s_recv_sem.at[sub, group])
                else:
                    arrivals = stop - begin // 2
                    drain(s_recv.at[pl.ds(begin, arrivals), :, at], s_recv_sem.at[sub, group])
                if sub == 0 and ahead:
                    drain(e_recv.at[pl.ds(begin, end - begin)], e_recv_sem.at[group])
                    late_states(begin, end - begin)
                state = lax.fori_loop(begin // 2, stop, chip, state, unroll=True)

    pl.loop(0, inner // chunk)(nearby)

    for sub in range(subs):

        @pl.when(owns)
        def _():
            if sub == 0:
                drain(p_recv, p_recv_sem)
            prefixes(sub)

    out_load.wait()

    def forward(sub):
        which = pl.ds(late_side * half_rows, half_rows)
        at = channels(sub)
        return copy_to(
            carry.at[which, :, at], carry.at[which, :, at], f_send_sem.at[sub],
            f_recv_sem.at[sub], sibling,
        )

    def take(sub):
        @pl.when(me > 1)
        def _():
            count = rows if sub in DIRECT else half_rows
            drain(carry.at[pl.ds(0, count), :, channels(sub)], c_recv_sem.at[sub])
            if sub not in DIRECT:
                forward(sub).start()

    def finish(sub):
        if sub not in DIRECT:

            @pl.when(me > 1)
            def _():
                forward(sub).wait()

        for turn in range(-(-sizes[sub] // chunk)):
            piece = min(chunk, sizes[sub] - turn * chunk)
            at = pl.ds(sum(sizes[:sub]) + turn * chunk, piece)
            state = carry[:, :, at]
            second = pair_p[:, :, at] * state.astype(F32) + pair_s[:, :, at].astype(F32)
            state = jnp.where(odd, second, state.astype(F32)).astype(BF16)
            state = state.reshape(rows * states, piece)
            seen = jnp.dot(
                from_carry[...], jnp.concatenate([state, state], axis=0),
                preferred_element_type=F32,
            )
            sums = seen_sum(seen, at)
            for row in range(rows):
                here = pl.ds(row * cols, cols)
                local[here, at] = (near[here, at] + far[here, at] * sums[row]).astype(BF16)
        result = None if sub == 0 else total_out[...]
        at = channels(sub)
        term = jnp.dot(local[:, at], w_out_ref[at, :], preferred_element_type=F32)
        result = term if result is None else result + term
        if sub == subs - 1:
            out_ref[...] = result.astype(BF16)
        else:
            total_out[...] = result

    @pl.when(odd)
    def _():
        drain(pair_p, pair_recv_sem.at[0])
        drain(pair_s.at[:, :, early_at], pair_recv_sem.at[2])

    for sub in range(subs):
        take(sub)
        if sub > 0:
            finish(sub - 1)
    finish(subs - 1)

    @pl.when(jnp.logical_not(odd))
    def _():
        for k in range(3):
            to_sibling(k).wait_send()

    def sent(count):
        drain(c_send.at[pl.ds(0, count), :, early_at], s_send_sem)
        drain(p_recv.at[pl.ds(0, count)], p_send_sem)
        if ahead:
            drain(e_recv.at[pl.ds(0, count)], e_send_sem)

        @pl.when(odd)
        def _():
            drain(c_send.at[pl.ds(0, count), :, rest_at], s_send_sem)

    @pl.when(owns)
    def _():
        for sub in range(subs):
            at = channels(sub)
            if sub in DIRECT:
                own_target, least = me > 1, n - 3
            else:
                own_target, least = (me > 1) & (core == late_side), n // 2 - 2
            drain(c_send.at[pl.ds(0, least), :, at], c_send_sem)

            @pl.when(jnp.logical_not(own_target))
            def _():
                drain(c_send.at[0, :, at], c_send_sem)

        @pl.when(me < last)
        def _():
            sent(rows - 1)

    @pl.when(jnp.logical_not(owns) & (me < last))
    def _():
        sent(rows)


def on_device(n, patches, norm_gain, w_in, conv_w, w_bc, skip, w_out, decay_h, decay_v):
    rows, cols, depth = patches.shape
    inner = w_out.shape[0]
    states = w_bc.shape[1] // 2
    sizes = cut(inner)
    subs = len(sizes)
    ahead = AHEAD
    early_part = sum(sizes[:ahead])
    count = rows * cols
    vmem = pl.BlockSpec(memory_space=pltpu.VMEM)
    dma = pltpu.SemaphoreType.DMA
    out = pl.pallas_call(
        functools.partial(kernel, n, ahead, rows, cols, states),
        out_shape=jax.ShapeDtypeStruct((count, w_out.shape[1]), BF16),
        in_specs=[pl.BlockSpec(memory_space=pltpu.HBM)] * 9,
        out_specs=vmem,
        scratch_shapes=[
            pltpu.VMEM((count, depth), BF16),
            pltpu.VMEM((1, depth), F32),
            pltpu.VMEM(w_in.shape, BF16),
            pltpu.VMEM(conv_w.shape, F32),
            pltpu.VMEM((2 * states, inner), BF16),
            pltpu.VMEM((1, inner), F32),
            pltpu.VMEM(w_out.shape, BF16),
            pltpu.VMEM((count, inner), F32),
            pltpu.VMEM((count, inner), F32),
            pltpu.VMEM((2, rows, inner), BF16),
            pltpu.VMEM((2, rows, inner), BF16),
            pltpu.VMEM((2, rows, inner), F32),
            pltpu.VMEM((2 * rows, inner), F32),
            pltpu.VMEM((2 * rows, inner), F32),
            pltpu.VMEM((2 * rows, inner), F32),
            pltpu.VMEM((count + 2 * cols, inner), F32),
            pltpu.VMEM((count, inner), F32),
            pltpu.VMEM((count, inner), F32),
            pltpu.VMEM((count, inner), F32),
            pltpu.VMEM((count, inner), BF16),
            pltpu.VMEM((rows * states, inner), F32),
            pltpu.VMEM((count, inner), F32),
            pltpu.VMEM((count, inner), F32),
            pltpu.VMEM((count, inner), BF16),
            pltpu.VMEM((count, inner), F32),
            pltpu.VMEM((count, inner), F32),
            pltpu.VMEM((count * (rows + 1) // 2, count), BF16),
            pltpu.VMEM((count * (rows + 1) // 2, 2 * rows * states), BF16),
            pltpu.VMEM((rows, states, inner), BF16),
            pltpu.VMEM((rows, 1, inner), F32),
            pltpu.VMEM((n - 1, states, inner), BF16),
            pltpu.VMEM((n - 1, 1, inner), F32),
            pltpu.VMEM((n, states, inner), BF16),
            pltpu.VMEM((rows, states, inner), BF16),
            pltpu.VMEM((rows, 1, early_part + rows * states), F32),
            pltpu.VMEM((n - 1, 1, early_part + rows * states), F32),
            pltpu.VMEM((-(-(n - 1) // rows) * rows * states, early_part), F32),
            pltpu.VMEM((rows, states, inner), BF16),
            pltpu.VMEM((count, w_out.shape[1]), F32),
            pltpu.VMEM((rows, states, inner), BF16),
            pltpu.VMEM((rows, 1, inner), F32),
            dma((10,)), dma((2,)), dma((2,)), dma, dma((subs, GROUPS)), dma, dma, dma, dma((subs,)), dma,
            dma((3,)), dma, dma((GROUPS,)), dma((subs,)), dma((subs,)),
        ],
        compiler_params=pltpu.CompilerParams(
            collective_id=0, has_side_effects=True, vmem_limit_bytes=40 << 20
        ),
    )(*[
        pltpu.with_memory_space_constraint(a, pltpu.HBM)
        for a in (
            patches.reshape(count, depth),
            norm_gain.reshape(1, depth),
            w_in,
            conv_w,
            w_bc.T,
            skip.reshape(1, inner),
            w_out,
            decay_h.reshape(count, inner),
            decay_v.reshape(count, inner),
        )
    ])
    return out.reshape(rows, cols, w_out.shape[1])


def solution(mesh):
    n = mesh.shape["cols"]
    banded = P("slides", "cols", None)
    return jax.shard_map(
        functools.partial(on_device, n),
        mesh=mesh,
        in_specs=(banded, P(), P(), P(), P(), P(), P(), banded, banded),
        out_specs=banded,
        check_vma=False,
    )
```

```python
import functools

import jax
import jax.numpy as jnp
from jax import lax
from jax.experimental import pallas as pl
from jax.experimental.pallas import tpu as pltpu
from jax.sharding import PartitionSpec as P

F32 = jnp.float32
BF16 = jnp.bfloat16
LANES = 128
SHARES = (3, 3, 2)
DIRECT = (2,)
AHEAD = 1
GROUPS = 4


def cut(inner):
    return [share * inner // 8 for share in SHARES]


def copy_to(src, dst, send_sem, recv_sem, target):
    return pltpu.make_async_remote_copy(
        src_ref=src,
        dst_ref=dst,
        send_sem=send_sem,
        recv_sem=recv_sem,
        device_id={"cols": target},
        device_id_type=pl.DeviceIdType.MESH,
    )


def drain(ref, sem):
    pltpu.make_async_copy(ref, ref, sem).wait()


def kernel(
    n, ahead, rows, cols, states,
    x_hbm, gain_hbm, w_in_hbm, conv_hbm, w_bc_hbm, skip_hbm, w_out_hbm, dh_hbm, dv_hbm,
    out_ref,
    x_ref, gain_ref, w_in_ref, conv_ref, w_bc_ref, skip_ref, w_out_ref, dh_ref, dv_ref,
    edge_out, edge_in, fix, edge_conv, edge_scale, edge_drive,
    grid, prefix, scale, signal, drive, ends, gate, across, local, far, near, from_drive, from_carry,
    s_send, p_send, s_recv, p_recv, c_send, carry, e_send, e_recv, extra, first_state, total_out,
    pair_s, pair_p, pair_early,
    load_sem, edge_send_sem, edge_recv_sem, s_send_sem, s_recv_sem, p_send_sem, p_recv_sem,
    c_send_sem, c_recv_sem, pair_send_sem, pair_recv_sem, e_send_sem, e_recv_sem,
    f_send_sem, f_recv_sem,
):
    me = lax.axis_index("cols")
    inner = w_out_ref.shape[0]
    sizes = cut(inner)
    subs = len(sizes)
    early_part = sum(sizes[:ahead])
    patches = rows * cols
    last = n - 1
    stride = -(-n // GROUPS)
    first = (n - rows) // 2
    mine = me - first
    owns = (me >= first) & (me < first + rows)

    late_side = lax.rem(me, 2)
    odd = late_side == 1
    sibling = me + 1 - 2 * late_side
    half_rows = rows // 2
    early_at, rest_at = pl.ds(0, early_part), pl.ds(early_part, inner - early_part)

    def each_owner(start_copy, sends=True):
        half = rows // 2
        far_half = jnp.where(me < n // 2, 1, 0)

        @pl.when((me < last) & sends)
        def _():
            @pl.loop(0, rows)
            def _(step):
                side = lax.rem(step // half + far_half, 2)
                row = side * half + lax.rem(step + me, half)

                @pl.when(first + row != me)
                def _():
                    start_copy(row, first + row)


    pairs = (
        (x_hbm, x_ref), (gain_hbm, gain_ref), (dh_hbm, dh_ref),
        (w_in_hbm.at[:, pl.ds(0, inner)], w_in_ref.at[:, pl.ds(0, inner)]),
        (conv_hbm, conv_ref),
        (w_in_hbm.at[:, pl.ds(inner, inner)], w_in_ref.at[:, pl.ds(inner, inner)]),
        (w_bc_hbm, w_bc_ref), (dv_hbm, dv_ref), (skip_hbm, skip_ref), (w_out_hbm, w_out_ref),
    )
    loads = [
        pltpu.make_async_copy(src, dst, load_sem.at[k]) for k, (src, dst) in enumerate(pairs)
    ]
    (
        x_load, gain_load, dh_load, branch_load, conv_load, gate_load, bc_load, dv_load,
        skip_load, out_load,
    ) = loads

    early = (x_load, gain_load, dh_load, branch_load, conv_load, bc_load)
    for load in early:
        load.start()

    barrier = pltpu.get_barrier_semaphore()

    def owner_at(band):
        return (band >= first) & (band < first + rows)

    @pl.loop(1, n)
    def _(turn):
        other = lax.rem(me + turn, n)

        @pl.when(owns | owner_at(other) | (other == me - 1) | (other == me + 1))
        def _():
            pl.semaphore_signal(
                barrier, inc=1, device_id={"cols": other}, device_id_type=pl.DeviceIdType.MESH
            )

    one_left = jnp.where((me > 0) & jnp.logical_not(owner_at(me - 1)), 1, 0)
    one_right = jnp.where((me < last) & jnp.logical_not(owner_at(me + 1)), 1, 0)
    partners = jnp.where(owns, n - 1, rows + one_left + one_right)

    chunk = 2 * LANES
    dh_load.wait()

    @pl.loop(0, inner // chunk)
    def _(turn):
        at = pl.ds(pl.multiple_of(turn * chunk, chunk), chunk)
        place = lax.broadcasted_iota(jnp.int32, (cols, chunk), 0)
        for row in range(rows):
            here = pl.ds(row * cols, cols)
            decay = dh_ref[here, at]
            product = decay
            step = 1
            while step < cols:
                product = product * jnp.where(place >= step, pltpu.roll(product, step, 0), 1.0)
                step *= 2
            prefix[here, at] = product
            p_send[row, :, at] = product[cols - 1 : cols]
            rest = 1.0 - decay * decay
            value = rest * lax.rsqrt(rest * (product * product))
            scale[here, at] = value
            edge_scale[pl.ds(row, 1), at] = value[0:1]
            edge_scale[pl.ds(rows + row, 1), at] = value[cols - 1 : cols]

    x_load.wait()
    gain_load.wait()
    feats = x_ref[...].astype(F32)
    meansq = jnp.mean(feats * feats, axis=-1, keepdims=True)
    normed = (feats * lax.rsqrt(meansq + 1e-05) * gain_ref[...]).astype(BF16)
    x_ref[...] = normed
    branch_load.wait()
    for load in (gate_load, dv_load, skip_load, out_load):
        load.start()
    branch = jnp.dot(normed, w_in_ref[:, :inner], preferred_element_type=F32)
    branch = branch.astype(BF16).astype(F32)
    grid[pl.ds(0, cols), :] = jnp.zeros((cols, inner), F32)
    grid[pl.ds((rows + 1) * cols, cols), :] = jnp.zeros((cols, inner), F32)
    grid[pl.ds(cols, patches), :] = branch
    for row in range(rows):
        for side, place in ((0, row * cols), (1, (row + 1) * cols - 1)):
            fix[side, row : row + 1, :] = branch[place : place + 1]
    for side in range(2):
        edge_out[side] = fix[side].astype(BF16)

    pl.semaphore_wait(barrier, partners)

    to_right = copy_to(
        edge_out.at[1], edge_in.at[0], edge_send_sem.at[0], edge_recv_sem.at[0],
        lax.rem(me + 1, n),
    )
    to_left = copy_to(
        edge_out.at[0], edge_in.at[1], edge_send_sem.at[1], edge_recv_sem.at[1],
        lax.rem(me + n - 1, n),
    )

    @pl.when(me < last)
    def _():
        to_right.start()

    @pl.when(me > 0)
    def _():
        to_left.start()

    def send_product(row, owner):
        copy_to(p_send.at[row], p_recv.at[me], p_send_sem, p_recv_sem, owner).start()

    each_owner(send_product)

    def to_sibling(k):
        source, target = (
            (p_send, pair_p),
            (s_send.at[:, :, rest_at], pair_s.at[:, :, rest_at]),
            (first_state.at[:, :, early_at], pair_s.at[:, :, early_at]),
            (s_send.at[:, :, early_at], pair_early),
        )[k]
        return copy_to(source, target, pair_send_sem, pair_recv_sem.at[k], sibling)

    @pl.when(jnp.logical_not(odd))
    def _():
        to_sibling(0).start()

    conv_load.wait()

    @pl.loop(0, inner // chunk)
    def _(turn):
        at = pl.ds(pl.multiple_of(turn * chunk, chunk), chunk)
        taps = [[conv_ref[a, pl.ds(b, 1), at] for b in range(3)] for a in range(3)]
        place = lax.broadcasted_iota(jnp.int32, (cols, chunk), 0)
        for row in range(rows):
            here = pl.ds(row * cols, cols)
            lines = [grid[pl.ds((row + a) * cols, cols), at] for a in range(3)]
            parts = [
                taps[0][b] * lines[0] + taps[1][b] * lines[1] + taps[2][b] * lines[2]
                for b in range(3)
            ]
            conv = (
                jnp.where(place > 0, pltpu.roll(parts[0], 1, 0), 0.0)
                + parts[1]
                + jnp.where(place < cols - 1, pltpu.roll(parts[2], cols - 1, 0), 0.0)
            )
            edge_conv[pl.ds(row, 1), at] = conv[0:1]
            edge_conv[pl.ds(rows + row, 1), at] = conv[cols - 1 : cols]
            sig = conv * jax.nn.sigmoid(conv)
            signal[here, at] = sig
            inside = (place > 0) & (place < cols - 1)
            drive[here, at] = jnp.where(inside, sig * scale[here, at], 0.0).astype(BF16)

    def project(values):
        return lax.dot_general(
            values.astype(BF16), w_bc_ref[...], (((1,), (1,)), ((), ())),
            preferred_element_type=F32,
        )

    def place_states(coefs, row_of):
        spread = jnp.concatenate([coefs[:, :states]] * rows, axis=1)
        src = row_of(lax.broadcasted_iota(jnp.int32, spread.shape, 0))
        dst = lax.broadcasted_iota(jnp.int32, spread.shape, 1) // states
        return jnp.where(src == dst, spread, 0.0).astype(BF16)

    line = lax.broadcasted_iota(jnp.int32, (rows, inner), 0)

    def edge(side):
        present = ((side == 0) & (me > 0)) | ((side == 1) & (me < last))

        @pl.when(present)
        def _():
            drain(edge_in.at[side], edge_recv_sem.at[side])

        value = jnp.where(present, edge_in[side].astype(F32), 0.0)
        above = jnp.where(line > 0, pltpu.roll(value, 1, 0), 0.0)
        below = jnp.where(line < rows - 1, pltpu.roll(value, rows - 1, 0), 0.0)
        which = pl.ds(pl.multiple_of(side * rows, rows), rows)
        tap = pl.ds(2 * side, 1)
        conv = edge_conv[which, :] + (
            conv_ref[0, tap, :] * above
            + conv_ref[1, tap, :] * value
            + conv_ref[2, tap, :] * below
        )
        sig = conv * jax.nn.sigmoid(conv)
        fix[side] = sig
        edge_drive[which, :] = sig * edge_scale[which, :]
        return project(sig), which

    bc_load.wait()
    inner_spread = place_states(project(signal[...]), lambda p: p // cols)
    inner_ends = lax.dot_general(
        inner_spread, drive[...], (((0,), (0,)), ((), ())), preferred_element_type=F32
    )
    soon_coefs, soon_rows = edge(1 - late_side)
    ends[...] = inner_ends + lax.dot_general(
        place_states(soon_coefs, lambda p: p), edge_drive[soon_rows, :].astype(BF16),
        (((0,), (0,)), ((), ())), preferred_element_type=F32,
    )

    def channels(sub):
        return pl.ds(sum(sizes[:sub]), sizes[sub])

    def send_states(sub):
        def send_state(row, owner):
            copy_to(
                s_send.at[row, :, channels(sub)], s_recv.at[me, :, channels(sub)], s_send_sem,
                s_recv_sem.at[sub, me // stride], owner,
            ).start()

        each_owner(send_state, odd)

    for sub in range(ahead):
        at = channels(sub)
        for row in range(rows):
            total = ends[pl.ds(row * states, states), at]
            s_send[row, :, at] = (total * p_send[row, :, at]).astype(BF16)

    def add_pair(sub, source):
        at = channels(sub)
        for row in range(rows):
            s_send[row, :, at] = (
                p_send[row, :, at] * source[row, :, at].astype(F32)
                + s_send[row, :, at].astype(F32)
            ).astype(BF16)

    @pl.when(jnp.logical_not(odd))
    def _():
        to_sibling(3).start()

    dv_load.wait()
    gate_load.wait()
    skip_load.wait()

    @pl.loop(0, inner // chunk)
    def _(turn):
        at = pl.ds(pl.multiple_of(turn * chunk, chunk), chunk)
        half_at = pl.ds(pl.multiple_of(inner + turn * chunk, chunk), chunk)
        half = jnp.dot(x_ref[...], w_in_ref[:, half_at], preferred_element_type=F32)
        half = half.astype(BF16).astype(F32)
        gate[:, at] = half * jax.nn.sigmoid(half)
        down = None
        for row in range(rows):
            here = pl.ds(row * cols, cols)
            decay = dv_ref[here, at]
            down = decay if down is None else down * decay
            rest = 1.0 - decay * decay
            across[here, at] = prefix[here, at] * (rest * lax.rsqrt(rest * (down * down)))
            far[here, at] = down * gate[here, at]

    @pl.when(odd)
    def _():
        drain(pair_early, pair_recv_sem.at[3])
        for sub in range(ahead):
            add_pair(sub, pair_early)

    for sub in range(ahead):
        send_states(sub)


    late_coefs, late_rows = edge(late_side)
    edge_spread = place_states(late_coefs, lambda p: p)
    edge_wide = jnp.concatenate([late_coefs[:, :states]] * rows, axis=1)

    @pl.when(me < last)
    def _():
        to_right.wait_send()

    @pl.when(me > 0)
    def _():
        to_left.wait_send()

    if ahead:
        source = pl.ds(0, early_part)
        late_drive = edge_drive[late_rows, source]
        for row in range(rows):
            e_send[row, :, source] = late_drive[row : row + 1] * p_send[row, :, source]
            e_send[row, :, pl.ds(early_part, rows * states)] = edge_wide[row : row + 1]

        def send_edges(row, owner):
            copy_to(
                e_send.at[row], e_recv.at[me], e_send_sem, e_recv_sem.at[me // stride], owner
            ).start()

        each_owner(send_edges)

    def whole_states(target, sub):
        at = channels(sub)
        added = lax.dot_general(
            edge_spread, edge_drive[late_rows, at].astype(BF16), (((0,), (0,)), ((), ())),
            preferred_element_type=F32,
        )
        for row in range(rows):
            total = ends[pl.ds(row * states, states), at] + (
                added[row * states : (row + 1) * states]
            )
            target[row, :, at] = (total * p_send[row, :, at]).astype(BF16)

    for sub in range(ahead, subs):
        whole_states(s_send, sub)

    @pl.when(jnp.logical_not(odd))
    def _():
        to_sibling(1).start()
        for sub in range(ahead):
            whole_states(first_state, sub)
        to_sibling(2).start()

    @pl.when(odd)
    def _():
        drain(pair_s.at[:, :, rest_at], pair_recv_sem.at[1])
        for sub in range(ahead, subs):
            add_pair(sub, pair_s)

    for sub in range(ahead, subs):
        send_states(sub)

    @pl.when(me < 2)
    def _():
        carry[...] = jnp.zeros_like(carry)

    @pl.when(owns & (me < last))
    def _():
        pltpu.make_async_copy(p_send.at[mine], p_recv.at[me], p_recv_sem).start()
        if ahead:
            pltpu.make_async_copy(
                e_send.at[mine], e_recv.at[me], e_recv_sem.at[me // stride]
            ).start()

        def keep(sub):
            pltpu.make_async_copy(
                s_send.at[mine, :, channels(sub)], s_recv.at[me, :, channels(sub)],
                s_recv_sem.at[sub, me // stride],
            ).start()

        @pl.when(odd)
        def _():
            for sub in range(subs):
                keep(sub)


    @pl.loop(0, inner // chunk)
    def _(turn):
        at = pl.ds(pl.multiple_of(turn * chunk, chunk), chunk)
        place = lax.broadcasted_iota(jnp.int32, (cols, chunk), 0)
        for row in range(rows):
            here = pl.ds(row * cols, cols)
            sig = jnp.where(
                place == 0,
                fix[0, row : row + 1, at],
                jnp.where(place == cols - 1, fix[1, row : row + 1, at], signal[here, at]),
            )
            signal[here, at] = sig
            drive[here, at] = (sig * scale[here, at]).astype(BF16)

    coeffs = project(signal[...])
    in_coef, out_coef = coeffs[:, :states], coeffs[:, states:]
    in_high, out_high = in_coef.astype(BF16), out_coef.astype(BF16)
    in_low = (in_coef - in_high.astype(F32)).astype(BF16)
    out_low = (out_coef - out_high.astype(F32)).astype(BF16)
    pairing = lax.dot_general(
        jnp.concatenate([out_high, out_low, out_high], axis=1),
        jnp.concatenate([in_high, in_high, in_low], axis=1),
        (((1,), (1,)), ((), ())),
        preferred_element_type=F32,
    )
    at_row = lax.broadcasted_iota(jnp.int32, pairing.shape, 0)
    at_col = lax.broadcasted_iota(jnp.int32, pairing.shape, 1)
    pairing = jnp.where(lax.rem(at_col, cols) <= lax.rem(at_row, cols), pairing, 0.0)
    high_wide = jnp.concatenate([out_high.astype(F32)] * rows, axis=1)
    low_wide = jnp.concatenate([out_low.astype(F32)] * rows, axis=1)
    wide_col = lax.broadcasted_iota(jnp.int32, high_wide.shape, 1) // states
    begins = [0]
    for source in range(rows):
        begin, count = begins[-1], (rows - source) * cols
        begins.append(begin + count)
        here = pl.ds(begin, count)
        below = slice(source * cols, patches)
        from_drive[here, :] = jnp.where(at_col // cols == source, pairing, 0.0)[below].astype(BF16)
        placed = wide_col == source
        from_carry[here, : rows * states] = jnp.where(placed, high_wide, 0.0)[below].astype(BF16)
        from_carry[here, rows * states :] = jnp.where(placed, low_wide, 0.0)[below].astype(BF16)

    def seen_sum(seen, at):
        sums = [None] * rows
        for source in range(rows):
            reach = across[pl.ds(source * cols, cols), at]
            for row in range(source, rows):
                begin = begins[source] + (row - source) * cols
                term = reach * seen[begin : begin + cols]
                sums[row] = term if sums[row] is None else sums[row] + term
        return sums

    def nearby(turn):
        at = pl.ds(pl.multiple_of(turn * chunk, chunk), chunk)
        seen = jnp.dot(from_drive[...], drive[:, at], preferred_element_type=F32)
        sums = seen_sum(seen, at)
        for row in range(rows):
            here = pl.ds(row * cols, cols)
            near[here, at] = (
                far[here, at] * sums[row] + skip_ref[:, at] * signal[here, at] * gate[here, at]
            )

    def late_states(begin, count):
        late = e_recv[pl.ds(begin, count)].reshape(count, e_recv.shape[-1])
        wide = jnp.concatenate([late[:, early_part:]] * -(-count // rows), axis=1)
        wide = wide[:, : count * states]
        own = lax.broadcasted_iota(jnp.int32, wide.shape, 1) // states
        own = own == lax.broadcasted_iota(jnp.int32, wide.shape, 0)
        extra[pl.ds(begin * states, count * states), :] = lax.dot_general(
            jnp.where(own, wide, 0.0).astype(BF16), late[:, :early_part].astype(BF16),
            (((0,), (0,)), ((), ())), preferred_element_type=F32,
        )

    core = jnp.where(mine < half_rows, 0, 1)

    def prefixes(sub):
        at = channels(sub)

        def send_carry(even, to):
            @pl.when(to != me)
            def _():
                copy_to(
                    c_send.at[even, :, at], carry.at[mine, :, at], c_send_sem,
                    c_recv_sem.at[sub], to,
                ).start()

            @pl.when(to == me)
            def _():
                pltpu.make_async_copy(
                    c_send.at[even, :, at], carry.at[mine, :, at], c_recv_sem.at[sub]
                ).start()

        def chip(turn, state):
            left, right = 2 * turn, 2 * turn + 1
            if sub < ahead:
                for band in (left, right):
                    late = extra[pl.ds(band * states, states), at]
                    state = p_recv[band, :, at] * state + late
                state = state + s_recv[right, :, at].astype(F32)
            else:
                product = p_recv[left, :, at] * p_recv[right, :, at]
                state = product * state + s_recv[right, :, at].astype(F32)
            even = left + 2
            c_send[even, :, at] = state.astype(BF16)
            if sub in DIRECT:
                send_carry(even, even)
                send_carry(even, even + 1)
            else:
                send_carry(even, even + core)
            return state

        state = jnp.zeros((states, sizes[sub]), F32)
        for group in range(GROUPS):
            begin = min(group * stride, last)
            end = min(begin + stride, last)
            stop = min((begin + stride) // 2, n // 2 - 1)
            if begin < end:
                arrivals = stop - begin // 2
                drain(s_recv.at[pl.ds(begin, arrivals), :, at], s_recv_sem.at[sub, group])
                if sub == 0 and ahead:
                    drain(e_recv.at[pl.ds(begin, end - begin)], e_recv_sem.at[group])
                    late_states(begin, end - begin)
                state = lax.fori_loop(begin // 2, stop, chip, state, unroll=True)

    pl.loop(0, inner // chunk)(nearby)

    for sub in range(subs):

        @pl.when(owns)
        def _():
            if sub == 0:
                drain(p_recv, p_recv_sem)
            prefixes(sub)

    out_load.wait()

    def forward(sub):
        which = pl.ds(late_side * half_rows, half_rows)
        at = channels(sub)
        return copy_to(
            carry.at[which, :, at], carry.at[which, :, at], f_send_sem.at[sub],
            f_recv_sem.at[sub], sibling,
        )

    def take(sub):
        @pl.when(me > 1)
        def _():
            count = rows if sub in DIRECT else half_rows
            drain(carry.at[pl.ds(0, count), :, channels(sub)], c_recv_sem.at[sub])
            if sub not in DIRECT:
                forward(sub).start()

    def finish(sub):
        if sub not in DIRECT:

            @pl.when(me > 1)
            def _():
                forward(sub).wait()

        for turn in range(-(-sizes[sub] // chunk)):
            piece = min(chunk, sizes[sub] - turn * chunk)
            at = pl.ds(sum(sizes[:sub]) + turn * chunk, piece)
            state = carry[:, :, at]
            second = pair_p[:, :, at] * state.astype(F32) + pair_s[:, :, at].astype(F32)
            state = jnp.where(odd, second, state.astype(F32)).astype(BF16)
            state = state.reshape(rows * states, piece)
            seen = jnp.dot(
                from_carry[...], jnp.concatenate([state, state], axis=0),
                preferred_element_type=F32,
            )
            sums = seen_sum(seen, at)
            for row in range(rows):
                here = pl.ds(row * cols, cols)
                local[here, at] = (near[here, at] + far[here, at] * sums[row]).astype(BF16)
        result = None if sub == 0 else total_out[...]
        at = channels(sub)
        term = jnp.dot(local[:, at], w_out_ref[at, :], preferred_element_type=F32)
        result = term if result is None else result + term
        if sub == subs - 1:
            out_ref[...] = result.astype(BF16)
        else:
            total_out[...] = result

    @pl.when(odd)
    def _():
        drain(pair_p, pair_recv_sem.at[0])
        drain(pair_s.at[:, :, early_at], pair_recv_sem.at[2])

    for sub in range(subs):
        take(sub)
        if sub > 0:
            finish(sub - 1)
    finish(subs - 1)

    @pl.when(jnp.logical_not(odd))
    def _():
        for k in range(4):
            to_sibling(k).wait_send()

    def sent(count):
        drain(p_recv.at[pl.ds(0, count)], p_send_sem)
        if ahead:
            drain(e_recv.at[pl.ds(0, count)], e_send_sem)

        @pl.when(odd)
        def _():
            drain(c_send.at[pl.ds(0, count)], s_send_sem)

    @pl.when(owns)
    def _():
        for sub in range(subs):
            at = channels(sub)
            if sub in DIRECT:
                own_target, least = me > 1, n - 3
            else:
                own_target, least = (me > 1) & (core == late_side), n // 2 - 2
            drain(c_send.at[pl.ds(0, least), :, at], c_send_sem)

            @pl.when(jnp.logical_not(own_target))
            def _():
                drain(c_send.at[0, :, at], c_send_sem)

        @pl.when(me < last)
        def _():
            sent(rows - 1)

    @pl.when(jnp.logical_not(owns) & (me < last))
    def _():
        sent(rows)


def on_device(n, patches, norm_gain, w_in, conv_w, w_bc, skip, w_out, decay_h, decay_v):
    rows, cols, depth = patches.shape
    inner = w_out.shape[0]
    states = w_bc.shape[1] // 2
    sizes = cut(inner)
    subs = len(sizes)
    ahead = AHEAD
    early_part = sum(sizes[:ahead])
    count = rows * cols
    vmem = pl.BlockSpec(memory_space=pltpu.VMEM)
    dma = pltpu.SemaphoreType.DMA
    out = pl.pallas_call(
        functools.partial(kernel, n, ahead, rows, cols, states),
        out_shape=jax.ShapeDtypeStruct((count, w_out.shape[1]), BF16),
        in_specs=[pl.BlockSpec(memory_space=pltpu.HBM)] * 9,
        out_specs=vmem,
        scratch_shapes=[
            pltpu.VMEM((count, depth), BF16),
            pltpu.VMEM((1, depth), F32),
            pltpu.VMEM(w_in.shape, BF16),
            pltpu.VMEM(conv_w.shape, F32),
            pltpu.VMEM((2 * states, inner), BF16),
            pltpu.VMEM((1, inner), F32),
            pltpu.VMEM(w_out.shape, BF16),
            pltpu.VMEM((count, inner), F32),
            pltpu.VMEM((count, inner), F32),
            pltpu.VMEM((2, rows, inner), BF16),
            pltpu.VMEM((2, rows, inner), BF16),
            pltpu.VMEM((2, rows, inner), F32),
            pltpu.VMEM((2 * rows, inner), F32),
            pltpu.VMEM((2 * rows, inner), F32),
            pltpu.VMEM((2 * rows, inner), F32),
            pltpu.VMEM((count + 2 * cols, inner), F32),
            pltpu.VMEM((count, inner), F32),
            pltpu.VMEM((count, inner), F32),
            pltpu.VMEM((count, inner), F32),
            pltpu.VMEM((count, inner), BF16),
            pltpu.VMEM((rows * states, inner), F32),
            pltpu.VMEM((count, inner), F32),
            pltpu.VMEM((count, inner), F32),
            pltpu.VMEM((count, inner), BF16),
            pltpu.VMEM((count, inner), F32),
            pltpu.VMEM((count, inner), F32),
            pltpu.VMEM((count * (rows + 1) // 2, count), BF16),
            pltpu.VMEM((count * (rows + 1) // 2, 2 * rows * states), BF16),
            pltpu.VMEM((rows, states, inner), BF16),
            pltpu.VMEM((rows, 1, inner), F32),
            pltpu.VMEM((n - 1, states, inner), BF16),
            pltpu.VMEM((n - 1, 1, inner), F32),
            pltpu.VMEM((n, states, inner), BF16),
            pltpu.VMEM((rows, states, inner), BF16),
            pltpu.VMEM((rows, 1, early_part + rows * states), F32),
            pltpu.VMEM((n - 1, 1, early_part + rows * states), F32),
            pltpu.VMEM((-(-(n - 1) // rows) * rows * states, early_part), F32),
            pltpu.VMEM((rows, states, inner), BF16),
            pltpu.VMEM((count, w_out.shape[1]), F32),
            pltpu.VMEM((rows, states, inner), BF16),
            pltpu.VMEM((rows, 1, inner), F32),
            pltpu.VMEM((rows, states, early_part), BF16),
            dma((10,)), dma((2,)), dma((2,)), dma, dma((subs, GROUPS)), dma, dma, dma, dma((subs,)), dma,
            dma((4,)), dma, dma((GROUPS,)), dma((subs,)), dma((subs,)),
        ],
        compiler_params=pltpu.CompilerParams(
            collective_id=0, has_side_effects=True, vmem_limit_bytes=40 << 20
        ),
    )(*[
        pltpu.with_memory_space_constraint(a, pltpu.HBM)
        for a in (
            patches.reshape(count, depth),
            norm_gain.reshape(1, depth),
            w_in,
            conv_w,
            w_bc.T,
            skip.reshape(1, inner),
            w_out,
            decay_h.reshape(count, inner),
            decay_v.reshape(count, inner),
        )
    ])
    return out.reshape(rows, cols, w_out.shape[1])


def solution(mesh):
    n = mesh.shape["cols"]
    banded = P("slides", "cols", None)
    return jax.shard_map(
        functools.partial(on_device, n),
        mesh=mesh,
        in_specs=(banded, P(), P(), P(), P(), P(), P(), banded, banded),
        out_specs=banded,
        check_vma=False,
    )
```

```python
import functools

import jax
import jax.numpy as jnp
from jax import lax
from jax.experimental import pallas as pl
from jax.experimental.pallas import tpu as pltpu
from jax.sharding import PartitionSpec as P

F32 = jnp.float32
BF16 = jnp.bfloat16
LANES = 128
SHARES = (3, 3, 2)
DIRECT = (2,)
AHEAD = 1
GROUPS = 4


def cut(inner):
    return [share * inner // 8 for share in SHARES]


def copy_to(src, dst, send_sem, recv_sem, target):
    return pltpu.make_async_remote_copy(
        src_ref=src,
        dst_ref=dst,
        send_sem=send_sem,
        recv_sem=recv_sem,
        device_id={"cols": target},
        device_id_type=pl.DeviceIdType.MESH,
    )


def drain(ref, sem):
    pltpu.make_async_copy(ref, ref, sem).wait()


def kernel(
    n, ahead, rows, cols, states,
    x_hbm, gain_hbm, w_in_hbm, conv_hbm, w_bc_hbm, skip_hbm, w_out_hbm, dh_hbm, dv_hbm,
    out_ref,
    x_ref, gain_ref, w_in_ref, conv_ref, w_bc_ref, skip_ref, w_out_ref, dh_ref, dv_ref,
    edge_out, edge_in, fix, edge_conv, edge_scale, edge_drive,
    grid, prefix, scale, signal, drive, ends, gate, across, local, far, near, from_drive, from_carry,
    s_send, p_send, s_recv, p_recv, c_send, carry, e_send, e_recv, extra, first_state, total_out,
    pair_s, pair_p, pair_early, w_wide,
    load_sem, edge_send_sem, edge_recv_sem, s_send_sem, s_recv_sem, p_send_sem, p_recv_sem,
    c_send_sem, c_recv_sem, pair_send_sem, pair_recv_sem, e_send_sem, e_recv_sem,
    f_send_sem, f_recv_sem,
):
    me = lax.axis_index("cols")
    inner = w_out_ref.shape[0]
    sizes = cut(inner)
    subs = len(sizes)
    early_part = sum(sizes[:ahead])
    patches = rows * cols
    last = n - 1
    stride = -(-n // GROUPS)
    first = (n - rows) // 2
    mine = me - first
    owns = (me >= first) & (me < first + rows)

    late_side = lax.rem(me, 2)
    odd = late_side == 1
    sibling = me + 1 - 2 * late_side
    half_rows = rows // 2
    early_at, rest_at = pl.ds(0, early_part), pl.ds(early_part, inner - early_part)

    def each_owner(start_copy, sends=True):
        half = rows // 2
        far_half = jnp.where(me < n // 2, 1, 0)

        @pl.when((me < last) & sends)
        def _():
            @pl.loop(0, rows)
            def _(step):
                side = lax.rem(step // half + far_half, 2)
                row = side * half + lax.rem(step + me, half)

                @pl.when(first + row != me)
                def _():
                    start_copy(row, first + row)


    pairs = (
        (x_hbm, x_ref), (gain_hbm, gain_ref), (dh_hbm, dh_ref),
        (w_in_hbm.at[:, pl.ds(0, inner)], w_in_ref.at[:, pl.ds(0, inner)]),
        (conv_hbm, conv_ref),
        (w_in_hbm.at[:, pl.ds(inner, inner)], w_in_ref.at[:, pl.ds(inner, inner)]),
        (w_bc_hbm, w_bc_ref), (dv_hbm, dv_ref), (skip_hbm, skip_ref), (w_out_hbm, w_out_ref),
    )
    loads = [
        pltpu.make_async_copy(src, dst, load_sem.at[k]) for k, (src, dst) in enumerate(pairs)
    ]
    (
        x_load, gain_load, dh_load, branch_load, conv_load, gate_load, bc_load, dv_load,
        skip_load, out_load,
    ) = loads

    early = (x_load, gain_load, dh_load, branch_load, conv_load, bc_load)
    for load in early:
        load.start()

    barrier = pltpu.get_barrier_semaphore()

    def owner_at(band):
        return (band >= first) & (band < first + rows)

    @pl.loop(1, n)
    def _(turn):
        other = lax.rem(me + turn, n)

        @pl.when(owns | owner_at(other) | (other == me - 1) | (other == me + 1))
        def _():
            pl.semaphore_signal(
                barrier, inc=1, device_id={"cols": other}, device_id_type=pl.DeviceIdType.MESH
            )

    one_left = jnp.where((me > 0) & jnp.logical_not(owner_at(me - 1)), 1, 0)
    one_right = jnp.where((me < last) & jnp.logical_not(owner_at(me + 1)), 1, 0)
    partners = jnp.where(owns, n - 1, rows + one_left + one_right)

    chunk = 2 * LANES
    dh_load.wait()

    @pl.loop(0, inner // chunk)
    def _(turn):
        at = pl.ds(pl.multiple_of(turn * chunk, chunk), chunk)
        place = lax.broadcasted_iota(jnp.int32, (cols, chunk), 0)
        for row in range(rows):
            here = pl.ds(row * cols, cols)
            decay = dh_ref[here, at]
            product = decay
            step = 1
            while step < cols:
                product = product * jnp.where(place >= step, pltpu.roll(product, step, 0), 1.0)
                step *= 2
            prefix[here, at] = product
            p_send[row, :, at] = product[cols - 1 : cols]
            rest = 1.0 - decay * decay
            value = rest * lax.rsqrt(rest * (product * product))
            scale[here, at] = value
            edge_scale[pl.ds(row, 1), at] = value[0:1]
            edge_scale[pl.ds(rows + row, 1), at] = value[cols - 1 : cols]

    x_load.wait()
    gain_load.wait()
    feats = x_ref[...].astype(F32)
    meansq = jnp.mean(feats * feats, axis=-1, keepdims=True)
    normed = (feats * lax.rsqrt(meansq + 1e-05) * gain_ref[...]).astype(BF16)
    x_ref[...] = normed
    branch_load.wait()
    for load in (gate_load, dv_load, skip_load, out_load):
        load.start()
    branch = jnp.dot(normed, w_in_ref[:, :inner], preferred_element_type=F32)
    branch = branch.astype(BF16).astype(F32)
    grid[pl.ds(0, cols), :] = jnp.zeros((cols, inner), F32)
    grid[pl.ds((rows + 1) * cols, cols), :] = jnp.zeros((cols, inner), F32)
    grid[pl.ds(cols, patches), :] = branch
    for row in range(rows):
        for side, place in ((0, row * cols), (1, (row + 1) * cols - 1)):
            fix[side, row : row + 1, :] = branch[place : place + 1]
    for side in range(2):
        edge_out[side] = fix[side].astype(BF16)

    bc_load.wait()
    for row in range(rows):
        w_wide[pl.ds(row * states, states), :] = w_bc_ref[pl.ds(0, states), :]

    pl.semaphore_wait(barrier, partners)

    to_right = copy_to(
        edge_out.at[1], edge_in.at[0], edge_send_sem.at[0], edge_recv_sem.at[0],
        lax.rem(me + 1, n),
    )
    to_left = copy_to(
        edge_out.at[0], edge_in.at[1], edge_send_sem.at[1], edge_recv_sem.at[1],
        lax.rem(me + n - 1, n),
    )

    @pl.when(me < last)
    def _():
        to_right.start()

    @pl.when(me > 0)
    def _():
        to_left.start()

    def send_product(row, owner):
        copy_to(p_send.at[row], p_recv.at[me], p_send_sem, p_recv_sem, owner).start()

    each_owner(send_product)

    def to_sibling(k):
        source, target = (
            (p_send, pair_p),
            (s_send.at[:, :, rest_at], pair_s.at[:, :, rest_at]),
            (first_state.at[:, :, early_at], pair_s.at[:, :, early_at]),
            (s_send.at[:, :, early_at], pair_early),
        )[k]
        return copy_to(source, target, pair_send_sem, pair_recv_sem.at[k], sibling)

    @pl.when(jnp.logical_not(odd))
    def _():
        to_sibling(0).start()

    conv_load.wait()

    @pl.loop(0, inner // chunk)
    def _(turn):
        at = pl.ds(pl.multiple_of(turn * chunk, chunk), chunk)
        taps = [[conv_ref[a, pl.ds(b, 1), at] for b in range(3)] for a in range(3)]
        place = lax.broadcasted_iota(jnp.int32, (cols, chunk), 0)
        for row in range(rows):
            here = pl.ds(row * cols, cols)
            lines = [grid[pl.ds((row + a) * cols, cols), at] for a in range(3)]
            parts = [
                taps[0][b] * lines[0] + taps[1][b] * lines[1] + taps[2][b] * lines[2]
                for b in range(3)
            ]
            conv = (
                jnp.where(place > 0, pltpu.roll(parts[0], 1, 0), 0.0)
                + parts[1]
                + jnp.where(place < cols - 1, pltpu.roll(parts[2], cols - 1, 0), 0.0)
            )
            edge_conv[pl.ds(row, 1), at] = conv[0:1]
            edge_conv[pl.ds(rows + row, 1), at] = conv[cols - 1 : cols]
            sig = conv * jax.nn.sigmoid(conv)
            signal[here, at] = sig
            inside = (place > 0) & (place < cols - 1)
            drive[here, at] = jnp.where(inside, sig * scale[here, at], 0.0).astype(BF16)

    def project(values):
        return lax.dot_general(
            values.astype(BF16), w_bc_ref[...], (((1,), (1,)), ((), ())),
            preferred_element_type=F32,
        )

    def spread_states(values):
        return lax.dot_general(
            values.astype(BF16), w_wide[...], (((1,), (1,)), ((), ())),
            preferred_element_type=F32,
        )

    def place_states(wide, row_of):
        src = row_of(lax.broadcasted_iota(jnp.int32, wide.shape, 0))
        dst = lax.broadcasted_iota(jnp.int32, wide.shape, 1) // states
        return jnp.where(src == dst, wide, 0.0).astype(BF16)

    line = lax.broadcasted_iota(jnp.int32, (rows, inner), 0)

    def edge(side):
        present = ((side == 0) & (me > 0)) | ((side == 1) & (me < last))

        @pl.when(present)
        def _():
            drain(edge_in.at[side], edge_recv_sem.at[side])

        value = jnp.where(present, edge_in[side].astype(F32), 0.0)
        above = jnp.where(line > 0, pltpu.roll(value, 1, 0), 0.0)
        below = jnp.where(line < rows - 1, pltpu.roll(value, rows - 1, 0), 0.0)
        which = pl.ds(pl.multiple_of(side * rows, rows), rows)
        tap = pl.ds(2 * side, 1)
        conv = edge_conv[which, :] + (
            conv_ref[0, tap, :] * above
            + conv_ref[1, tap, :] * value
            + conv_ref[2, tap, :] * below
        )
        sig = conv * jax.nn.sigmoid(conv)
        fix[side] = sig
        edge_drive[which, :] = sig * edge_scale[which, :]
        return spread_states(sig), which

    inner_spread = place_states(spread_states(signal[...]), lambda p: p // cols)
    inner_ends = lax.dot_general(
        inner_spread, drive[...], (((0,), (0,)), ((), ())), preferred_element_type=F32
    )
    soon_coefs, soon_rows = edge(1 - late_side)
    ends[...] = inner_ends + lax.dot_general(
        place_states(soon_coefs, lambda p: p), edge_drive[soon_rows, :].astype(BF16),
        (((0,), (0,)), ((), ())), preferred_element_type=F32,
    )

    def channels(sub):
        return pl.ds(sum(sizes[:sub]), sizes[sub])

    def send_states(sub):
        def send_state(row, owner):
            copy_to(
                s_send.at[row, :, channels(sub)], s_recv.at[me, :, channels(sub)], s_send_sem,
                s_recv_sem.at[sub, me // stride], owner,
            ).start()

        each_owner(send_state, odd)

    for sub in range(ahead):
        at = channels(sub)
        for row in range(rows):
            total = ends[pl.ds(row * states, states), at]
            s_send[row, :, at] = (total * p_send[row, :, at]).astype(BF16)

    def add_pair(sub, source):
        at = channels(sub)
        for row in range(rows):
            s_send[row, :, at] = (
                p_send[row, :, at] * source[row, :, at].astype(F32)
                + s_send[row, :, at].astype(F32)
            ).astype(BF16)

    @pl.when(jnp.logical_not(odd))
    def _():
        to_sibling(3).start()

    dv_load.wait()
    gate_load.wait()
    skip_load.wait()

    @pl.loop(0, inner // chunk)
    def _(turn):
        at = pl.ds(pl.multiple_of(turn * chunk, chunk), chunk)
        half_at = pl.ds(pl.multiple_of(inner + turn * chunk, chunk), chunk)
        half = jnp.dot(x_ref[...], w_in_ref[:, half_at], preferred_element_type=F32)
        half = half.astype(BF16).astype(F32)
        gate[:, at] = half * jax.nn.sigmoid(half)
        down = None
        for row in range(rows):
            here = pl.ds(row * cols, cols)
            decay = dv_ref[here, at]
            down = decay if down is None else down * decay
            rest = 1.0 - decay * decay
            across[here, at] = prefix[here, at] * (rest * lax.rsqrt(rest * (down * down)))
            far[here, at] = down * gate[here, at]

    @pl.when(odd)
    def _():
        drain(pair_early, pair_recv_sem.at[3])
        for sub in range(ahead):
            add_pair(sub, pair_early)

    for sub in range(ahead):
        send_states(sub)


    late_coefs, late_rows = edge(late_side)
    edge_spread = place_states(late_coefs, lambda p: p)
    edge_wide = late_coefs

    @pl.when(me < last)
    def _():
        to_right.wait_send()

    @pl.when(me > 0)
    def _():
        to_left.wait_send()

    if ahead:
        source = pl.ds(0, early_part)
        late_drive = edge_drive[late_rows, source]
        for row in range(rows):
            e_send[row, :, source] = late_drive[row : row + 1] * p_send[row, :, source]
            e_send[row, :, pl.ds(early_part, rows * states)] = edge_wide[row : row + 1]

        def send_edges(row, owner):
            copy_to(
                e_send.at[row], e_recv.at[me], e_send_sem, e_recv_sem.at[me // stride], owner
            ).start()

        each_owner(send_edges)

    def whole_states(target, sub):
        at = channels(sub)
        added = lax.dot_general(
            edge_spread, edge_drive[late_rows, at].astype(BF16), (((0,), (0,)), ((), ())),
            preferred_element_type=F32,
        )
        for row in range(rows):
            total = ends[pl.ds(row * states, states), at] + (
                added[row * states : (row + 1) * states]
            )
            target[row, :, at] = (total * p_send[row, :, at]).astype(BF16)

    for sub in range(ahead, subs):
        whole_states(s_send, sub)

    @pl.when(jnp.logical_not(odd))
    def _():
        to_sibling(1).start()
        for sub in range(ahead):
            whole_states(first_state, sub)
        to_sibling(2).start()

    @pl.when(odd)
    def _():
        drain(pair_s.at[:, :, rest_at], pair_recv_sem.at[1])
        for sub in range(ahead, subs):
            add_pair(sub, pair_s)

    for sub in range(ahead, subs):
        send_states(sub)

    @pl.when(me < 2)
    def _():
        carry[...] = jnp.zeros_like(carry)

    @pl.when(owns & (me < last))
    def _():
        pltpu.make_async_copy(p_send.at[mine], p_recv.at[me], p_recv_sem).start()
        if ahead:
            pltpu.make_async_copy(
                e_send.at[mine], e_recv.at[me], e_recv_sem.at[me // stride]
            ).start()

        def keep(sub):
            pltpu.make_async_copy(
                s_send.at[mine, :, channels(sub)], s_recv.at[me, :, channels(sub)],
                s_recv_sem.at[sub, me // stride],
            ).start()

        @pl.when(odd)
        def _():
            for sub in range(subs):
                keep(sub)


    @pl.loop(0, inner // chunk)
    def _(turn):
        at = pl.ds(pl.multiple_of(turn * chunk, chunk), chunk)
        place = lax.broadcasted_iota(jnp.int32, (cols, chunk), 0)
        for row in range(rows):
            here = pl.ds(row * cols, cols)
            sig = jnp.where(
                place == 0,
                fix[0, row : row + 1, at],
                jnp.where(place == cols - 1, fix[1, row : row + 1, at], signal[here, at]),
            )
            signal[here, at] = sig
            drive[here, at] = (sig * scale[here, at]).astype(BF16)

    coeffs = project(signal[...])
    in_coef, out_coef = coeffs[:, :states], coeffs[:, states:]
    in_high, out_high = in_coef.astype(BF16), out_coef.astype(BF16)
    in_low = (in_coef - in_high.astype(F32)).astype(BF16)
    out_low = (out_coef - out_high.astype(F32)).astype(BF16)
    pairing = lax.dot_general(
        jnp.concatenate([out_high, out_low, out_high], axis=1),
        jnp.concatenate([in_high, in_high, in_low], axis=1),
        (((1,), (1,)), ((), ())),
        preferred_element_type=F32,
    )
    at_row = lax.broadcasted_iota(jnp.int32, pairing.shape, 0)
    at_col = lax.broadcasted_iota(jnp.int32, pairing.shape, 1)
    pairing = jnp.where(lax.rem(at_col, cols) <= lax.rem(at_row, cols), pairing, 0.0)
    high_wide = jnp.concatenate([out_high.astype(F32)] * rows, axis=1)
    low_wide = jnp.concatenate([out_low.astype(F32)] * rows, axis=1)
    wide_col = lax.broadcasted_iota(jnp.int32, high_wide.shape, 1) // states
    begins = [0]
    for source in range(rows):
        begin, count = begins[-1], (rows - source) * cols
        begins.append(begin + count)
        here = pl.ds(begin, count)
        below = slice(source * cols, patches)
        from_drive[here, :] = jnp.where(at_col // cols == source, pairing, 0.0)[below].astype(BF16)
        placed = wide_col == source
        from_carry[here, : rows * states] = jnp.where(placed, high_wide, 0.0)[below].astype(BF16)
        from_carry[here, rows * states :] = jnp.where(placed, low_wide, 0.0)[below].astype(BF16)

    def seen_sum(seen, at):
        sums = [None] * rows
        for source in range(rows):
            reach = across[pl.ds(source * cols, cols), at]
            for row in range(source, rows):
                begin = begins[source] + (row - source) * cols
                term = reach * seen[begin : begin + cols]
                sums[row] = term if sums[row] is None else sums[row] + term
        return sums

    def nearby(turn):
        at = pl.ds(pl.multiple_of(turn * chunk, chunk), chunk)
        seen = jnp.dot(from_drive[...], drive[:, at], preferred_element_type=F32)
        sums = seen_sum(seen, at)
        for row in range(rows):
            here = pl.ds(row * cols, cols)
            near[here, at] = (
                far[here, at] * sums[row] + skip_ref[:, at] * signal[here, at] * gate[here, at]
            )

    def late_states(begin, count):
        late = e_recv[pl.ds(begin, count)].reshape(count, e_recv.shape[-1])
        wide = jnp.concatenate([late[:, early_part:]] * -(-count // rows), axis=1)
        wide = wide[:, : count * states]
        own = lax.broadcasted_iota(jnp.int32, wide.shape, 1) // states
        own = own == lax.broadcasted_iota(jnp.int32, wide.shape, 0)
        extra[pl.ds(begin * states, count * states), :] = lax.dot_general(
            jnp.where(own, wide, 0.0).astype(BF16), late[:, :early_part].astype(BF16),
            (((0,), (0,)), ((), ())), preferred_element_type=F32,
        )

    core = jnp.where(mine < half_rows, 0, 1)

    def prefixes(sub):
        at = channels(sub)

        def send_carry(even, to):
            @pl.when(to != me)
            def _():
                copy_to(
                    c_send.at[even, :, at], carry.at[mine, :, at], c_send_sem,
                    c_recv_sem.at[sub], to,
                ).start()

            @pl.when(to == me)
            def _():
                pltpu.make_async_copy(
                    c_send.at[even, :, at], carry.at[mine, :, at], c_recv_sem.at[sub]
                ).start()

        def chip(turn, state):
            left, right = 2 * turn, 2 * turn + 1
            if sub < ahead:
                for band in (left, right):
                    late = extra[pl.ds(band * states, states), at]
                    state = p_recv[band, :, at] * state + late
                state = state + s_recv[right, :, at].astype(F32)
            else:
                product = p_recv[left, :, at] * p_recv[right, :, at]
                state = product * state + s_recv[right, :, at].astype(F32)
            even = left + 2
            c_send[even, :, at] = state.astype(BF16)
            if sub in DIRECT:
                send_carry(even, even)
                send_carry(even, even + 1)
            else:
                send_carry(even, even + core)
            return state

        state = jnp.zeros((states, sizes[sub]), F32)
        for group in range(GROUPS):
            begin = min(group * stride, last)
            end = min(begin + stride, last)
            stop = min((begin + stride) // 2, n // 2 - 1)
            if begin < end:
                arrivals = stop - begin // 2
                drain(s_recv.at[pl.ds(begin, arrivals), :, at], s_recv_sem.at[sub, group])
                if sub == 0 and ahead:
                    drain(e_recv.at[pl.ds(begin, end - begin)], e_recv_sem.at[group])
                    late_states(begin, end - begin)
                state = lax.fori_loop(begin // 2, stop, chip, state, unroll=True)

    pl.loop(0, inner // chunk)(nearby)

    for sub in range(subs):

        @pl.when(owns)
        def _():
            if sub == 0:
                drain(p_recv, p_recv_sem)
            prefixes(sub)

    out_load.wait()

    def forward(sub):
        which = pl.ds(late_side * half_rows, half_rows)
        at = channels(sub)
        return copy_to(
            carry.at[which, :, at], carry.at[which, :, at], f_send_sem.at[sub],
            f_recv_sem.at[sub], sibling,
        )

    def take(sub):
        @pl.when(me > 1)
        def _():
            count = rows if sub in DIRECT else half_rows
            drain(carry.at[pl.ds(0, count), :, channels(sub)], c_recv_sem.at[sub])
            if sub not in DIRECT:
                forward(sub).start()

    def finish(sub):
        if sub not in DIRECT:

            @pl.when(me > 1)
            def _():
                forward(sub).wait()

        for turn in range(-(-sizes[sub] // chunk)):
            piece = min(chunk, sizes[sub] - turn * chunk)
            at = pl.ds(sum(sizes[:sub]) + turn * chunk, piece)
            state = carry[:, :, at]
            second = pair_p[:, :, at] * state.astype(F32) + pair_s[:, :, at].astype(F32)
            state = jnp.where(odd, second, state.astype(F32)).astype(BF16)
            state = state.reshape(rows * states, piece)
            seen = jnp.dot(
                from_carry[...], jnp.concatenate([state, state], axis=0),
                preferred_element_type=F32,
            )
            sums = seen_sum(seen, at)
            for row in range(rows):
                here = pl.ds(row * cols, cols)
                local[here, at] = (near[here, at] + far[here, at] * sums[row]).astype(BF16)
        result = None if sub == 0 else total_out[...]
        at = channels(sub)
        term = jnp.dot(local[:, at], w_out_ref[at, :], preferred_element_type=F32)
        result = term if result is None else result + term
        if sub == subs - 1:
            out_ref[...] = result.astype(BF16)
        else:
            total_out[...] = result

    @pl.when(odd)
    def _():
        drain(pair_p, pair_recv_sem.at[0])
        drain(pair_s.at[:, :, early_at], pair_recv_sem.at[2])

    for sub in range(subs):
        take(sub)
        if sub > 0:
            finish(sub - 1)
    finish(subs - 1)

    @pl.when(jnp.logical_not(odd))
    def _():
        for k in range(4):
            to_sibling(k).wait_send()

    def sent(count):
        drain(p_recv.at[pl.ds(0, count)], p_send_sem)
        if ahead:
            drain(e_recv.at[pl.ds(0, count)], e_send_sem)

        @pl.when(odd)
        def _():
            drain(c_send.at[pl.ds(0, count)], s_send_sem)

    @pl.when(owns)
    def _():
        for sub in range(subs):
            at = channels(sub)
            if sub in DIRECT:
                own_target, least = me > 1, n - 3
            else:
                own_target, least = (me > 1) & (core == late_side), n // 2 - 2
            drain(c_send.at[pl.ds(0, least), :, at], c_send_sem)

            @pl.when(jnp.logical_not(own_target))
            def _():
                drain(c_send.at[0, :, at], c_send_sem)

        @pl.when(me < last)
        def _():
            sent(rows - 1)

    @pl.when(jnp.logical_not(owns) & (me < last))
    def _():
        sent(rows)


def on_device(n, patches, norm_gain, w_in, conv_w, w_bc, skip, w_out, decay_h, decay_v):
    rows, cols, depth = patches.shape
    inner = w_out.shape[0]
    states = w_bc.shape[1] // 2
    sizes = cut(inner)
    subs = len(sizes)
    ahead = AHEAD
    early_part = sum(sizes[:ahead])
    count = rows * cols
    vmem = pl.BlockSpec(memory_space=pltpu.VMEM)
    dma = pltpu.SemaphoreType.DMA
    out = pl.pallas_call(
        functools.partial(kernel, n, ahead, rows, cols, states),
        out_shape=jax.ShapeDtypeStruct((count, w_out.shape[1]), BF16),
        in_specs=[pl.BlockSpec(memory_space=pltpu.HBM)] * 9,
        out_specs=vmem,
        scratch_shapes=[
            pltpu.VMEM((count, depth), BF16),
            pltpu.VMEM((1, depth), F32),
            pltpu.VMEM(w_in.shape, BF16),
            pltpu.VMEM(conv_w.shape, F32),
            pltpu.VMEM((2 * states, inner), BF16),
            pltpu.VMEM((1, inner), F32),
            pltpu.VMEM(w_out.shape, BF16),
            pltpu.VMEM((count, inner), F32),
            pltpu.VMEM((count, inner), F32),
            pltpu.VMEM((2, rows, inner), BF16),
            pltpu.VMEM((2, rows, inner), BF16),
            pltpu.VMEM((2, rows, inner), F32),
            pltpu.VMEM((2 * rows, inner), F32),
            pltpu.VMEM((2 * rows, inner), F32),
            pltpu.VMEM((2 * rows, inner), F32),
            pltpu.VMEM((count + 2 * cols, inner), F32),
            pltpu.VMEM((count, inner), F32),
            pltpu.VMEM((count, inner), F32),
            pltpu.VMEM((count, inner), F32),
            pltpu.VMEM((count, inner), BF16),
            pltpu.VMEM((rows * states, inner), F32),
            pltpu.VMEM((count, inner), F32),
            pltpu.VMEM((count, inner), F32),
            pltpu.VMEM((count, inner), BF16),
            pltpu.VMEM((count, inner), F32),
            pltpu.VMEM((count, inner), F32),
            pltpu.VMEM((count * (rows + 1) // 2, count), BF16),
            pltpu.VMEM((count * (rows + 1) // 2, 2 * rows * states), BF16),
            pltpu.VMEM((rows, states, inner), BF16),
            pltpu.VMEM((rows, 1, inner), F32),
            pltpu.VMEM((n - 1, states, inner), BF16),
            pltpu.VMEM((n - 1, 1, inner), F32),
            pltpu.VMEM((n, states, inner), BF16),
            pltpu.VMEM((rows, states, inner), BF16),
            pltpu.VMEM((rows, 1, early_part + rows * states), F32),
            pltpu.VMEM((n - 1, 1, early_part + rows * states), F32),
            pltpu.VMEM((-(-(n - 1) // rows) * rows * states, early_part), F32),
            pltpu.VMEM((rows, states, inner), BF16),
            pltpu.VMEM((count, w_out.shape[1]), F32),
            pltpu.VMEM((rows, states, inner), BF16),
            pltpu.VMEM((rows, 1, inner), F32),
            pltpu.VMEM((rows, states, early_part), BF16),
            pltpu.VMEM((rows * states, inner), BF16),
            dma((10,)), dma((2,)), dma((2,)), dma, dma((subs, GROUPS)), dma, dma, dma, dma((subs,)), dma,
            dma((4,)), dma, dma((GROUPS,)), dma((subs,)), dma((subs,)),
        ],
        compiler_params=pltpu.CompilerParams(
            collective_id=0, has_side_effects=True, vmem_limit_bytes=40 << 20
        ),
    )(*[
        pltpu.with_memory_space_constraint(a, pltpu.HBM)
        for a in (
            patches.reshape(count, depth),
            norm_gain.reshape(1, depth),
            w_in,
            conv_w,
            w_bc.T,
            skip.reshape(1, inner),
            w_out,
            decay_h.reshape(count, inner),
            decay_v.reshape(count, inner),
        )
    ])
    return out.reshape(rows, cols, w_out.shape[1])


def solution(mesh):
    n = mesh.shape["cols"]
    banded = P("slides", "cols", None)
    return jax.shard_map(
        functools.partial(on_device, n),
        mesh=mesh,
        in_specs=(banded, P(), P(), P(), P(), P(), P(), banded, banded),
        out_specs=banded,
        check_vma=False,
    )
```

```python
import functools

import jax
import jax.numpy as jnp
from jax import lax
from jax.experimental import pallas as pl
from jax.experimental.pallas import tpu as pltpu
from jax.sharding import PartitionSpec as P

F32 = jnp.float32
BF16 = jnp.bfloat16
LANES = 128
SHARES = (3, 3, 2)
DIRECT = (2,)
AHEAD = 1
GROUPS = 2


def cut(inner):
    return [share * inner // 8 for share in SHARES]


def copy_to(src, dst, send_sem, recv_sem, target):
    return pltpu.make_async_remote_copy(
        src_ref=src,
        dst_ref=dst,
        send_sem=send_sem,
        recv_sem=recv_sem,
        device_id={"cols": target},
        device_id_type=pl.DeviceIdType.MESH,
    )


def drain(ref, sem):
    pltpu.make_async_copy(ref, ref, sem).wait()


def kernel(
    n, ahead, rows, cols, states,
    x_hbm, gain_hbm, w_in_hbm, conv_hbm, w_bc_hbm, skip_hbm, w_out_hbm, dh_hbm, dv_hbm,
    out_ref,
    x_ref, gain_ref, w_in_ref, conv_ref, w_bc_ref, skip_ref, w_out_ref, dh_ref, dv_ref,
    edge_out, edge_in, fix, edge_conv, edge_scale, edge_drive,
    grid, prefix, scale, signal, drive, ends, gate, across, local, far, near, from_drive, from_carry,
    s_send, p_send, s_recv, p_recv, c_send, carry, e_send, e_recv, extra, first_state, total_out,
    pair_s, pair_p, pair_early, w_wide,
    load_sem, edge_send_sem, edge_recv_sem, s_send_sem, s_recv_sem, p_send_sem, p_recv_sem,
    c_send_sem, c_recv_sem, pair_send_sem, pair_recv_sem, e_send_sem, e_recv_sem,
    f_send_sem, f_recv_sem,
):
    me = lax.axis_index("cols")
    inner = w_out_ref.shape[0]
    sizes = cut(inner)
    subs = len(sizes)
    early_part = sum(sizes[:ahead])
    patches = rows * cols
    last = n - 1
    stride = -(-n // GROUPS)
    first = (n - rows) // 2
    mine = me - first
    owns = (me >= first) & (me < first + rows)

    late_side = lax.rem(me, 2)
    odd = late_side == 1
    sibling = me + 1 - 2 * late_side
    half_rows = rows // 2
    early_at, rest_at = pl.ds(0, early_part), pl.ds(early_part, inner - early_part)

    def each_owner(start_copy, sends=True):
        half = rows // 2
        far_half = jnp.where(me < n // 2, 1, 0)

        @pl.when((me < last) & sends)
        def _():
            @pl.loop(0, rows, unroll=True)
            def _(step):
                side = lax.rem(step // half + far_half, 2)
                row = side * half + lax.rem(step + me, half)

                @pl.when(first + row != me)
                def _():
                    start_copy(row, first + row)


    pairs = (
        (x_hbm, x_ref), (gain_hbm, gain_ref), (dh_hbm, dh_ref),
        (w_in_hbm.at[:, pl.ds(0, inner)], w_in_ref.at[:, pl.ds(0, inner)]),
        (conv_hbm, conv_ref),
        (w_in_hbm.at[:, pl.ds(inner, inner)], w_in_ref.at[:, pl.ds(inner, inner)]),
        (w_bc_hbm, w_bc_ref), (dv_hbm, dv_ref), (skip_hbm, skip_ref), (w_out_hbm, w_out_ref),
    )
    loads = [
        pltpu.make_async_copy(src, dst, load_sem.at[k]) for k, (src, dst) in enumerate(pairs)
    ]
    (
        x_load, gain_load, dh_load, branch_load, conv_load, gate_load, bc_load, dv_load,
        skip_load, out_load,
    ) = loads

    early = (x_load, gain_load, dh_load, branch_load, conv_load, bc_load)
    for load in early:
        load.start()

    barrier = pltpu.get_barrier_semaphore()

    def owner_at(band):
        return (band >= first) & (band < first + rows)

    @pl.loop(1, n)
    def _(turn):
        other = lax.rem(me + turn, n)

        @pl.when(owns | owner_at(other) | (other == me - 1) | (other == me + 1))
        def _():
            pl.semaphore_signal(
                barrier, inc=1, device_id={"cols": other}, device_id_type=pl.DeviceIdType.MESH
            )

    one_left = jnp.where((me > 0) & jnp.logical_not(owner_at(me - 1)), 1, 0)
    one_right = jnp.where((me < last) & jnp.logical_not(owner_at(me + 1)), 1, 0)
    partners = jnp.where(owns, n - 1, rows + one_left + one_right)

    chunk = 2 * LANES
    dh_load.wait()

    @pl.loop(0, inner // chunk)
    def _(turn):
        at = pl.ds(pl.multiple_of(turn * chunk, chunk), chunk)
        place = lax.broadcasted_iota(jnp.int32, (cols, chunk), 0)
        for row in range(rows):
            here = pl.ds(row * cols, cols)
            decay = dh_ref[here, at]
            product = decay
            step = 1
            while step < cols:
                product = product * jnp.where(place >= step, pltpu.roll(product, step, 0), 1.0)
                step *= 2
            prefix[here, at] = product
            p_send[row, :, at] = product[cols - 1 : cols]
            rest = 1.0 - decay * decay
            value = rest * lax.rsqrt(rest * (product * product))
            scale[here, at] = value
            edge_scale[pl.ds(row, 1), at] = value[0:1]
            edge_scale[pl.ds(rows + row, 1), at] = value[cols - 1 : cols]

    x_load.wait()
    gain_load.wait()
    feats = x_ref[...].astype(F32)
    meansq = jnp.mean(feats * feats, axis=-1, keepdims=True)
    normed = (feats * lax.rsqrt(meansq + 1e-05) * gain_ref[...]).astype(BF16)
    x_ref[...] = normed
    branch_load.wait()
    for load in (gate_load, dv_load, skip_load, out_load):
        load.start()
    branch = jnp.dot(normed, w_in_ref[:, :inner], preferred_element_type=F32)
    branch = branch.astype(BF16).astype(F32)
    grid[pl.ds(0, cols), :] = jnp.zeros((cols, inner), F32)
    grid[pl.ds((rows + 1) * cols, cols), :] = jnp.zeros((cols, inner), F32)
    grid[pl.ds(cols, patches), :] = branch
    for row in range(rows):
        for side, place in ((0, row * cols), (1, (row + 1) * cols - 1)):
            fix[side, row : row + 1, :] = branch[place : place + 1]
    for side in range(2):
        edge_out[side] = fix[side].astype(BF16)

    bc_load.wait()
    for row in range(rows):
        w_wide[pl.ds(row * states, states), :] = w_bc_ref[pl.ds(0, states), :]

    pl.semaphore_wait(barrier, partners)

    to_right = copy_to(
        edge_out.at[1], edge_in.at[0], edge_send_sem.at[0], edge_recv_sem.at[0],
        lax.rem(me + 1, n),
    )
    to_left = copy_to(
        edge_out.at[0], edge_in.at[1], edge_send_sem.at[1], edge_recv_sem.at[1],
        lax.rem(me + n - 1, n),
    )

    @pl.when(me < last)
    def _():
        to_right.start()

    @pl.when(me > 0)
    def _():
        to_left.start()

    def send_product(row, owner):
        copy_to(p_send.at[row], p_recv.at[me], p_send_sem, p_recv_sem, owner).start()

    each_owner(send_product)

    def to_sibling(k):
        source, target = (
            (p_send, pair_p),
            (s_send.at[:, :, rest_at], pair_s.at[:, :, rest_at]),
            (first_state.at[:, :, early_at], pair_s.at[:, :, early_at]),
            (s_send.at[:, :, early_at], pair_early),
        )[k]
        return copy_to(source, target, pair_send_sem, pair_recv_sem.at[k], sibling)

    @pl.when(jnp.logical_not(odd))
    def _():
        to_sibling(0).start()

    conv_load.wait()

    @pl.loop(0, inner // chunk)
    def _(turn):
        at = pl.ds(pl.multiple_of(turn * chunk, chunk), chunk)
        taps = [[conv_ref[a, pl.ds(b, 1), at] for b in range(3)] for a in range(3)]
        place = lax.broadcasted_iota(jnp.int32, (cols, chunk), 0)
        for row in range(rows):
            here = pl.ds(row * cols, cols)
            lines = [grid[pl.ds((row + a) * cols, cols), at] for a in range(3)]
            parts = [
                taps[0][b] * lines[0] + taps[1][b] * lines[1] + taps[2][b] * lines[2]
                for b in range(3)
            ]
            conv = (
                jnp.where(place > 0, pltpu.roll(parts[0], 1, 0), 0.0)
                + parts[1]
                + jnp.where(place < cols - 1, pltpu.roll(parts[2], cols - 1, 0), 0.0)
            )
            edge_conv[pl.ds(row, 1), at] = conv[0:1]
            edge_conv[pl.ds(rows + row, 1), at] = conv[cols - 1 : cols]
            sig = conv * jax.nn.sigmoid(conv)
            signal[here, at] = sig
            inside = (place > 0) & (place < cols - 1)
            drive[here, at] = jnp.where(inside, sig * scale[here, at], 0.0).astype(BF16)

    def project(values):
        return lax.dot_general(
            values.astype(BF16), w_bc_ref[...], (((1,), (1,)), ((), ())),
            preferred_element_type=F32,
        )

    def spread_states(values):
        return lax.dot_general(
            values.astype(BF16), w_wide[...], (((1,), (1,)), ((), ())),
            preferred_element_type=F32,
        )

    def place_states(wide, row_of):
        src = row_of(lax.broadcasted_iota(jnp.int32, wide.shape, 0))
        dst = lax.broadcasted_iota(jnp.int32, wide.shape, 1) // states
        return jnp.where(src == dst, wide, 0.0).astype(BF16)

    line = lax.broadcasted_iota(jnp.int32, (rows, inner), 0)

    def edge(side):
        present = ((side == 0) & (me > 0)) | ((side == 1) & (me < last))

        @pl.when(present)
        def _():
            drain(edge_in.at[side], edge_recv_sem.at[side])

        value = jnp.where(present, edge_in[side].astype(F32), 0.0)
        above = jnp.where(line > 0, pltpu.roll(value, 1, 0), 0.0)
        below = jnp.where(line < rows - 1, pltpu.roll(value, rows - 1, 0), 0.0)
        which = pl.ds(pl.multiple_of(side * rows, rows), rows)
        tap = pl.ds(2 * side, 1)
        conv = edge_conv[which, :] + (
            conv_ref[0, tap, :] * above
            + conv_ref[1, tap, :] * value
            + conv_ref[2, tap, :] * below
        )
        sig = conv * jax.nn.sigmoid(conv)
        fix[side] = sig
        edge_drive[which, :] = sig * edge_scale[which, :]
        return spread_states(sig), which

    inner_spread = place_states(spread_states(signal[...]), lambda p: p // cols)
    inner_ends = lax.dot_general(
        inner_spread, drive[...], (((0,), (0,)), ((), ())), preferred_element_type=F32
    )
    soon_coefs, soon_rows = edge(1 - late_side)
    ends[...] = inner_ends + lax.dot_general(
        place_states(soon_coefs, lambda p: p), edge_drive[soon_rows, :].astype(BF16),
        (((0,), (0,)), ((), ())), preferred_element_type=F32,
    )

    def channels(sub):
        return pl.ds(sum(sizes[:sub]), sizes[sub])

    def send_states(sub):
        def send_state(row, owner):
            copy_to(
                s_send.at[row, :, channels(sub)], s_recv.at[me, :, channels(sub)], s_send_sem,
                s_recv_sem.at[sub, me // stride], owner,
            ).start()

        each_owner(send_state, odd)

    for sub in range(ahead):
        at = channels(sub)
        for row in range(rows):
            total = ends[pl.ds(row * states, states), at]
            s_send[row, :, at] = (total * p_send[row, :, at]).astype(BF16)

    def add_pair(sub, source):
        at = channels(sub)
        for row in range(rows):
            s_send[row, :, at] = (
                p_send[row, :, at] * source[row, :, at].astype(F32)
                + s_send[row, :, at].astype(F32)
            ).astype(BF16)

    @pl.when(jnp.logical_not(odd))
    def _():
        to_sibling(3).start()

    dv_load.wait()
    gate_load.wait()
    skip_load.wait()

    @pl.loop(0, inner // chunk)
    def _(turn):
        at = pl.ds(pl.multiple_of(turn * chunk, chunk), chunk)
        half_at = pl.ds(pl.multiple_of(inner + turn * chunk, chunk), chunk)
        half = jnp.dot(x_ref[...], w_in_ref[:, half_at], preferred_element_type=F32)
        half = half.astype(BF16).astype(F32)
        gate[:, at] = half * jax.nn.sigmoid(half)
        down = None
        for row in range(rows):
            here = pl.ds(row * cols, cols)
            decay = dv_ref[here, at]
            down = decay if down is None else down * decay
            rest = 1.0 - decay * decay
            across[here, at] = prefix[here, at] * (rest * lax.rsqrt(rest * (down * down)))
            far[here, at] = down * gate[here, at]

    @pl.when(odd)
    def _():
        drain(pair_early, pair_recv_sem.at[3])
        for sub in range(ahead):
            add_pair(sub, pair_early)

    for sub in range(ahead):
        send_states(sub)


    late_coefs, late_rows = edge(late_side)
    edge_spread = place_states(late_coefs, lambda p: p)
    edge_wide = late_coefs

    @pl.when(me < last)
    def _():
        to_right.wait_send()

    @pl.when(me > 0)
    def _():
        to_left.wait_send()

    if ahead:
        source = pl.ds(0, early_part)
        late_drive = edge_drive[late_rows, source]
        for row in range(rows):
            e_send[row, :, source] = late_drive[row : row + 1] * p_send[row, :, source]
            e_send[row, :, pl.ds(early_part, rows * states)] = edge_wide[row : row + 1]

        def send_edges(row, owner):
            copy_to(
                e_send.at[row], e_recv.at[me], e_send_sem, e_recv_sem.at[me // stride], owner
            ).start()

        each_owner(send_edges)

    def whole_states(target, sub):
        at = channels(sub)
        added = lax.dot_general(
            edge_spread, edge_drive[late_rows, at].astype(BF16), (((0,), (0,)), ((), ())),
            preferred_element_type=F32,
        )
        for row in range(rows):
            total = ends[pl.ds(row * states, states), at] + (
                added[row * states : (row + 1) * states]
            )
            target[row, :, at] = (total * p_send[row, :, at]).astype(BF16)

    for sub in range(ahead, subs):
        whole_states(s_send, sub)

    @pl.when(jnp.logical_not(odd))
    def _():
        to_sibling(1).start()
        for sub in range(ahead):
            whole_states(first_state, sub)
        to_sibling(2).start()

    @pl.when(odd)
    def _():
        drain(pair_s.at[:, :, rest_at], pair_recv_sem.at[1])
        for sub in range(ahead, subs):
            add_pair(sub, pair_s)

    for sub in range(ahead, subs):
        send_states(sub)

    @pl.when(me < 2)
    def _():
        carry[...] = jnp.zeros_like(carry)

    @pl.when(owns & (me < last))
    def _():
        pltpu.make_async_copy(p_send.at[mine], p_recv.at[me], p_recv_sem).start()
        if ahead:
            pltpu.make_async_copy(
                e_send.at[mine], e_recv.at[me], e_recv_sem.at[me // stride]
            ).start()

        def keep(sub):
            pltpu.make_async_copy(
                s_send.at[mine, :, channels(sub)], s_recv.at[me, :, channels(sub)],
                s_recv_sem.at[sub, me // stride],
            ).start()

        @pl.when(odd)
        def _():
            for sub in range(subs):
                keep(sub)


    @pl.loop(0, inner // chunk)
    def _(turn):
        at = pl.ds(pl.multiple_of(turn * chunk, chunk), chunk)
        place = lax.broadcasted_iota(jnp.int32, (cols, chunk), 0)
        for row in range(rows):
            here = pl.ds(row * cols, cols)
            sig = jnp.where(
                place == 0,
                fix[0, row : row + 1, at],
                jnp.where(place == cols - 1, fix[1, row : row + 1, at], signal[here, at]),
            )
            signal[here, at] = sig
            drive[here, at] = (sig * scale[here, at]).astype(BF16)

    coeffs = project(signal[...])
    in_coef, out_coef = coeffs[:, :states], coeffs[:, states:]
    in_high, out_high = in_coef.astype(BF16), out_coef.astype(BF16)
    in_low = (in_coef - in_high.astype(F32)).astype(BF16)
    out_low = (out_coef - out_high.astype(F32)).astype(BF16)
    pairing = lax.dot_general(
        jnp.concatenate([out_high, out_low, out_high], axis=1),
        jnp.concatenate([in_high, in_high, in_low], axis=1),
        (((1,), (1,)), ((), ())),
        preferred_element_type=F32,
    )
    at_row = lax.broadcasted_iota(jnp.int32, pairing.shape, 0)
    at_col = lax.broadcasted_iota(jnp.int32, pairing.shape, 1)
    pairing = jnp.where(lax.rem(at_col, cols) <= lax.rem(at_row, cols), pairing, 0.0)
    high_wide = jnp.concatenate([out_high.astype(F32)] * rows, axis=1)
    low_wide = jnp.concatenate([out_low.astype(F32)] * rows, axis=1)
    wide_col = lax.broadcasted_iota(jnp.int32, high_wide.shape, 1) // states
    begins = [0]
    for source in range(rows):
        begin, count = begins[-1], (rows - source) * cols
        begins.append(begin + count)
        here = pl.ds(begin, count)
        below = slice(source * cols, patches)
        from_drive[here, :] = jnp.where(at_col // cols == source, pairing, 0.0)[below].astype(BF16)
        placed = wide_col == source
        from_carry[here, : rows * states] = jnp.where(placed, high_wide, 0.0)[below].astype(BF16)
        from_carry[here, rows * states :] = jnp.where(placed, low_wide, 0.0)[below].astype(BF16)

    def seen_sum(seen, at):
        sums = [None] * rows
        for source in range(rows):
            reach = across[pl.ds(source * cols, cols), at]
            for row in range(source, rows):
                begin = begins[source] + (row - source) * cols
                term = reach * seen[begin : begin + cols]
                sums[row] = term if sums[row] is None else sums[row] + term
        return sums

    def nearby(turn):
        at = pl.ds(pl.multiple_of(turn * chunk, chunk), chunk)
        seen = jnp.dot(from_drive[...], drive[:, at], preferred_element_type=F32)
        sums = seen_sum(seen, at)
        for row in range(rows):
            here = pl.ds(row * cols, cols)
            near[here, at] = (
                far[here, at] * sums[row] + skip_ref[:, at] * signal[here, at] * gate[here, at]
            )

    def late_states(begin, count):
        late = e_recv[pl.ds(begin, count)].reshape(count, e_recv.shape[-1])
        wide = jnp.concatenate([late[:, early_part:]] * -(-count // rows), axis=1)
        wide = wide[:, : count * states]
        own = lax.broadcasted_iota(jnp.int32, wide.shape, 1) // states
        own = own == lax.broadcasted_iota(jnp.int32, wide.shape, 0)
        extra[pl.ds(begin * states, count * states), :] = lax.dot_general(
            jnp.where(own, wide, 0.0).astype(BF16), late[:, :early_part].astype(BF16),
            (((0,), (0,)), ((), ())), preferred_element_type=F32,
        )

    core = jnp.where(mine < half_rows, 0, 1)

    def prefixes(sub):
        at = channels(sub)

        def send_carry(even, to):
            @pl.when(to != me)
            def _():
                copy_to(
                    c_send.at[even, :, at], carry.at[mine, :, at], c_send_sem,
                    c_recv_sem.at[sub], to,
                ).start()

            @pl.when(to == me)
            def _():
                pltpu.make_async_copy(
                    c_send.at[even, :, at], carry.at[mine, :, at], c_recv_sem.at[sub]
                ).start()

        def chip(turn, state):
            left, right = 2 * turn, 2 * turn + 1
            if sub < ahead:
                for band in (left, right):
                    late = extra[pl.ds(band * states, states), at]
                    state = p_recv[band, :, at] * state + late
                state = state + s_recv[right, :, at].astype(F32)
            else:
                product = p_recv[left, :, at] * p_recv[right, :, at]
                state = product * state + s_recv[right, :, at].astype(F32)
            even = left + 2
            c_send[even, :, at] = state.astype(BF16)
            if sub in DIRECT:
                send_carry(even, even + 1)
                send_carry(even, even)
            else:
                send_carry(even, even + core)
            return state

        state = jnp.zeros((states, sizes[sub]), F32)
        for group in range(GROUPS):
            begin = min(group * stride, last)
            end = min(begin + stride, last)
            stop = min((begin + stride) // 2, n // 2 - 1)
            if begin < end:
                arrivals = stop - begin // 2
                drain(s_recv.at[pl.ds(begin, arrivals), :, at], s_recv_sem.at[sub, group])
                if sub == 0 and ahead:
                    drain(e_recv.at[pl.ds(begin, end - begin)], e_recv_sem.at[group])
                    late_states(begin, end - begin)
                state = lax.fori_loop(begin // 2, stop, chip, state, unroll=True)

    pl.loop(0, inner // chunk)(nearby)

    for sub in range(subs):

        @pl.when(owns)
        def _():
            if sub == 0:
                drain(p_recv, p_recv_sem)
            prefixes(sub)

    out_load.wait()

    def forward(sub):
        which = pl.ds(late_side * half_rows, half_rows)
        at = channels(sub)
        return copy_to(
            carry.at[which, :, at], carry.at[which, :, at], f_send_sem.at[sub],
            f_recv_sem.at[sub], sibling,
        )

    def take(sub):
        @pl.when(me > 1)
        def _():
            count = rows if sub in DIRECT else half_rows
            drain(carry.at[pl.ds(0, count), :, channels(sub)], c_recv_sem.at[sub])
            if sub not in DIRECT:
                forward(sub).start()

    def finish(sub):
        if sub not in DIRECT:

            @pl.when(me > 1)
            def _():
                forward(sub).wait()

        for turn in range(-(-sizes[sub] // chunk)):
            piece = min(chunk, sizes[sub] - turn * chunk)
            at = pl.ds(sum(sizes[:sub]) + turn * chunk, piece)
            state = carry[:, :, at]
            second = pair_p[:, :, at] * state.astype(F32) + pair_s[:, :, at].astype(F32)
            state = jnp.where(odd, second, state.astype(F32)).astype(BF16)
            state = state.reshape(rows * states, piece)
            seen = jnp.dot(
                from_carry[...], jnp.concatenate([state, state], axis=0),
                preferred_element_type=F32,
            )
            sums = seen_sum(seen, at)
            for row in range(rows):
                here = pl.ds(row * cols, cols)
                local[here, at] = (near[here, at] + far[here, at] * sums[row]).astype(BF16)
        result = None if sub == 0 else total_out[...]
        at = channels(sub)
        term = jnp.dot(local[:, at], w_out_ref[at, :], preferred_element_type=F32)
        result = term if result is None else result + term
        if sub == subs - 1:
            out_ref[...] = result.astype(BF16)
        else:
            total_out[...] = result

    @pl.when(odd)
    def _():
        drain(pair_p, pair_recv_sem.at[0])
        drain(pair_s.at[:, :, early_at], pair_recv_sem.at[2])

    for sub in range(subs):
        take(sub)
        if sub > 0:
            finish(sub - 1)
    finish(subs - 1)

    @pl.when(jnp.logical_not(odd))
    def _():
        for k in range(4):
            to_sibling(k).wait_send()

    def sent(count):
        drain(p_recv.at[pl.ds(0, count)], p_send_sem)
        if ahead:
            drain(e_recv.at[pl.ds(0, count)], e_send_sem)

        @pl.when(odd)
        def _():
            drain(c_send.at[pl.ds(0, count)], s_send_sem)

    @pl.when(owns)
    def _():
        for sub in range(subs):
            at = channels(sub)
            if sub in DIRECT:
                own_target, least = me > 1, n - 3
            else:
                own_target, least = (me > 1) & (core == late_side), n // 2 - 2
            drain(c_send.at[pl.ds(0, least), :, at], c_send_sem)

            @pl.when(jnp.logical_not(own_target))
            def _():
                drain(c_send.at[0, :, at], c_send_sem)

        @pl.when(me < last)
        def _():
            sent(rows - 1)

    @pl.when(jnp.logical_not(owns) & (me < last))
    def _():
        sent(rows)


def on_device(n, patches, norm_gain, w_in, conv_w, w_bc, skip, w_out, decay_h, decay_v):
    rows, cols, depth = patches.shape
    inner = w_out.shape[0]
    states = w_bc.shape[1] // 2
    sizes = cut(inner)
    subs = len(sizes)
    ahead = AHEAD
    early_part = sum(sizes[:ahead])
    count = rows * cols
    vmem = pl.BlockSpec(memory_space=pltpu.VMEM)
    dma = pltpu.SemaphoreType.DMA
    out = pl.pallas_call(
        functools.partial(kernel, n, ahead, rows, cols, states),
        out_shape=jax.ShapeDtypeStruct((count, w_out.shape[1]), BF16),
        in_specs=[pl.BlockSpec(memory_space=pltpu.HBM)] * 9,
        out_specs=vmem,
        scratch_shapes=[
            pltpu.VMEM((count, depth), BF16),
            pltpu.VMEM((1, depth), F32),
            pltpu.VMEM(w_in.shape, BF16),
            pltpu.VMEM(conv_w.shape, F32),
            pltpu.VMEM((2 * states, inner), BF16),
            pltpu.VMEM((1, inner), F32),
            pltpu.VMEM(w_out.shape, BF16),
            pltpu.VMEM((count, inner), F32),
            pltpu.VMEM((count, inner), F32),
            pltpu.VMEM((2, rows, inner), BF16),
            pltpu.VMEM((2, rows, inner), BF16),
            pltpu.VMEM((2, rows, inner), F32),
            pltpu.VMEM((2 * rows, inner), F32),
            pltpu.VMEM((2 * rows, inner), F32),
            pltpu.VMEM((2 * rows, inner), F32),
            pltpu.VMEM((count + 2 * cols, inner), F32),
            pltpu.VMEM((count, inner), F32),
            pltpu.VMEM((count, inner), F32),
            pltpu.VMEM((count, inner), F32),
            pltpu.VMEM((count, inner), BF16),
            pltpu.VMEM((rows * states, inner), F32),
            pltpu.VMEM((count, inner), F32),
            pltpu.VMEM((count, inner), F32),
            pltpu.VMEM((count, inner), BF16),
            pltpu.VMEM((count, inner), F32),
            pltpu.VMEM((count, inner), F32),
            pltpu.VMEM((count * (rows + 1) // 2, count), BF16),
            pltpu.VMEM((count * (rows + 1) // 2, 2 * rows * states), BF16),
            pltpu.VMEM((rows, states, inner), BF16),
            pltpu.VMEM((rows, 1, inner), F32),
            pltpu.VMEM((n - 1, states, inner), BF16),
            pltpu.VMEM((n - 1, 1, inner), F32),
            pltpu.VMEM((n, states, inner), BF16),
            pltpu.VMEM((rows, states, inner), BF16),
            pltpu.VMEM((rows, 1, early_part + rows * states), F32),
            pltpu.VMEM((n - 1, 1, early_part + rows * states), F32),
            pltpu.VMEM((-(-(n - 1) // rows) * rows * states, early_part), F32),
            pltpu.VMEM((rows, states, inner), BF16),
            pltpu.VMEM((count, w_out.shape[1]), F32),
            pltpu.VMEM((rows, states, inner), BF16),
            pltpu.VMEM((rows, 1, inner), F32),
            pltpu.VMEM((rows, states, early_part), BF16),
            pltpu.VMEM((rows * states, inner), BF16),
            dma((10,)), dma((2,)), dma((2,)), dma, dma((subs, GROUPS)), dma, dma, dma, dma((subs,)), dma,
            dma((4,)), dma, dma((GROUPS,)), dma((subs,)), dma((subs,)),
        ],
        compiler_params=pltpu.CompilerParams(
            collective_id=0, has_side_effects=True, vmem_limit_bytes=40 << 20
        ),
    )(*[
        pltpu.with_memory_space_constraint(a, pltpu.HBM)
        for a in (
            patches.reshape(count, depth),
            norm_gain.reshape(1, depth),
            w_in,
            conv_w,
            w_bc.T,
            skip.reshape(1, inner),
            w_out,
            decay_h.reshape(count, inner),
            decay_v.reshape(count, inner),
        )
    ])
    return out.reshape(rows, cols, w_out.shape[1])


def solution(mesh):
    n = mesh.shape["cols"]
    banded = P("slides", "cols", None)
    return jax.shard_map(
        functools.partial(on_device, n),
        mesh=mesh,
        in_specs=(banded, P(), P(), P(), P(), P(), P(), banded, banded),
        out_specs=banded,
        check_vma=False,
    )
```

```python
import functools

import jax
import jax.numpy as jnp
from jax import lax
from jax.experimental import pallas as pl
from jax.experimental.pallas import tpu as pltpu
from jax.sharding import PartitionSpec as P

F32 = jnp.float32
BF16 = jnp.bfloat16
LANES = 128
SHARES = (3, 3, 2)
DIRECT = (2,)
AHEAD = 1
GROUPS = 2


def cut(inner):
    return [share * inner // 8 for share in SHARES]


def copy_to(src, dst, send_sem, recv_sem, target):
    return pltpu.make_async_remote_copy(
        src_ref=src,
        dst_ref=dst,
        send_sem=send_sem,
        recv_sem=recv_sem,
        device_id={"cols": target},
        device_id_type=pl.DeviceIdType.MESH,
    )


def drain(ref, sem):
    pltpu.make_async_copy(ref, ref, sem).wait()


def kernel(
    n, ahead, rows, cols, states,
    x_hbm, gain_hbm, w_in_hbm, conv_hbm, w_bc_hbm, skip_hbm, w_out_hbm, dh_hbm, dv_hbm,
    out_ref,
    x_ref, gain_ref, w_in_ref, conv_ref, w_bc_ref, skip_ref, w_out_ref, dh_ref, dv_ref,
    edge_out, edge_in, fix, edge_conv, edge_scale, edge_drive,
    grid, prefix, scale, signal, drive, ends, gate, across, local, far, near, from_drive, from_carry,
    s_send, p_send, s_recv, p_recv, c_send, carry, e_send, e_recv, extra, first_state, total_out,
    pair_s, pair_p, pair_early, w_wide,
    load_sem, edge_send_sem, edge_recv_sem, s_send_sem, s_recv_sem, p_send_sem, p_recv_sem,
    c_send_sem, c_recv_sem, pair_send_sem, pair_recv_sem, e_send_sem, e_recv_sem,
    f_send_sem, f_recv_sem,
):
    me = lax.axis_index("cols")
    inner = w_out_ref.shape[0]
    sizes = cut(inner)
    subs = len(sizes)
    early_part = sum(sizes[:ahead])
    patches = rows * cols
    last = n - 1
    stride = -(-n // GROUPS)
    first = (n - rows) // 2
    mine = me - first
    owns = (me >= first) & (me < first + rows)

    late_side = lax.rem(me, 2)
    odd = late_side == 1
    sibling = me + 1 - 2 * late_side
    half_rows = rows // 2
    early_at, rest_at = pl.ds(0, early_part), pl.ds(early_part, inner - early_part)

    def each_owner(start_copy, sends=True):
        half = rows // 2
        far_half = jnp.where(me < n // 2, 1, 0)

        @pl.when((me < last) & sends)
        def _():
            @pl.loop(0, rows, unroll=True)
            def _(step):
                side = lax.rem(step // half + far_half, 2)
                row = side * half + lax.rem(step + me, half)

                @pl.when(first + row != me)
                def _():
                    start_copy(row, first + row)


    pairs = (
        (x_hbm, x_ref), (gain_hbm, gain_ref), (dh_hbm, dh_ref),
        (w_in_hbm.at[:, pl.ds(0, inner)], w_in_ref.at[:, pl.ds(0, inner)]),
        (conv_hbm, conv_ref),
        (w_in_hbm.at[:, pl.ds(inner, inner)], w_in_ref.at[:, pl.ds(inner, inner)]),
        (w_bc_hbm, w_bc_ref), (dv_hbm, dv_ref), (skip_hbm, skip_ref), (w_out_hbm, w_out_ref),
    )
    loads = [
        pltpu.make_async_copy(src, dst, load_sem.at[k]) for k, (src, dst) in enumerate(pairs)
    ]
    (
        x_load, gain_load, dh_load, branch_load, conv_load, gate_load, bc_load, dv_load,
        skip_load, out_load,
    ) = loads

    early = (x_load, gain_load, dh_load, branch_load, conv_load, bc_load)
    for load in early:
        load.start()

    barrier = pltpu.get_barrier_semaphore()

    def owner_at(band):
        return (band >= first) & (band < first + rows)

    @pl.loop(1, n)
    def _(turn):
        other = lax.rem(me + turn, n)

        @pl.when(owns | owner_at(other) | (other == me - 1) | (other == me + 1))
        def _():
            pl.semaphore_signal(
                barrier, inc=1, device_id={"cols": other}, device_id_type=pl.DeviceIdType.MESH
            )

    one_left = jnp.where((me > 0) & jnp.logical_not(owner_at(me - 1)), 1, 0)
    one_right = jnp.where((me < last) & jnp.logical_not(owner_at(me + 1)), 1, 0)
    partners = jnp.where(owns, n - 1, rows + one_left + one_right)

    chunk = 2 * LANES
    dh_load.wait()

    @pl.loop(0, inner // chunk)
    def _(turn):
        at = pl.ds(pl.multiple_of(turn * chunk, chunk), chunk)
        place = lax.broadcasted_iota(jnp.int32, (cols, chunk), 0)
        for row in range(rows):
            here = pl.ds(row * cols, cols)
            decay = dh_ref[here, at]
            product = decay
            step = 1
            while step < cols:
                product = product * jnp.where(place >= step, pltpu.roll(product, step, 0), 1.0)
                step *= 2
            prefix[here, at] = product
            p_send[row, :, at] = product[cols - 1 : cols]
            rest = 1.0 - decay * decay
            value = rest * lax.rsqrt(rest * (product * product))
            scale[here, at] = value
            edge_scale[pl.ds(row, 1), at] = value[0:1]
            edge_scale[pl.ds(rows + row, 1), at] = value[cols - 1 : cols]

    for load in (gate_load, dv_load, skip_load, out_load):
        load.start()

    x_load.wait()
    gain_load.wait()
    feats = x_ref[...].astype(F32)
    meansq = jnp.mean(feats * feats, axis=-1, keepdims=True)
    normed = (feats * lax.rsqrt(meansq + 1e-05) * gain_ref[...]).astype(BF16)
    x_ref[...] = normed
    branch_load.wait()
    branch = jnp.dot(normed, w_in_ref[:, :inner], preferred_element_type=F32)
    branch = branch.astype(BF16).astype(F32)
    grid[pl.ds(0, cols), :] = jnp.zeros((cols, inner), F32)
    grid[pl.ds((rows + 1) * cols, cols), :] = jnp.zeros((cols, inner), F32)
    grid[pl.ds(cols, patches), :] = branch
    for row in range(rows):
        for side, place in ((0, row * cols), (1, (row + 1) * cols - 1)):
            fix[side, row : row + 1, :] = branch[place : place + 1]
    for side in range(2):
        edge_out[side] = fix[side].astype(BF16)

    bc_load.wait()
    for row in range(rows):
        w_wide[pl.ds(row * states, states), :] = w_bc_ref[pl.ds(0, states), :]

    pl.semaphore_wait(barrier, partners)

    to_right = copy_to(
        edge_out.at[1], edge_in.at[0], edge_send_sem.at[0], edge_recv_sem.at[0],
        lax.rem(me + 1, n),
    )
    to_left = copy_to(
        edge_out.at[0], edge_in.at[1], edge_send_sem.at[1], edge_recv_sem.at[1],
        lax.rem(me + n - 1, n),
    )

    @pl.when(me < last)
    def _():
        to_right.start()

    @pl.when(me > 0)
    def _():
        to_left.start()

    def send_product(row, owner):
        copy_to(p_send.at[row], p_recv.at[me], p_send_sem, p_recv_sem, owner).start()

    each_owner(send_product)

    def to_sibling(k):
        source, target = (
            (p_send, pair_p),
            (s_send.at[:, :, rest_at], pair_s.at[:, :, rest_at]),
            (first_state.at[:, :, early_at], pair_s.at[:, :, early_at]),
            (s_send.at[:, :, early_at], pair_early),
        )[k]
        return copy_to(source, target, pair_send_sem, pair_recv_sem.at[k], sibling)

    @pl.when(jnp.logical_not(odd))
    def _():
        to_sibling(0).start()

    conv_load.wait()

    @pl.loop(0, inner // chunk)
    def _(turn):
        at = pl.ds(pl.multiple_of(turn * chunk, chunk), chunk)
        taps = [[conv_ref[a, pl.ds(b, 1), at] for b in range(3)] for a in range(3)]
        place = lax.broadcasted_iota(jnp.int32, (cols, chunk), 0)
        for row in range(rows):
            here = pl.ds(row * cols, cols)
            lines = [grid[pl.ds((row + a) * cols, cols), at] for a in range(3)]
            parts = [
                taps[0][b] * lines[0] + taps[1][b] * lines[1] + taps[2][b] * lines[2]
                for b in range(3)
            ]
            conv = (
                jnp.where(place > 0, pltpu.roll(parts[0], 1, 0), 0.0)
                + parts[1]
                + jnp.where(place < cols - 1, pltpu.roll(parts[2], cols - 1, 0), 0.0)
            )
            edge_conv[pl.ds(row, 1), at] = conv[0:1]
            edge_conv[pl.ds(rows + row, 1), at] = conv[cols - 1 : cols]
            sig = conv * jax.nn.sigmoid(conv)
            signal[here, at] = sig
            inside = (place > 0) & (place < cols - 1)
            drive[here, at] = jnp.where(inside, sig * scale[here, at], 0.0).astype(BF16)

    def project(values):
        return lax.dot_general(
            values.astype(BF16), w_bc_ref[...], (((1,), (1,)), ((), ())),
            preferred_element_type=F32,
        )

    def spread_states(values):
        return lax.dot_general(
            values.astype(BF16), w_wide[...], (((1,), (1,)), ((), ())),
            preferred_element_type=F32,
        )

    def place_states(wide, row_of):
        src = row_of(lax.broadcasted_iota(jnp.int32, wide.shape, 0))
        dst = lax.broadcasted_iota(jnp.int32, wide.shape, 1) // states
        return jnp.where(src == dst, wide, 0.0).astype(BF16)

    line = lax.broadcasted_iota(jnp.int32, (rows, inner), 0)

    def edge(side):
        present = ((side == 0) & (me > 0)) | ((side == 1) & (me < last))

        @pl.when(present)
        def _():
            drain(edge_in.at[side], edge_recv_sem.at[side])

        value = jnp.where(present, edge_in[side].astype(F32), 0.0)
        above = jnp.where(line > 0, pltpu.roll(value, 1, 0), 0.0)
        below = jnp.where(line < rows - 1, pltpu.roll(value, rows - 1, 0), 0.0)
        which = pl.ds(pl.multiple_of(side * rows, rows), rows)
        tap = pl.ds(2 * side, 1)
        conv = edge_conv[which, :] + (
            conv_ref[0, tap, :] * above
            + conv_ref[1, tap, :] * value
            + conv_ref[2, tap, :] * below
        )
        sig = conv * jax.nn.sigmoid(conv)
        fix[side] = sig
        edge_drive[which, :] = sig * edge_scale[which, :]
        return spread_states(sig), which

    inner_spread = place_states(spread_states(signal[...]), lambda p: p // cols)
    inner_ends = lax.dot_general(
        inner_spread, drive[...], (((0,), (0,)), ((), ())), preferred_element_type=F32
    )
    soon_coefs, soon_rows = edge(1 - late_side)
    ends[...] = inner_ends + lax.dot_general(
        place_states(soon_coefs, lambda p: p), edge_drive[soon_rows, :].astype(BF16),
        (((0,), (0,)), ((), ())), preferred_element_type=F32,
    )

    def channels(sub):
        return pl.ds(sum(sizes[:sub]), sizes[sub])

    def send_states(sub):
        def send_state(row, owner):
            copy_to(
                s_send.at[row, :, channels(sub)], s_recv.at[me, :, channels(sub)], s_send_sem,
                s_recv_sem.at[sub, me // stride], owner,
            ).start()

        each_owner(send_state, odd)

    for sub in range(ahead):
        at = channels(sub)
        for row in range(rows):
            total = ends[pl.ds(row * states, states), at]
            s_send[row, :, at] = (total * p_send[row, :, at]).astype(BF16)

    def add_pair(sub, source):
        at = channels(sub)
        for row in range(rows):
            s_send[row, :, at] = (
                p_send[row, :, at] * source[row, :, at].astype(F32)
                + s_send[row, :, at].astype(F32)
            ).astype(BF16)

    @pl.when(jnp.logical_not(odd))
    def _():
        to_sibling(3).start()

    dv_load.wait()
    gate_load.wait()
    skip_load.wait()

    @pl.loop(0, inner // chunk)
    def _(turn):
        at = pl.ds(pl.multiple_of(turn * chunk, chunk), chunk)
        half_at = pl.ds(pl.multiple_of(inner + turn * chunk, chunk), chunk)
        half = jnp.dot(x_ref[...], w_in_ref[:, half_at], preferred_element_type=F32)
        half = half.astype(BF16).astype(F32)
        gate[:, at] = half * jax.nn.sigmoid(half)
        down = None
        for row in range(rows):
            here = pl.ds(row * cols, cols)
            decay = dv_ref[here, at]
            down = decay if down is None else down * decay
            rest = 1.0 - decay * decay
            across[here, at] = prefix[here, at] * (rest * lax.rsqrt(rest * (down * down)))
            far[here, at] = down * gate[here, at]

    @pl.when(odd)
    def _():
        drain(pair_early, pair_recv_sem.at[3])
        for sub in range(ahead):
            add_pair(sub, pair_early)

    for sub in range(ahead):
        send_states(sub)


    late_coefs, late_rows = edge(late_side)
    edge_spread = place_states(late_coefs, lambda p: p)
    edge_wide = late_coefs

    @pl.when(me < last)
    def _():
        to_right.wait_send()

    @pl.when(me > 0)
    def _():
        to_left.wait_send()

    if ahead:
        source = pl.ds(0, early_part)
        late_drive = edge_drive[late_rows, source]
        for row in range(rows):
            e_send[row, :, source] = late_drive[row : row + 1] * p_send[row, :, source]
            e_send[row, :, pl.ds(early_part, rows * states)] = edge_wide[row : row + 1]

        def send_edges(row, owner):
            copy_to(
                e_send.at[row], e_recv.at[me], e_send_sem, e_recv_sem.at[me // stride], owner
            ).start()

        each_owner(send_edges)

    def whole_states(target, sub):
        at = channels(sub)
        added = lax.dot_general(
            edge_spread, edge_drive[late_rows, at].astype(BF16), (((0,), (0,)), ((), ())),
            preferred_element_type=F32,
        )
        for row in range(rows):
            total = ends[pl.ds(row * states, states), at] + (
                added[row * states : (row + 1) * states]
            )
            target[row, :, at] = (total * p_send[row, :, at]).astype(BF16)

    for sub in range(ahead, subs):
        whole_states(s_send, sub)

    @pl.when(jnp.logical_not(odd))
    def _():
        to_sibling(1).start()
        for sub in range(ahead):
            whole_states(first_state, sub)
        to_sibling(2).start()

    @pl.when(odd)
    def _():
        drain(pair_s.at[:, :, rest_at], pair_recv_sem.at[1])

    for sub in range(ahead, subs):
        pl.when(odd)(functools.partial(add_pair, sub, pair_s))
        send_states(sub)

    @pl.when(me < 2)
    def _():
        carry[...] = jnp.zeros_like(carry)

    @pl.when(owns & (me < last))
    def _():
        pltpu.make_async_copy(p_send.at[mine], p_recv.at[me], p_recv_sem).start()
        if ahead:
            pltpu.make_async_copy(
                e_send.at[mine], e_recv.at[me], e_recv_sem.at[me // stride]
            ).start()

        def keep(sub):
            pltpu.make_async_copy(
                s_send.at[mine, :, channels(sub)], s_recv.at[me, :, channels(sub)],
                s_recv_sem.at[sub, me // stride],
            ).start()

        @pl.when(odd)
        def _():
            for sub in range(subs):
                keep(sub)


    @pl.loop(0, inner // chunk)
    def _(turn):
        at = pl.ds(pl.multiple_of(turn * chunk, chunk), chunk)
        place = lax.broadcasted_iota(jnp.int32, (cols, chunk), 0)
        for row in range(rows):
            here = pl.ds(row * cols, cols)
            sig = jnp.where(
                place == 0,
                fix[0, row : row + 1, at],
                jnp.where(place == cols - 1, fix[1, row : row + 1, at], signal[here, at]),
            )
            signal[here, at] = sig
            drive[here, at] = (sig * scale[here, at]).astype(BF16)

    coeffs = project(signal[...])
    in_coef, out_coef = coeffs[:, :states], coeffs[:, states:]
    in_high, out_high = in_coef.astype(BF16), out_coef.astype(BF16)
    in_low = (in_coef - in_high.astype(F32)).astype(BF16)
    out_low = (out_coef - out_high.astype(F32)).astype(BF16)
    pairing = lax.dot_general(
        jnp.concatenate([out_high, out_low, out_high], axis=1),
        jnp.concatenate([in_high, in_high, in_low], axis=1),
        (((1,), (1,)), ((), ())),
        preferred_element_type=F32,
    )
    at_row = lax.broadcasted_iota(jnp.int32, pairing.shape, 0)
    at_col = lax.broadcasted_iota(jnp.int32, pairing.shape, 1)
    pairing = jnp.where(lax.rem(at_col, cols) <= lax.rem(at_row, cols), pairing, 0.0)
    high_wide = jnp.concatenate([out_high.astype(F32)] * rows, axis=1)
    low_wide = jnp.concatenate([out_low.astype(F32)] * rows, axis=1)
    wide_col = lax.broadcasted_iota(jnp.int32, high_wide.shape, 1) // states
    begins = [0]
    for source in range(rows):
        begin, count = begins[-1], (rows - source) * cols
        begins.append(begin + count)
        here = pl.ds(begin, count)
        below = slice(source * cols, patches)
        from_drive[here, :] = jnp.where(at_col // cols == source, pairing, 0.0)[below].astype(BF16)
        placed = wide_col == source
        from_carry[here, : rows * states] = jnp.where(placed, high_wide, 0.0)[below].astype(BF16)
        from_carry[here, rows * states :] = jnp.where(placed, low_wide, 0.0)[below].astype(BF16)

    def seen_sum(seen, at):
        sums = [None] * rows
        for source in range(rows):
            reach = across[pl.ds(source * cols, cols), at]
            for row in range(source, rows):
                begin = begins[source] + (row - source) * cols
                term = reach * seen[begin : begin + cols]
                sums[row] = term if sums[row] is None else sums[row] + term
        return sums

    def nearby(turn):
        at = pl.ds(pl.multiple_of(turn * chunk, chunk), chunk)
        seen = jnp.dot(from_drive[...], drive[:, at], preferred_element_type=F32)
        sums = seen_sum(seen, at)
        for row in range(rows):
            here = pl.ds(row * cols, cols)
            near[here, at] = (
                far[here, at] * sums[row] + skip_ref[:, at] * signal[here, at] * gate[here, at]
            )

    def late_states(begin, count):
        late = e_recv[pl.ds(begin, count)].reshape(count, e_recv.shape[-1])
        wide = jnp.concatenate([late[:, early_part:]] * -(-count // rows), axis=1)
        wide = wide[:, : count * states]
        own = lax.broadcasted_iota(jnp.int32, wide.shape, 1) // states
        own = own == lax.broadcasted_iota(jnp.int32, wide.shape, 0)
        extra[pl.ds(begin * states, count * states), :] = lax.dot_general(
            jnp.where(own, wide, 0.0).astype(BF16), late[:, :early_part].astype(BF16),
            (((0,), (0,)), ((), ())), preferred_element_type=F32,
        )

    core = jnp.where(mine < half_rows, 0, 1)

    def prefixes(sub):
        at = channels(sub)

        def send_carry(even, to):
            @pl.when(to != me)
            def _():
                copy_to(
                    c_send.at[even, :, at], carry.at[mine, :, at], c_send_sem,
                    c_recv_sem.at[sub], to,
                ).start()

            @pl.when(to == me)
            def _():
                pltpu.make_async_copy(
                    c_send.at[even, :, at], carry.at[mine, :, at], c_recv_sem.at[sub]
                ).start()

        def chip(turn, state):
            left, right = 2 * turn, 2 * turn + 1
            if sub < ahead:
                for band in (left, right):
                    late = extra[pl.ds(band * states, states), at]
                    state = p_recv[band, :, at] * state + late
                state = state + s_recv[right, :, at].astype(F32)
            else:
                product = p_recv[left, :, at] * p_recv[right, :, at]
                state = product * state + s_recv[right, :, at].astype(F32)
            even = left + 2
            c_send[even, :, at] = state.astype(BF16)
            if sub in DIRECT:
                send_carry(even, even + 1)
                send_carry(even, even)
            else:
                send_carry(even, even + core)
            return state

        state = jnp.zeros((states, sizes[sub]), F32)
        for group in range(GROUPS):
            begin = min(group * stride, last)
            end = min(begin + stride, last)
            stop = min((begin + stride) // 2, n // 2 - 1)
            if begin < end:
                arrivals = stop - begin // 2
                drain(s_recv.at[pl.ds(begin, arrivals), :, at], s_recv_sem.at[sub, group])
                if sub == 0 and ahead:
                    drain(e_recv.at[pl.ds(begin, end - begin)], e_recv_sem.at[group])
                    late_states(begin, end - begin)
                state = lax.fori_loop(begin // 2, stop, chip, state, unroll=True)

    pl.loop(0, inner // chunk)(nearby)

    for sub in range(subs):

        @pl.when(owns)
        def _():
            if sub == 0:
                drain(p_recv, p_recv_sem)
            prefixes(sub)

    out_load.wait()

    def forward(sub):
        which = pl.ds(late_side * half_rows, half_rows)
        at = channels(sub)
        return copy_to(
            carry.at[which, :, at], carry.at[which, :, at], f_send_sem.at[sub],
            f_recv_sem.at[sub], sibling,
        )

    def take(sub):
        @pl.when(me > 1)
        def _():
            count = rows if sub in DIRECT else half_rows
            drain(carry.at[pl.ds(0, count), :, channels(sub)], c_recv_sem.at[sub])
            if sub not in DIRECT:
                forward(sub).start()

    def finish(sub):
        if sub not in DIRECT:

            @pl.when(me > 1)
            def _():
                forward(sub).wait()

        for turn in range(-(-sizes[sub] // chunk)):
            piece = min(chunk, sizes[sub] - turn * chunk)
            at = pl.ds(sum(sizes[:sub]) + turn * chunk, piece)
            state = carry[:, :, at]
            second = pair_p[:, :, at] * state.astype(F32) + pair_s[:, :, at].astype(F32)
            state = jnp.where(odd, second, state.astype(F32)).astype(BF16)
            state = state.reshape(rows * states, piece)
            seen = jnp.dot(
                from_carry[...], jnp.concatenate([state, state], axis=0),
                preferred_element_type=F32,
            )
            sums = seen_sum(seen, at)
            for row in range(rows):
                here = pl.ds(row * cols, cols)
                local[here, at] = (near[here, at] + far[here, at] * sums[row]).astype(BF16)
        result = None if sub == 0 else total_out[...]
        at = channels(sub)
        term = jnp.dot(local[:, at], w_out_ref[at, :], preferred_element_type=F32)
        result = term if result is None else result + term
        if sub == subs - 1:
            out_ref[...] = result.astype(BF16)
        else:
            total_out[...] = result

    @pl.when(odd)
    def _():
        drain(pair_p, pair_recv_sem.at[0])
        drain(pair_s.at[:, :, early_at], pair_recv_sem.at[2])

    for sub in range(subs):
        take(sub)
        if sub > 0:
            finish(sub - 1)
    finish(subs - 1)

    @pl.when(jnp.logical_not(odd))
    def _():
        for k in range(4):
            to_sibling(k).wait_send()

    def sent(count):
        drain(p_recv.at[pl.ds(0, count)], p_send_sem)
        if ahead:
            drain(e_recv.at[pl.ds(0, count)], e_send_sem)

        @pl.when(odd)
        def _():
            drain(c_send.at[pl.ds(0, count)], s_send_sem)

    @pl.when(owns)
    def _():
        for sub in range(subs):
            at = channels(sub)
            if sub in DIRECT:
                own_target, least = me > 1, n - 3
            else:
                own_target, least = (me > 1) & (core == late_side), n // 2 - 2
            drain(c_send.at[pl.ds(0, least), :, at], c_send_sem)

            @pl.when(jnp.logical_not(own_target))
            def _():
                drain(c_send.at[0, :, at], c_send_sem)

        @pl.when(me < last)
        def _():
            sent(rows - 1)

    @pl.when(jnp.logical_not(owns) & (me < last))
    def _():
        sent(rows)


def on_device(n, patches, norm_gain, w_in, conv_w, w_bc, skip, w_out, decay_h, decay_v):
    rows, cols, depth = patches.shape
    inner = w_out.shape[0]
    states = w_bc.shape[1] // 2
    sizes = cut(inner)
    subs = len(sizes)
    ahead = AHEAD
    early_part = sum(sizes[:ahead])
    count = rows * cols
    vmem = pl.BlockSpec(memory_space=pltpu.VMEM)
    dma = pltpu.SemaphoreType.DMA
    out = pl.pallas_call(
        functools.partial(kernel, n, ahead, rows, cols, states),
        out_shape=jax.ShapeDtypeStruct((count, w_out.shape[1]), BF16),
        in_specs=[pl.BlockSpec(memory_space=pltpu.HBM)] * 9,
        out_specs=vmem,
        scratch_shapes=[
            pltpu.VMEM((count, depth), BF16),
            pltpu.VMEM((1, depth), F32),
            pltpu.VMEM(w_in.shape, BF16),
            pltpu.VMEM(conv_w.shape, F32),
            pltpu.VMEM((2 * states, inner), BF16),
            pltpu.VMEM((1, inner), F32),
            pltpu.VMEM(w_out.shape, BF16),
            pltpu.VMEM((count, inner), F32),
            pltpu.VMEM((count, inner), F32),
            pltpu.VMEM((2, rows, inner), BF16),
            pltpu.VMEM((2, rows, inner), BF16),
            pltpu.VMEM((2, rows, inner), F32),
            pltpu.VMEM((2 * rows, inner), F32),
            pltpu.VMEM((2 * rows, inner), F32),
            pltpu.VMEM((2 * rows, inner), F32),
            pltpu.VMEM((count + 2 * cols, inner), F32),
            pltpu.VMEM((count, inner), F32),
            pltpu.VMEM((count, inner), F32),
            pltpu.VMEM((count, inner), F32),
            pltpu.VMEM((count, inner), BF16),
            pltpu.VMEM((rows * states, inner), F32),
            pltpu.VMEM((count, inner), F32),
            pltpu.VMEM((count, inner), F32),
            pltpu.VMEM((count, inner), BF16),
            pltpu.VMEM((count, inner), F32),
            pltpu.VMEM((count, inner), F32),
            pltpu.VMEM((count * (rows + 1) // 2, count), BF16),
            pltpu.VMEM((count * (rows + 1) // 2, 2 * rows * states), BF16),
            pltpu.VMEM((rows, states, inner), BF16),
            pltpu.VMEM((rows, 1, inner), F32),
            pltpu.VMEM((n - 1, states, inner), BF16),
            pltpu.VMEM((n - 1, 1, inner), F32),
            pltpu.VMEM((n, states, inner), BF16),
            pltpu.VMEM((rows, states, inner), BF16),
            pltpu.VMEM((rows, 1, early_part + rows * states), F32),
            pltpu.VMEM((n - 1, 1, early_part + rows * states), F32),
            pltpu.VMEM((-(-(n - 1) // rows) * rows * states, early_part), F32),
            pltpu.VMEM((rows, states, inner), BF16),
            pltpu.VMEM((count, w_out.shape[1]), F32),
            pltpu.VMEM((rows, states, inner), BF16),
            pltpu.VMEM((rows, 1, inner), F32),
            pltpu.VMEM((rows, states, early_part), BF16),
            pltpu.VMEM((rows * states, inner), BF16),
            dma((10,)), dma((2,)), dma((2,)), dma, dma((subs, GROUPS)), dma, dma, dma, dma((subs,)), dma,
            dma((4,)), dma, dma((GROUPS,)), dma((subs,)), dma((subs,)),
        ],
        compiler_params=pltpu.CompilerParams(
            collective_id=0, has_side_effects=True, vmem_limit_bytes=40 << 20
        ),
    )(*[
        pltpu.with_memory_space_constraint(a, pltpu.HBM)
        for a in (
            patches.reshape(count, depth),
            norm_gain.reshape(1, depth),
            w_in,
            conv_w,
            w_bc.T,
            skip.reshape(1, inner),
            w_out,
            decay_h.reshape(count, inner),
            decay_v.reshape(count, inner),
        )
    ])
    return out.reshape(rows, cols, w_out.shape[1])


def solution(mesh):
    n = mesh.shape["cols"]
    banded = P("slides", "cols", None)
    return jax.shard_map(
        functools.partial(on_device, n),
        mesh=mesh,
        in_specs=(banded, P(), P(), P(), P(), P(), P(), banded, banded),
        out_specs=banded,
        check_vma=False,
    )
```
